32 devices in a mesh: rep: 2 (over core), grp: 16 (over z, y, x).
Axes of the slice: x: 2, y: 2, z: 4, core: 2. Of those that a mesh axis runs over, the one named last changes fastest.
Arguments:
- grad_parts: float32 [2, 1024, 9216], P('rep', 'grp'), may hold values from -6 to 6
- gain_grad_parts: float32 [2, 2, 1024], P('rep', None, 'grp'), may hold values from -6 to 6
- weights: float32 [1024, 9216], P('grp'), may hold values from -0.1875 to 0.1875
- basis: float32 [1024, 256], P('grp'), may hold values from -0.1875 to 0.1875
- moment_first: float32 [9216, 256], P('grp'), may hold values from -12 to 12
- moment_second: float32 [9216, 256], P('grp'), may hold values from 0.01 to 1
- gains: float32 [2, 1024], P(None, 'grp'), may hold values from 0.5 to 1.5
- gain_first: float32 [2, 1024], P(None, 'grp'), may hold values from -12 to 12
- gain_second: float32 [2, 1024], P(None, 'grp'), may hold values from 0.01 to 1
Outputs:
- new_weights: float32 [1024, 9216], P('grp')
- new_first: float32 [9216, 256], P('grp')
- new_second: float32 [9216, 256], P('grp')
- new_basis: float32 [1024, 256], P('grp')
- new_gains: float32 [2, 1024], P(None, 'grp')
- new_gain_first: float32 [2, 1024], P(None, 'grp')
- new_gain_second: float32 [2, 1024], P(None, 'grp')
The draws below stay inside these ranges and needn't reach their ends.
All inputs are finite; a program needn't handle non-finite values.
Results may differ from the reference program's by a relative error of at most 0.0001.
Values sent between devices are 32-bit elements; how exact they have to be, the bound alone decides.
A program may use at most 64 MiB of HBM per device.

```python
import math
import jax
import jax.numpy as jnp
from jax import lax

D = 1024
RANK = 256
NS_STEPS = 3
NCOL = 9216
N_REP = 2


def shard_levels(own_key, shape, cuts, smallest, top_value):
    loudness, own = 1.0, jax.random.fold_in(own_key, 6)
    for axis_at, blocks in cuts:
        draws = jnp.exp(jax.random.uniform(jax.random.fold_in(own, axis_at), (blocks,), jnp.float32, smallest / len(cuts), top_value / len(cuts)))
        loudness = loudness * jnp.repeat(draws, shape[axis_at] // blocks).reshape([-1 if axis == axis_at else 1 for axis in range(len(shape))])
    return loudness


def bell_draw(rng, shape, deviation, limit, cuts=(), dtype=jnp.bfloat16):
    result = jax.random.normal(rng, shape, jnp.float32) * deviation
    if len(cuts) > 0:
        result = shard_levels(rng, shape, cuts, -0.22, 0.18) * result
    return jnp.clip(result, min=-limit, max=limit).astype(dtype)


def setup_inputs(seed: int = 0) -> dict:
    seeds = jax.random.split(jax.random.key(seed), 10)
    return {
        "grad_parts": bell_draw(seeds[0], (N_REP, D, NCOL), 1.0, 6.0, ((0, 2), (1, 16)), jnp.float32),
        "gain_grad_parts": bell_draw(seeds[1], (N_REP, 2, D), 1.0, 6.0, ((0, 2), (2, 16)), jnp.float32),
        "weights": bell_draw(seeds[2], (D, NCOL), D ** -0.5, 0.1875, ((0, 16),), jnp.float32),
        "basis": bell_draw(seeds[3], (D, RANK), D ** -0.5, 0.1875, ((0, 16),), jnp.float32),
        "moment_first": bell_draw(seeds[4], (NCOL, RANK), 2.0, 12.0, ((0, 16),), jnp.float32),
        "moment_second": jnp.clip(jnp.exp(math.log(1.0) - 4.6051702 * jax.random.uniform(seeds[5], (NCOL, RANK), jnp.float32) ** shard_levels(seeds[5], (NCOL, RANK), ((0, 16),), -0.2, 0.2)), 0.01, 1.0),
        "gains": jnp.clip(1.0 + 0.1 * jax.random.normal(seeds[6], (2, D), jnp.float32), 0.5, 1.5),
        "gain_first": bell_draw(seeds[7], (2, D), 2.0, 12.0, ((1, 16),), jnp.float32),
        "gain_second": jnp.clip(jnp.exp(math.log(1.0) - 4.6051702 * jax.random.uniform(seeds[8], (2, D), jnp.float32) ** shard_levels(seeds[8], (2, D), ((1, 16),), -0.2, 0.2)), 0.01, 1.0),
    }


beta_first = 0.9
beta_second = 0.999
learn_rate = 0.1
galore_scale = 0.25
adam_eps = 1e-08

def exact_dot(left, right):
    return jnp.dot(left, right, precision=lax.Precision.HIGHEST, preferred_element_type=jnp.float32)

def reference(grad_parts, gain_grad_parts, weights, basis, moment_first, moment_second, gains, gain_first, gain_second):
    corr_first = 1.0 - beta_first ** 10
    corr_second = 1.0 - beta_second ** 10
    grad = lax.optimization_barrier(jnp.sum(grad_parts, axis=0))
    gain_grad = lax.optimization_barrier(jnp.sum(gain_grad_parts, axis=0))
    projected = exact_dot(grad.T, basis)
    new_first = beta_first * moment_first + (1.0 - beta_first) * projected
    new_second = beta_second * moment_second + (1.0 - beta_second) * projected * projected
    direction = new_first / corr_first / (jnp.sqrt(new_second / corr_second) + adam_eps)
    new_weights = weights - learn_rate * galore_scale * exact_dot(basis, direction.T)
    subspace = exact_dot(grad, projected)
    gram = exact_dot(subspace.T, subspace)
    scale = jnp.sqrt(jnp.sqrt(jnp.sum(gram * gram) + 1e-06))
    iterate = subspace / scale
    for step in range(NS_STEPS):
        iterate = 1.5 * iterate - 0.5 * exact_dot(iterate, exact_dot(iterate.T, iterate))
    new_gain_first = beta_first * gain_first + (1.0 - beta_first) * gain_grad
    new_gain_second = beta_second * gain_second + (1.0 - beta_second) * gain_grad * gain_grad
    new_gains = gains - learn_rate * (new_gain_first / corr_first) / (jnp.sqrt(new_gain_second / corr_second) + adam_eps)
    return (new_weights, new_first, new_second, iterate, new_gains, new_gain_first, new_gain_second)
```

```python
import jax
import jax.numpy as jnp
from jax import lax
from jax.experimental import pallas as pl
from jax.experimental.pallas import tpu as pltpu
from jax.sharding import PartitionSpec as P

NS_STEPS = 3
GRANT = 24 << 20
WIDE_GRANT = 48 << 20


beta_first = 0.9
beta_second = 0.999
learn_rate = 0.1
galore_scale = 0.25
adam_eps = 1e-08


def exact_dot(left, right):
    return jnp.dot(left, right, precision=lax.Precision.HIGHEST, preferred_element_type=jnp.float32)


def far_first(n):
    return sorted(range(1, n), key=lambda k: abs(k - n // 2))


def peer_copy(src, dst, send_sem, recv_sem, where):
    return pltpu.make_async_remote_copy(
        src_ref=src,
        dst_ref=dst,
        send_sem=send_sem,
        recv_sem=recv_sem,
        device_id=where,
        device_id_type=pl.DeviceIdType.MESH,
    )


def greet(others):
    barrier = pltpu.get_barrier_semaphore()
    for other in others:
        pl.semaphore_signal(barrier, inc=1, device_id=other, device_id_type=pl.DeviceIdType.MESH)
    pl.semaphore_wait(barrier, len(others))


def groups(n):
    fan = 4 if n % 4 == 0 else 1
    return n // fan, fan


def peer_maps(n, me):
    depth, fan = groups(n)
    layer, spot = me // fan, lax.rem(me, fan)
    column = {d: lax.rem(layer + d, depth) * fan + spot for d in range(1, depth)}
    plane = {f: layer * fan + lax.rem(spot + f, fan) for f in range(1, fan)}
    return layer, spot, column, plane


def spread(n, me, ref, send, recv, sent):
    depth, fan = groups(n)
    layer, spot, column, plane = peer_maps(n, me)
    down = []
    for d in sorted(column, key=lambda d: abs(d - depth // 2)):
        down.append((d, peer_copy(ref.at[me], ref.at[me], send.at[d * fan], recv.at[d * fan], {"grp": column[d]})))
        down[-1][1].start()
    for f in plane:
        sent.append(peer_copy(ref.at[me], ref.at[me], send.at[f], recv.at[f], {"grp": plane[f]}))
        sent[-1].start()

    def pass_on():
        for d, copy in down:
            copy.wait()
            slot = lax.rem(layer - d + depth, depth) * fan + spot
            for f in plane:
                at = d * fan + f
                sent.append(peer_copy(ref.at[slot], ref.at[slot], send.at[at], recv.at[at], {"grp": plane[f]}))
                sent[-1].start()

    return pass_on


def split_of(half, block):
    rest = block % 128
    return (block - rest, rest) if 2 * rest == 128 and half % 16 == 0 else (block, 0)


def tails_of(n, half, block):
    rest = split_of(half, block)[1]
    return pltpu.VMEM((n, half // 2, 128) if rest else (1, 8, 128), jnp.float32)


def pack_tails(ref, tails):
    half = ref.shape[1]
    main, rest = split_of(half, ref.shape[2])
    if rest:
        tails[:, :, :rest] = ref[:, : half // 2, main:]
        tails[:, :, rest:] = ref[:, half // 2 :, main:]


def unpack_tails(tails, ref):
    half = ref.shape[1]
    main, rest = split_of(half, ref.shape[2])
    if rest:
        ref[:, : half // 2, main:] = tails[:, :, :rest]
        ref[:, half // 2 :, main:] = tails[:, :, rest:]


def keep_own(me, source, target, tails_out, tails_in):
    target[pl.ds(me, 1)] = source[pl.ds(me, 1)]
    if split_of(*source.shape[1:])[1]:
        tails_in[pl.ds(me, 1)] = tails_out[pl.ds(me, 1)]


def send_block(me, k, where, source, target, tails_out, tails_in, send, recv):
    main, rest = split_of(*source.shape[1:])
    peer = where["grp"]
    copies = [peer_copy(source.at[peer, :, :main], target.at[me, :, :main], send.at[0, k], recv.at[0, k], where)]
    if rest:
        copies.append(peer_copy(tails_out.at[peer], tails_in.at[me], send.at[1, k], recv.at[1, k], where))
    for copy in copies:
        copy.start()
    return copies


def scatter_grad(n, grad, basis, cols, full, mine, swap, parts, tails_out, tails_in, load_sem, swap_sems, basis_send, basis_recv, col_send, col_recv):
    me, rep = lax.axis_index("grp"), lax.axis_index("rep")
    half = swap.shape[0]
    block = cols.shape[2]
    offsets = far_first(n)
    peers = {k: {"grp": lax.rem(me + k, n)} for k in offsets}
    own = pl.ds(pl.multiple_of(rep * half, half), half)
    other = pl.ds(pl.multiple_of((1 - rep) * half, half), half)
    load = pltpu.make_async_copy(grad.at[own], mine, load_sem)
    load.start()
    full[pl.ds(me, 1)] = basis[own][None]
    greet([{"rep": 1 - rep}] + [peers[k] for k in offsets])
    trade = peer_copy(grad.at[other], swap, swap_sems.at[0], swap_sems.at[1], {"rep": 1 - rep})
    trade.start()
    copies = []
    pass_on = spread(n, me, full, basis_send, basis_recv, copies)
    load.wait()
    trade.wait()
    for j in range(n):
        parts[j] = mine[:, j * block : (j + 1) * block] + swap[:, j * block : (j + 1) * block]
    pack_tails(parts, tails_out)
    keep_own(me, parts, cols, tails_out, tails_in)
    late = n // 4
    for at, k in enumerate(offsets):
        if at == late:
            pass_on()
        copies += send_block(me, k, peers[k], parts, cols, tails_out, tails_in, col_send, col_recv)
    for copy in copies:
        copy.wait()
    unpack_tails(tails_in, cols)


def reduce_and_return(
    n, terms, moved, rows, update, near, sums, far, tails_out, tails_in, near_send, near_recv, far_send, far_recv, row_send, row_recv, up_send, up_recv
):
    me = lax.axis_index("grp")
    depth, fan = groups(n)
    layer, spot, column, plane = peer_maps(n, me)
    offsets = far_first(n)
    peers = {k: {"grp": lax.rem(me + k, n)} for k in offsets}
    greet([peers[k] for k in offsets])
    late = []
    waiting = list(offsets)

    def send_update(count):
        for k in waiting[:count]:
            late.extend(send_block(me, k, peers[k], moved, update, tails_out, tails_in, up_send, up_recv))
        del waiting[:count]

    first = []
    for f in plane:
        source = terms.at[:, lax.rem(spot + f, fan)]
        first.append(peer_copy(source, near.at[f], near_send.at[f], near_recv.at[f], {"grp": plane[f]}))
        first[-1].start()
    pack_tails(moved, tails_out)
    send_update(n // 4)
    keep_own(me, moved, update, tails_out, tails_in)
    near[0] = terms[:, pl.ds(spot, 1)][:, 0]
    for copy in first:
        copy.wait()
    partial = near[0]
    for f in plane:
        partial = partial + near[f]
    sums[...] = partial
    second = []
    for d in column:
        source = sums.at[lax.rem(layer + d, depth)]
        second.append(peer_copy(source, far.at[d], far_send.at[d], far_recv.at[d], {"grp": column[d]}))
        second[-1].start()
    send_update(n // 8)
    far[0] = sums[pl.ds(layer, 1)][0]
    for copy in second:
        copy.wait()
    total = far[0]
    for d in column:
        total = total + far[d]
    rows[pl.ds(me, 1)] = total[None]
    pass_on = spread(n, me, rows, row_send, row_recv, late)
    send_update(n // 4)
    pass_on()
    send_update(n)
    for copy in late:
        copy.wait()
    unpack_tails(tails_in, update)


def in_vmem(count):
    return [pl.BlockSpec(memory_space=pltpu.VMEM)] * count


def call_scatter(n, grad, basis):
    rows, ncol = grad.shape
    half, block, rank = rows // 2, ncol // n, basis.shape[1]
    sems = pltpu.SemaphoreType.DMA((n,))
    return pl.pallas_call(
        lambda *refs: scatter_grad(n, *refs),
        out_shape=(
            jax.ShapeDtypeStruct((n, half, block), jnp.float32),
            jax.ShapeDtypeStruct((n, half, rank), jnp.float32),
        ),
        in_specs=[pl.BlockSpec(memory_space=pltpu.HBM)] + in_vmem(1),
        out_specs=tuple(in_vmem(2)),
        scratch_shapes=[
            pltpu.VMEM((half, ncol), jnp.float32),
            pltpu.VMEM((half, ncol), jnp.float32),
            pltpu.VMEM((n, half, block), jnp.float32),
            tails_of(n, half, block),
            tails_of(n, half, block),
            pltpu.SemaphoreType.DMA,
            pltpu.SemaphoreType.DMA((2,)),
            sems,
            sems,
            pltpu.SemaphoreType.DMA((2, n)),
            pltpu.SemaphoreType.DMA((2, n)),
        ],
        compiler_params=pltpu.CompilerParams(collective_id=0, has_side_effects=True, vmem_limit_bytes=GRANT),
        name="scatter_grad",
    )(grad, basis)


def call_return(n, terms, moved):
    half, rank = terms.shape[2:]
    depth, fan = groups(n)
    sems = pltpu.SemaphoreType.DMA((n,))
    return pl.pallas_call(
        lambda *refs: reduce_and_return(n, *refs),
        out_shape=(
            jax.ShapeDtypeStruct((n, half, rank), jnp.float32),
            jax.ShapeDtypeStruct(moved.shape, jnp.float32),
        ),
        in_specs=in_vmem(2),
        out_specs=tuple(in_vmem(2)),
        scratch_shapes=[
            pltpu.VMEM((fan, depth, half, rank), jnp.float32),
            pltpu.VMEM((depth, half, rank), jnp.float32),
            pltpu.VMEM((depth, half, rank), jnp.float32),
            tails_of(*moved.shape),
            tails_of(*moved.shape),
        ]
        + [sems] * 6
        + [pltpu.SemaphoreType.DMA((2, n))] * 2,
        compiler_params=pltpu.CompilerParams(collective_id=1, has_side_effects=True, vmem_limit_bytes=GRANT),
        name="reduce_and_return",
    )(terms, moved)


def split_body(
    grad_parts,
    gain_grad_parts,
    weights,
    basis,
    moment_first,
    moment_second,
    gains,
    gain_first,
    gain_second,
):
    corr_first = 1.0 - beta_first**10
    corr_second = 1.0 - beta_second**10
    n = lax.axis_size("grp")
    rep = lax.axis_index("rep")
    swap = [(0, 1), (1, 0)]
    local_grad = grad_parts[0]
    local_gain = gain_grad_parts[0]
    rows, ncol = local_grad.shape
    half = rows // 2
    block = ncol // n
    rank = basis.shape[1]

    def own_half(x):
        return lax.dynamic_slice_in_dim(x, rep * half, half, 0)

    def swapped(x):
        return lax.ppermute(x, "rep", swap)

    def joined(mine, other):
        return jnp.where(rep == 0, jnp.concatenate([mine, other], 0), jnp.concatenate([other, mine], 0))

    gain_grad = local_gain + swapped(local_gain)
    col_block, half_basis = call_scatter(n, local_grad, basis)
    col_block = col_block.reshape(n * half, block)
    half_basis = half_basis.reshape(n * half, rank)
    partial = exact_dot(col_block.T, half_basis)
    projected = partial + swapped(partial)
    new_first = beta_first * moment_first + (1.0 - beta_first) * projected
    new_second = beta_second * moment_second + (1.0 - beta_second) * projected * projected
    direction = new_first / corr_first / (jnp.sqrt(new_second / corr_second) + adam_eps)
    terms = exact_dot(col_block, projected).reshape(*groups(n), half, rank)
    update_cols = exact_dot(half_basis, direction.T).reshape(n, half, block)
    sub_all, update = call_return(n, terms, update_cols)
    sub_half = lax.dynamic_index_in_dim(sub_all, lax.axis_index("grp"), 0, keepdims=False)
    sub_all = sub_all.reshape(n * half, rank)
    update = jnp.swapaxes(update, 0, 1).reshape(half, ncol)
    gram_half = exact_dot(sub_all.T, sub_all)
    gram = gram_half + swapped(gram_half)
    subspace = joined(sub_half, swapped(sub_half))
    new_half = own_half(weights) - learn_rate * galore_scale * update
    new_weights = joined(new_half, swapped(new_half))
    scale = jnp.sqrt(jnp.sqrt(jnp.sum(gram * gram) + 1e-06))
    iterate = subspace / scale
    current = gram / scale / scale
    for step in range(NS_STEPS):
        iterate = 1.5 * iterate - 0.5 * exact_dot(iterate, current)
        if step + 1 < NS_STEPS:
            side = 1.5 * current - 0.5 * exact_dot(current, current)
            current = 1.5 * side - 0.5 * exact_dot(side, current)
    new_gain_first = beta_first * gain_first + (1.0 - beta_first) * gain_grad
    new_gain_second = beta_second * gain_second + (1.0 - beta_second) * gain_grad * gain_grad
    new_gains = gains - learn_rate * (new_gain_first / corr_first) / (
        jnp.sqrt(new_gain_second / corr_second) + adam_eps
    )
    return (new_weights, new_first, new_second, iterate, new_gains, new_gain_first, new_gain_second)


def rows_dot(left, right):
    return lax.dot_general(
        left, right, (((0,), (0,)), ((), ())), precision=lax.Precision.HIGHEST, preferred_element_type=jnp.float32
    )


def lanes_dot(left, right):
    return lax.dot_general(
        left, right, (((1,), (1,)), ((), ())), precision=lax.Precision.HIGHEST, preferred_element_type=jnp.float32
    )


def exchange_tails(top, bottom):
    low = lax.broadcasted_iota(jnp.int32, top.shape, 1) < 64
    even = jnp.where(low, top, pltpu.roll(bottom, 64, 1))
    odd = jnp.where(low, pltpu.roll(top, 64, 1), bottom)
    return even, odd


def lane_tiles(ref, group, half, tiles):
    return jnp.concatenate(
        [ref[group, t * half : (t + 1) * half].reshape(-1, 128) for t in range(tiles)], axis=1
    )


def one_step(
    n,
    grad,
    gain_part,
    weights,
    basis,
    moment_first,
    moment_second,
    gains,
    gain_first,
    gain_second,
    new_weights,
    new_first,
    new_second,
    new_basis,
    new_gains,
    new_gain_first,
    new_gain_second,
    mine,
    swap,
    parts,
    cols,
    full,
    partial,
    other_partial,
    projected,
    direction,
    pair_proj,
    pair_dir,
    first_in,
    second_in,
    weights_in,
    basis_in,
    gain_in,
    gain_mine,
    gain_other,
    terms,
    near,
    sums,
    far,
    rows,
    other_rows,
    gram,
    other_gram,
    up_out,
    up_in,
    chunk_sem,
    trade_send,
    trade_recv,
    load_sem,
    gain_sems,
    basis_send,
    basis_recv,
    col_send,
    col_recv,
    part_send,
    part_recv,
    near_send,
    near_recv,
    far_send,
    far_recv,
    row_send,
    row_recv,
    swap_sems,
    up_send,
    up_recv,
    out_send,
    out_recv,
):
    corr_first = 1.0 - beta_first**10
    corr_second = 1.0 - beta_second**10
    me, rep = lax.axis_index("grp"), lax.axis_index("rep")
    depth, fan = groups(n)
    layer, spot, column, plane = peer_maps(n, me)
    half, ncol = mine.shape
    wide = 2 * ncol // n
    block = ncol // n
    tiles = block // 128
    main = tiles * 128
    rest = block - main
    rank = basis.shape[1]
    upper, deep = layer // 2, lax.rem(layer, 2)
    line, side = spot // 2, lax.rem(spot, 2)
    partner = {"rep": 1 - rep}
    own = pl.ds(pl.multiple_of(rep * half, half), half)
    other = pl.ds(pl.multiple_of((1 - rep) * half, half), half)
    layers = [2 * (1 - upper) + deep, 2 * (1 - upper) + 1 - deep, 2 * upper + 1 - deep, layer]
    order = [(z, y) for z in layers for y in (line, 1 - line)]
    order[-2:] = order[-2:][::-1]
    spans = [pl.ds(pl.multiple_of((z * 2 + y) * wide, 128), wide) for z, y in order]

    loads = [
        pltpu.make_async_copy(grad.at[own, span], mine.at[:, span], chunk_sem.at[i]) for i, span in enumerate(spans)
    ]
    for load in loads:
        load.start()
    basis_load = pltpu.make_async_copy(basis, basis_in, load_sem.at[0])
    basis_load.start()
    small = [
        pltpu.make_async_copy(gain_part.at[0], gain_mine, load_sem.at[1]),
        pltpu.make_async_copy(gains, gain_in.at[0], load_sem.at[2]),
        pltpu.make_async_copy(gain_first, gain_in.at[1], load_sem.at[3]),
        pltpu.make_async_copy(gain_second, gain_in.at[2], load_sem.at[4]),
        pltpu.make_async_copy(moment_first, first_in, load_sem.at[5]),
        pltpu.make_async_copy(moment_second, second_in, load_sem.at[6]),
        pltpu.make_async_copy(weights.at[own], weights_in, load_sem.at[7]),
    ]
    basis_load.wait()
    full[pl.ds(me, 1)] = basis_in[own][None]
    greet([partner] + [{"grp": lax.rem(me + k, n)} for k in far_first(n)])
    late = []
    trades = [
        peer_copy(grad.at[other, span], swap.at[:, span], trade_send.at[i], trade_recv.at[i], partner)
        for i, span in enumerate(spans)
    ]
    for trade in trades:
        trade.start()
    pass_basis = spread(n, me, full, basis_send, basis_recv, late)
    for load in small:
        load.start()

    for i, (z, y) in enumerate(order):
        loads[i].wait()
        trades[i].wait()
        span = spans[i]
        total = mine[:, span] + swap[:, span]
        base = (z * 2 + y) * 2
        even_tail, odd_tail = exchange_tails(total[: half // 2, main : main + 128], total[half // 2 :, main : main + 128])
        packed = [
            [total[:, 128 * t : 128 * (t + 1)] for t in range(tiles)] + [even_tail],
            [total[:, main + 128 * (t + 1) : main + 128 * (t + 2)] for t in range(tiles)] + [odd_tail],
        ]
        last = i + 1 == len(order)
        for x in range(2):
            at = 0
            for piece in packed[x]:
                parts[base + x, at : at + piece.shape[0]] = piece
                at += piece.shape[0]
        for x in [1 - side] if last else [side, 1 - side]:
            copy = peer_copy(
                parts.at[base + x], cols.at[me], col_send.at[base + x], col_recv.at[me], {"grp": base + x}
            )
            copy.start()
        if i == 1:
            pass_basis()
    cols[pl.ds(me, 1)] = parts[pl.ds(me, 1)]
    for copy in late:
        copy.wait()
    late = []
    gain_trade = peer_copy(gain_mine, gain_other, gain_sems.at[0], gain_sems.at[1], partner)
    small[0].wait()
    gain_trade.start()

    def landed(buffer, send, recv, source):
        return peer_copy(buffer.at[source], buffer.at[source], send.at[source], recv.at[source], {"grp": source})

    near_group = pl.ds(pl.multiple_of(upper * (n // 2), n // 2), n // 2)
    far_group = pl.ds(pl.multiple_of((1 - upper) * (n // 2), n // 2), n // 2)
    near_sources = [2 * (2 * z + y) + x for z, y in order[4:] for x in (side, 1 - side)]
    far_sources = [2 * (2 * z + y) + x for z, y in order[:4] for x in (side, 1 - side)]
    del near_sources[-2]

    def products(group):
        depths = full[group].reshape(-1, rank)
        tops = full[group, : half // 2].reshape(-1, rank)
        bottoms = full[group, half // 2 :].reshape(-1, rank)
        left = lane_tiles(cols, group, half, tiles)
        tail = cols[group, tiles * half :].reshape(-1, 128)
        yield rows_dot(left[:, : main // 2], depths)
        yield rows_dot(left[:, main // 2 :], depths)
        yield rows_dot(tail, tops)[:rest] + rows_dot(tail, bottoms)[rest:]

    pieces = [pl.ds(0, main // 2), pl.ds(main // 2, main // 2), pl.ds(main, rest)]
    for source in near_sources:
        landed(cols, col_send, col_recv, source).wait_recv()
    for piece, product in zip(pieces, products(near_group)):
        partial[piece] = product
    for source in far_sources:
        landed(cols, col_send, col_recv, source).wait_recv()
    joins = []
    for i, (piece, product) in enumerate(zip(pieces, products(far_group))):
        partial[piece] += product
        joins.append(peer_copy(partial.at[piece], other_partial.at[piece], part_send.at[i], part_recv.at[i], partner))
        joins[-1].start()
    small[4].wait()
    small[5].wait()
    natural = [
        pl.ds(pl.multiple_of(side * rest, rest), main // 2),
        pl.ds(pl.multiple_of(side * rest + main // 2, rest), main // 2),
        pl.ds(pl.multiple_of((1 - side) * main, rest), rest),
    ]
    for piece, place, join in zip(pieces, natural, joins):
        join.wait()
        proj = partial[piece] + other_partial[piece]
        projected[piece] = proj
        first = beta_first * first_in[place] + (1.0 - beta_first) * proj
        second = beta_second * second_in[place] + (1.0 - beta_second) * proj * proj
        new_first[place] = first
        new_second[place] = second
        direction[piece] = first / corr_first / (jnp.sqrt(second / corr_second) + adam_eps)
    blank = jnp.zeros((rest, rank), jnp.float32)
    for source, target in ((projected, pair_proj), (direction, pair_dir)):
        target[:rest, :rank] = source[main:]
        target[:rest, rank:] = blank
        target[rest:, :rank] = blank
        target[rest:, rank:] = source[main:]

    whole = exact_dot(lane_tiles(cols, pl.ds(0, n), half, tiles), projected[:main]).reshape(n, half, rank)
    tail = exact_dot(cols[:, tiles * half :].reshape(-1, 128), pair_proj[...])
    terms[:, : half // 2] = whole[:, : half // 2] + tail[:, :rank].reshape(n, half // 2, rank)
    terms[:, half // 2 :] = whole[:, half // 2 :] + tail[:, rank:].reshape(n, half // 2, rank)

    first_hop = []
    for f in plane:
        for d in range(depth):
            source = d * fan + lax.rem(spot + f, fan)
            first_hop.append(
                peer_copy(
                    terms.at[source],
                    near.at[f * depth + d],
                    near_send.at[f * depth + d],
                    near_recv.at[f * depth + d],
                    {"grp": plane[f]},
                )
            )
            first_hop[-1].start()

    def make_update(group, start):
        depths = full[group].reshape(-1, rank)
        sides = jnp.concatenate(
            [full[group, : half // 2].reshape(-1, rank), full[group, half // 2 :].reshape(-1, rank)], axis=1
        )
        wide_part = lanes_dot(depths, direction[:main])
        for t in range(tiles):
            up_out[group, t * half : (t + 1) * half] = wide_part[:, 128 * t : 128 * (t + 1)].reshape(n // 2, half, 128)
        up_out[group, tiles * half :] = lanes_dot(sides, pair_dir[...]).reshape(n // 2, half // 2, 128)

    def send_update(targets):
        for target in targets:
            peer_copy(
                up_out.at[target], up_in.at[me], up_send.at[target], up_recv.at[me], {"grp": target}
            ).start()

    make_update(far_group, 1 - upper)
    send_update(far_sources)
    for copy in first_hop:
        copy.wait()
    for d in range(depth):
        total = terms[d * fan + spot]
        for f in plane:
            total = total + near[f * depth + d]
        sums[d] = total
    second_hop = []
    for d in column:
        source = sums.at[lax.rem(layer + d, depth)]
        second_hop.append(peer_copy(source, far.at[d], far_send.at[d], far_recv.at[d], {"grp": column[d]}))
        second_hop[-1].start()
    make_update(near_group, upper)
    send_update(near_sources)
    up_in[pl.ds(me, 1)] = up_out[pl.ds(me, 1)]
    for copy in second_hop:
        copy.wait()
    total = sums[layer]
    for d in column:
        total = total + far[d]
    rows[pl.ds(me, 1)] = total[None]
    pass_rows = spread(n, me, rows, row_send, row_recv, late)
    row_trade = peer_copy(rows.at[me], other_rows, swap_sems.at[0], swap_sems.at[1], partner)
    row_trade.start()

    for load in small[1:4]:
        load.wait()
    gain_trade.wait()
    gain_grad = gain_mine[...] + gain_other[...]
    gain_one = beta_first * gain_in[1] + (1.0 - beta_first) * gain_grad
    gain_two = beta_second * gain_in[2] + (1.0 - beta_second) * gain_grad * gain_grad
    new_gain_first[...] = gain_one
    new_gain_second[...] = gain_two
    new_gains[...] = gain_in[0] - learn_rate * (gain_one / corr_first) / (jnp.sqrt(gain_two / corr_second) + adam_eps)

    pass_rows()
    for copy in late:
        copy.wait()
    everything = rows[...].reshape(-1, rank)
    gram[...] = rows_dot(everything, everything)
    gram_trade = peer_copy(gram, other_gram, swap_sems.at[2], swap_sems.at[3], partner)
    gram_trade.start()
    row_trade.wait()
    gram_trade.wait()
    current = gram[...] + other_gram[...]
    scale = jnp.sqrt(jnp.sqrt(jnp.sum(current * current, keepdims=True) + 1e-06))
    current = current / scale / scale
    first_rows = rows[me]
    second_rows = other_rows[...]
    upper_rows = jnp.where(rep == 0, first_rows, second_rows)
    lower_rows = jnp.where(rep == 0, second_rows, first_rows)
    iterate = jnp.concatenate([upper_rows, lower_rows], axis=0) / scale
    for step in range(NS_STEPS):
        iterate = 1.5 * iterate - 0.5 * exact_dot(iterate, current)
        if step + 1 < NS_STEPS:
            beside = 1.5 * current - 0.5 * exact_dot(current, current)
            current = 1.5 * beside - 0.5 * exact_dot(beside, current)
    new_basis[...] = iterate

    small[6].wait()
    rate = learn_rate * galore_scale
    returns = []
    for i, (z, y) in enumerate(order[4:][::-1] + order[:4][::-1]):
        base = (z * 2 + y) * 2
        for x in [1 - side] if i == 0 else [side, 1 - side]:
            landed(up_in, up_send, up_recv, base + x).wait_recv()
        start = pl.multiple_of((z * 2 + y) * wide, 128)
        top, bottom = exchange_tails(up_in[base, tiles * half :], up_in[base + 1, tiles * half :])
        for t in range(2 * tiles + 1):
            lanes = pl.ds(pl.multiple_of(start + 128 * t, 128), 128)
            if t < tiles:
                change = up_in[base, t * half : (t + 1) * half]
            elif t == tiles:
                change = jnp.concatenate([top, bottom], axis=0)
            else:
                change = up_in[base + 1, (t - tiles - 1) * half : (t - tiles) * half]
            new_weights[own, lanes] = weights_in[:, lanes] - rate * change
        span = pl.ds(start, wide)
        returns.append(
            peer_copy(new_weights.at[own, span], new_weights.at[own, span], out_send.at[i], out_recv.at[i], partner)
        )
        returns[-1].start()
    for source in far_sources + near_sources:
        landed(parts, col_send, col_recv, source).wait_send()
        landed(up_out, up_send, up_recv, source).wait_send()
    for copy in returns:
        copy.wait()


def call_step(n, *arrays):
    grad, gain_part, weights, basis, moment_first, moment_second, gains, gain_first, gain_second = arrays
    rows, ncol = grad.shape
    half, block, rank = rows // 2, ncol // n, basis.shape[1]
    depth, fan = groups(n)
    message = half * block // 128
    pairs = n // 2

    def held(*shape):
        return pltpu.VMEM(shape, jnp.float32)

    def sems(*shape):
        return pltpu.SemaphoreType.DMA(shape)

    return pl.pallas_call(
        lambda *refs: one_step(n, *refs),
        out_shape=tuple(
            jax.ShapeDtypeStruct(x.shape, jnp.float32)
            for x in (weights, moment_first, moment_second, basis, gains, gain_first, gain_second)
        ),
        in_specs=[pl.BlockSpec(memory_space=pltpu.HBM)] * 9,
        out_specs=tuple(in_vmem(7)),
        scratch_shapes=[
            held(half, ncol),
            held(half, ncol),
            held(n, message, 128),
            held(n, message, 128),
            held(n, half, rank),
            held(block, rank),
            held(block, rank),
            held(block, rank),
            held(block, rank),
            held(128, 2 * rank),
            held(128, 2 * rank),
            held(block, rank),
            held(block, rank),
            held(half, ncol),
            held(rows, rank),
            held(3, 2, rows),
            held(2, rows),
            held(2, rows),
            held(n, half, rank),
            held(n, half, rank),
            held(depth, half, rank),
            held(depth, half, rank),
            held(n, half, rank),
            held(half, rank),
            held(rank, rank),
            held(rank, rank),
            held(n, message, 128),
            held(n, message, 128),
            sems(pairs),
            sems(pairs),
            sems(pairs),
            sems(8),
            sems(2),
            sems(n),
            sems(n),
            sems(n),
            sems(n),
            sems(3),
            sems(3),
            sems(n),
            sems(n),
            sems(n),
            sems(n),
            sems(n),
            sems(n),
            sems(4),
            sems(n),
            sems(n),
            sems(pairs),
            sems(pairs),
        ],
        compiler_params=pltpu.CompilerParams(collective_id=2, has_side_effects=True, vmem_limit_bytes=WIDE_GRANT),
        name="one_step",
    )(*arrays)


def body(grad_parts, *rest):
    n = lax.axis_size("grp")
    rows, ncol = grad_parts.shape[1:]
    half, block = rows // 2, ncol // n
    if n == 16 and half == 32 and block % 128 == 64:
        return call_step(n, grad_parts[0], *rest)
    return split_body(grad_parts, *rest)


def solution(mesh):
    in_specs = (
        P("rep", "grp", None),
        P("rep", None, "grp"),
        P("grp", None),
        P("grp", None),
        P("grp", None),
        P("grp", None),
        P(None, "grp"),
        P(None, "grp"),
        P(None, "grp"),
    )
    out_specs = (
        P("grp", None),
        P("grp", None),
        P("grp", None),
        P("grp", None),
        P(None, "grp"),
        P(None, "grp"),
        P(None, "grp"),
    )
    return jax.shard_map(body, mesh=mesh, in_specs=in_specs, out_specs=out_specs, check_vma=False)
```

```python
import jax
import jax.numpy as jnp
from jax import lax
from jax.experimental import pallas as pl
from jax.experimental.pallas import tpu as pltpu
from jax.sharding import PartitionSpec as P

NS_STEPS = 3
GRANT = 24 << 20
WIDE_GRANT = 60 << 20


beta_first = 0.9
beta_second = 0.999
learn_rate = 0.1
galore_scale = 0.25
adam_eps = 1e-08


def exact_dot(left, right):
    return jnp.dot(left, right, precision=lax.Precision.HIGHEST, preferred_element_type=jnp.float32)


def far_first(n):
    return sorted(range(1, n), key=lambda k: abs(k - n // 2))


def peer_copy(src, dst, send_sem, recv_sem, where):
    return pltpu.make_async_remote_copy(
        src_ref=src,
        dst_ref=dst,
        send_sem=send_sem,
        recv_sem=recv_sem,
        device_id=where,
        device_id_type=pl.DeviceIdType.MESH,
    )


def greet(others):
    barrier = pltpu.get_barrier_semaphore()
    for other in others:
        pl.semaphore_signal(barrier, inc=1, device_id=other, device_id_type=pl.DeviceIdType.MESH)
    pl.semaphore_wait(barrier, len(others))


def groups(n):
    fan = 4 if n % 4 == 0 else 1
    return n // fan, fan


def peer_maps(n, me):
    depth, fan = groups(n)
    layer, spot = me // fan, lax.rem(me, fan)
    column = {d: lax.rem(layer + d, depth) * fan + spot for d in range(1, depth)}
    plane = {f: layer * fan + lax.rem(spot + f, fan) for f in range(1, fan)}
    return layer, spot, column, plane


def spread(n, me, ref, send, recv, sent):
    depth, fan = groups(n)
    layer, spot, column, plane = peer_maps(n, me)
    down = []
    for d in sorted(column, key=lambda d: abs(d - depth // 2)):
        down.append((d, peer_copy(ref.at[me], ref.at[me], send.at[d * fan], recv.at[d * fan], {"grp": column[d]})))
        down[-1][1].start()
    for f in plane:
        sent.append(peer_copy(ref.at[me], ref.at[me], send.at[f], recv.at[f], {"grp": plane[f]}))
        sent[-1].start()

    def pass_on():
        for d, copy in down:
            copy.wait()
            slot = lax.rem(layer - d + depth, depth) * fan + spot
            for f in plane:
                at = d * fan + f
                sent.append(peer_copy(ref.at[slot], ref.at[slot], send.at[at], recv.at[at], {"grp": plane[f]}))
                sent[-1].start()

    return pass_on


def split_of(half, block):
    rest = block % 128
    return (block - rest, rest) if 2 * rest == 128 and half % 16 == 0 else (block, 0)


def tails_of(n, half, block):
    rest = split_of(half, block)[1]
    return pltpu.VMEM((n, half // 2, 128) if rest else (1, 8, 128), jnp.float32)


def pack_tails(ref, tails):
    half = ref.shape[1]
    main, rest = split_of(half, ref.shape[2])
    if rest:
        tails[:, :, :rest] = ref[:, : half // 2, main:]
        tails[:, :, rest:] = ref[:, half // 2 :, main:]


def unpack_tails(tails, ref):
    half = ref.shape[1]
    main, rest = split_of(half, ref.shape[2])
    if rest:
        ref[:, : half // 2, main:] = tails[:, :, :rest]
        ref[:, half // 2 :, main:] = tails[:, :, rest:]


def keep_own(me, source, target, tails_out, tails_in):
    target[pl.ds(me, 1)] = source[pl.ds(me, 1)]
    if split_of(*source.shape[1:])[1]:
        tails_in[pl.ds(me, 1)] = tails_out[pl.ds(me, 1)]


def send_block(me, k, where, source, target, tails_out, tails_in, send, recv):
    main, rest = split_of(*source.shape[1:])
    peer = where["grp"]
    copies = [peer_copy(source.at[peer, :, :main], target.at[me, :, :main], send.at[0, k], recv.at[0, k], where)]
    if rest:
        copies.append(peer_copy(tails_out.at[peer], tails_in.at[me], send.at[1, k], recv.at[1, k], where))
    for copy in copies:
        copy.start()
    return copies


def scatter_grad(n, grad, basis, cols, full, mine, swap, parts, tails_out, tails_in, load_sem, swap_sems, basis_send, basis_recv, col_send, col_recv):
    me, rep = lax.axis_index("grp"), lax.axis_index("rep")
    half = swap.shape[0]
    block = cols.shape[2]
    offsets = far_first(n)
    peers = {k: {"grp": lax.rem(me + k, n)} for k in offsets}
    own = pl.ds(pl.multiple_of(rep * half, half), half)
    other = pl.ds(pl.multiple_of((1 - rep) * half, half), half)
    load = pltpu.make_async_copy(grad.at[own], mine, load_sem)
    load.start()
    full[pl.ds(me, 1)] = basis[own][None]
    greet([{"rep": 1 - rep}] + [peers[k] for k in offsets])
    trade = peer_copy(grad.at[other], swap, swap_sems.at[0], swap_sems.at[1], {"rep": 1 - rep})
    trade.start()
    copies = []
    pass_on = spread(n, me, full, basis_send, basis_recv, copies)
    load.wait()
    trade.wait()
    for j in range(n):
        parts[j] = mine[:, j * block : (j + 1) * block] + swap[:, j * block : (j + 1) * block]
    pack_tails(parts, tails_out)
    keep_own(me, parts, cols, tails_out, tails_in)
    late = n // 4
    for at, k in enumerate(offsets):
        if at == late:
            pass_on()
        copies += send_block(me, k, peers[k], parts, cols, tails_out, tails_in, col_send, col_recv)
    for copy in copies:
        copy.wait()
    unpack_tails(tails_in, cols)


def reduce_and_return(
    n, terms, moved, rows, update, near, sums, far, tails_out, tails_in, near_send, near_recv, far_send, far_recv, row_send, row_recv, up_send, up_recv
):
    me = lax.axis_index("grp")
    depth, fan = groups(n)
    layer, spot, column, plane = peer_maps(n, me)
    offsets = far_first(n)
    peers = {k: {"grp": lax.rem(me + k, n)} for k in offsets}
    greet([peers[k] for k in offsets])
    late = []
    waiting = list(offsets)

    def send_update(count):
        for k in waiting[:count]:
            late.extend(send_block(me, k, peers[k], moved, update, tails_out, tails_in, up_send, up_recv))
        del waiting[:count]

    first = []
    for f in plane:
        source = terms.at[:, lax.rem(spot + f, fan)]
        first.append(peer_copy(source, near.at[f], near_send.at[f], near_recv.at[f], {"grp": plane[f]}))
        first[-1].start()
    pack_tails(moved, tails_out)
    send_update(n // 4)
    keep_own(me, moved, update, tails_out, tails_in)
    near[0] = terms[:, pl.ds(spot, 1)][:, 0]
    for copy in first:
        copy.wait()
    partial = near[0]
    for f in plane:
        partial = partial + near[f]
    sums[...] = partial
    second = []
    for d in column:
        source = sums.at[lax.rem(layer + d, depth)]
        second.append(peer_copy(source, far.at[d], far_send.at[d], far_recv.at[d], {"grp": column[d]}))
        second[-1].start()
    send_update(n // 8)
    far[0] = sums[pl.ds(layer, 1)][0]
    for copy in second:
        copy.wait()
    total = far[0]
    for d in column:
        total = total + far[d]
    rows[pl.ds(me, 1)] = total[None]
    pass_on = spread(n, me, rows, row_send, row_recv, late)
    send_update(n // 4)
    pass_on()
    send_update(n)
    for copy in late:
        copy.wait()
    unpack_tails(tails_in, update)


def in_vmem(count):
    return [pl.BlockSpec(memory_space=pltpu.VMEM)] * count


def call_scatter(n, grad, basis):
    rows, ncol = grad.shape
    half, block, rank = rows // 2, ncol // n, basis.shape[1]
    sems = pltpu.SemaphoreType.DMA((n,))
    return pl.pallas_call(
        lambda *refs: scatter_grad(n, *refs),
        out_shape=(
            jax.ShapeDtypeStruct((n, half, block), jnp.float32),
            jax.ShapeDtypeStruct((n, half, rank), jnp.float32),
        ),
        in_specs=[pl.BlockSpec(memory_space=pltpu.HBM)] + in_vmem(1),
        out_specs=tuple(in_vmem(2)),
        scratch_shapes=[
            pltpu.VMEM((half, ncol), jnp.float32),
            pltpu.VMEM((half, ncol), jnp.float32),
            pltpu.VMEM((n, half, block), jnp.float32),
            tails_of(n, half, block),
            tails_of(n, half, block),
            pltpu.SemaphoreType.DMA,
            pltpu.SemaphoreType.DMA((2,)),
            sems,
            sems,
            pltpu.SemaphoreType.DMA((2, n)),
            pltpu.SemaphoreType.DMA((2, n)),
        ],
        compiler_params=pltpu.CompilerParams(collective_id=0, has_side_effects=True, vmem_limit_bytes=GRANT),
        name="scatter_grad",
    )(grad, basis)


def call_return(n, terms, moved):
    half, rank = terms.shape[2:]
    depth, fan = groups(n)
    sems = pltpu.SemaphoreType.DMA((n,))
    return pl.pallas_call(
        lambda *refs: reduce_and_return(n, *refs),
        out_shape=(
            jax.ShapeDtypeStruct((n, half, rank), jnp.float32),
            jax.ShapeDtypeStruct(moved.shape, jnp.float32),
        ),
        in_specs=in_vmem(2),
        out_specs=tuple(in_vmem(2)),
        scratch_shapes=[
            pltpu.VMEM((fan, depth, half, rank), jnp.float32),
            pltpu.VMEM((depth, half, rank), jnp.float32),
            pltpu.VMEM((depth, half, rank), jnp.float32),
            tails_of(*moved.shape),
            tails_of(*moved.shape),
        ]
        + [sems] * 6
        + [pltpu.SemaphoreType.DMA((2, n))] * 2,
        compiler_params=pltpu.CompilerParams(collective_id=1, has_side_effects=True, vmem_limit_bytes=GRANT),
        name="reduce_and_return",
    )(terms, moved)


def split_body(
    grad_parts,
    gain_grad_parts,
    weights,
    basis,
    moment_first,
    moment_second,
    gains,
    gain_first,
    gain_second,
):
    corr_first = 1.0 - beta_first**10
    corr_second = 1.0 - beta_second**10
    n = lax.axis_size("grp")
    rep = lax.axis_index("rep")
    swap = [(0, 1), (1, 0)]
    local_grad = grad_parts[0]
    local_gain = gain_grad_parts[0]
    rows, ncol = local_grad.shape
    half = rows // 2
    block = ncol // n
    rank = basis.shape[1]

    def own_half(x):
        return lax.dynamic_slice_in_dim(x, rep * half, half, 0)

    def swapped(x):
        return lax.ppermute(x, "rep", swap)

    def joined(mine, other):
        return jnp.where(rep == 0, jnp.concatenate([mine, other], 0), jnp.concatenate([other, mine], 0))

    gain_grad = local_gain + swapped(local_gain)
    col_block, half_basis = call_scatter(n, local_grad, basis)
    col_block = col_block.reshape(n * half, block)
    half_basis = half_basis.reshape(n * half, rank)
    partial = exact_dot(col_block.T, half_basis)
    projected = partial + swapped(partial)
    new_first = beta_first * moment_first + (1.0 - beta_first) * projected
    new_second = beta_second * moment_second + (1.0 - beta_second) * projected * projected
    direction = new_first / corr_first / (jnp.sqrt(new_second / corr_second) + adam_eps)
    terms = exact_dot(col_block, projected).reshape(*groups(n), half, rank)
    update_cols = exact_dot(half_basis, direction.T).reshape(n, half, block)
    sub_all, update = call_return(n, terms, update_cols)
    sub_half = lax.dynamic_index_in_dim(sub_all, lax.axis_index("grp"), 0, keepdims=False)
    sub_all = sub_all.reshape(n * half, rank)
    update = jnp.swapaxes(update, 0, 1).reshape(half, ncol)
    gram_half = exact_dot(sub_all.T, sub_all)
    gram = gram_half + swapped(gram_half)
    subspace = joined(sub_half, swapped(sub_half))
    new_half = own_half(weights) - learn_rate * galore_scale * update
    new_weights = joined(new_half, swapped(new_half))
    scale = jnp.sqrt(jnp.sqrt(jnp.sum(gram * gram) + 1e-06))
    iterate = subspace / scale
    current = gram / scale / scale
    for step in range(NS_STEPS):
        iterate = 1.5 * iterate - 0.5 * exact_dot(iterate, current)
        if step + 1 < NS_STEPS:
            side = 1.5 * current - 0.5 * exact_dot(current, current)
            current = 1.5 * side - 0.5 * exact_dot(side, current)
    new_gain_first = beta_first * gain_first + (1.0 - beta_first) * gain_grad
    new_gain_second = beta_second * gain_second + (1.0 - beta_second) * gain_grad * gain_grad
    new_gains = gains - learn_rate * (new_gain_first / corr_first) / (
        jnp.sqrt(new_gain_second / corr_second) + adam_eps
    )
    return (new_weights, new_first, new_second, iterate, new_gains, new_gain_first, new_gain_second)


def rows_dot(left, right):
    return lax.dot_general(
        left, right, (((0,), (0,)), ((), ())), precision=lax.Precision.HIGHEST, preferred_element_type=jnp.float32
    )


def lanes_dot(left, right):
    return lax.dot_general(
        left, right, (((1,), (1,)), ((), ())), precision=lax.Precision.HIGHEST, preferred_element_type=jnp.float32
    )


def exchange_tails(top, bottom):
    low = lax.broadcasted_iota(jnp.int32, top.shape, 1) < 64
    even = jnp.where(low, top, pltpu.roll(bottom, 64, 1))
    odd = jnp.where(low, pltpu.roll(top, 64, 1), bottom)
    return even, odd


def lane_tiles(ref, group, half, tiles):
    return jnp.concatenate(
        [ref[group, t * half : (t + 1) * half].reshape(-1, 128) for t in range(tiles)], axis=1
    )


def one_step(
    n,
    grad,
    gain_part,
    weights,
    basis,
    moment_first,
    moment_second,
    gains,
    gain_first,
    gain_second,
    new_weights,
    new_first,
    new_second,
    new_basis,
    new_gains,
    new_gain_first,
    new_gain_second,
    mine,
    swap,
    parts,
    cols,
    full,
    partial,
    other_partial,
    projected,
    direction,
    pair_proj,
    first_in,
    second_in,
    weights_in,
    basis_in,
    gain_in,
    gain_mine,
    gain_other,
    terms,
    near,
    sums,
    far,
    rows,
    other_rows,
    gram,
    other_gram,
    up_out,
    up_in,
    chunk_sem,
    trade_send,
    trade_recv,
    load_sem,
    gain_sems,
    basis_send,
    basis_recv,
    col_send,
    col_recv,
    part_send,
    part_recv,
    near_send,
    near_recv,
    far_send,
    far_recv,
    row_send,
    row_recv,
    swap_sems,
    pass_send,
    pass_recv,
    cross_send,
    cross_recv,
    up_send,
    up_recv,
    out_send,
    out_recv,
):
    corr_first = 1.0 - beta_first**10
    corr_second = 1.0 - beta_second**10
    me, rep = lax.axis_index("grp"), lax.axis_index("rep")
    depth, fan = groups(n)
    layer, spot, column, plane = peer_maps(n, me)
    half, ncol = mine.shape
    wide = 2 * ncol // n
    block = ncol // n
    tiles = block // 128
    main = tiles * 128
    rest = block - main
    rank = basis.shape[1]
    upper, deep = layer // 2, lax.rem(layer, 2)
    line, side = spot // 2, lax.rem(spot, 2)
    partner = {"rep": 1 - rep}
    own = pl.ds(pl.multiple_of(rep * half, half), half)
    other = pl.ds(pl.multiple_of((1 - rep) * half, half), half)
    layers = [2 * (1 - upper) + deep, 2 * (1 - upper) + 1 - deep, 2 * upper + 1 - deep, layer]
    order = [(z, y) for z in layers for y in (line, 1 - line)]
    order[-2:] = order[-2:][::-1]
    spans = [pl.ds(pl.multiple_of((z * 2 + y) * wide, 128), wide) for z, y in order]

    loads = [
        pltpu.make_async_copy(grad.at[own, span], mine.at[:, span], chunk_sem.at[i]) for i, span in enumerate(spans)
    ]
    for load in loads:
        load.start()
    basis_load = pltpu.make_async_copy(basis, basis_in, load_sem.at[0])
    basis_load.start()
    small = [
        pltpu.make_async_copy(gain_part.at[0], gain_mine, load_sem.at[1]),
        pltpu.make_async_copy(gains, gain_in.at[0], load_sem.at[2]),
        pltpu.make_async_copy(gain_first, gain_in.at[1], load_sem.at[3]),
        pltpu.make_async_copy(gain_second, gain_in.at[2], load_sem.at[4]),
        pltpu.make_async_copy(moment_first, first_in, load_sem.at[5]),
        pltpu.make_async_copy(moment_second, second_in, load_sem.at[6]),
        pltpu.make_async_copy(weights.at[own], weights_in, load_sem.at[7]),
    ]
    basis_load.wait()
    full[pl.ds(me, 1)] = basis_in[own][None]
    greet([partner] + [{"grp": lax.rem(me + k, n)} for k in far_first(n)])
    late = []
    trades = [
        peer_copy(grad.at[other, span], swap.at[:, span], trade_send.at[i], trade_recv.at[i], partner)
        for i, span in enumerate(spans)
    ]
    for trade in trades:
        trade.start()
    pass_basis = spread(n, me, full, basis_send, basis_recv, late)
    for load in small:
        load.start()

    for i, (z, y) in enumerate(order):
        loads[i].wait()
        trades[i].wait()
        span = spans[i]
        total = mine[:, span] + swap[:, span]
        base = (z * 2 + y) * 2
        even_tail, odd_tail = exchange_tails(total[: half // 2, main : main + 128], total[half // 2 :, main : main + 128])
        packed = [
            [total[:, 128 * t : 128 * (t + 1)] for t in range(tiles)] + [even_tail],
            [total[:, main + 128 * (t + 1) : main + 128 * (t + 2)] for t in range(tiles)] + [odd_tail],
        ]
        last = i + 1 == len(order)
        for x in range(2):
            at = 0
            for piece in packed[x]:
                parts[base + x, at : at + piece.shape[0]] = piece
                at += piece.shape[0]
        for x in [1 - side] if last else [side, 1 - side]:
            copy = peer_copy(
                parts.at[base + x], cols.at[me], col_send.at[base + x], col_recv.at[me], {"grp": base + x}
            )
            copy.start()
        if i == 1:
            pass_basis()
    cols[pl.ds(me, 1)] = parts[pl.ds(me, 1)]
    for copy in late:
        copy.wait()
    late = []
    gain_trade = peer_copy(gain_mine, gain_other, gain_sems.at[0], gain_sems.at[1], partner)
    small[0].wait()
    gain_trade.start()

    def landed(buffer, send, recv, source):
        return peer_copy(buffer.at[source], buffer.at[source], send.at[source], recv.at[source], {"grp": source})

    near_group = pl.ds(pl.multiple_of(upper * (n // 2), n // 2), n // 2)
    far_group = pl.ds(pl.multiple_of((1 - upper) * (n // 2), n // 2), n // 2)
    near_sources = [2 * (2 * z + y) + x for z, y in order[4:] for x in (side, 1 - side)]
    far_sources = [2 * (2 * z + y) + x for z, y in order[:4] for x in (side, 1 - side)]
    del near_sources[-2]

    def products(group):
        depths = full[group].reshape(-1, rank)
        tops = full[group, : half // 2].reshape(-1, rank)
        bottoms = full[group, half // 2 :].reshape(-1, rank)
        left = lane_tiles(cols, group, half, tiles)
        tail = cols[group, tiles * half :].reshape(-1, 128)
        yield rows_dot(left[:, : main // 2], depths)
        yield rows_dot(left[:, main // 2 :], depths)
        yield rows_dot(tail, tops)[:rest] + rows_dot(tail, bottoms)[rest:]

    pieces = [pl.ds(0, main // 2), pl.ds(main // 2, main // 2), pl.ds(main, rest)]
    for source in near_sources:
        landed(cols, col_send, col_recv, source).wait_recv()
    for piece, product in zip(pieces, products(near_group)):
        partial[piece] = product
    for source in far_sources:
        landed(cols, col_send, col_recv, source).wait_recv()
    joins = []
    for i, (piece, product) in enumerate(zip(pieces, products(far_group))):
        partial[piece] += product
        joins.append(peer_copy(partial.at[piece], other_partial.at[piece], part_send.at[i], part_recv.at[i], partner))
        joins[-1].start()
    small[4].wait()
    small[5].wait()
    natural = [
        pl.ds(pl.multiple_of(side * rest, rest), main // 2),
        pl.ds(pl.multiple_of(side * rest + main // 2, rest), main // 2),
        pl.ds(pl.multiple_of((1 - side) * main, rest), rest),
    ]
    for piece, place, join in zip(pieces, natural, joins):
        join.wait()
        proj = partial[piece] + other_partial[piece]
        projected[piece] = proj
        first = beta_first * first_in[place] + (1.0 - beta_first) * proj
        second = beta_second * second_in[place] + (1.0 - beta_second) * proj * proj
        new_first[place] = first
        new_second[place] = second
        direction[layer, piece] = first / corr_first / (jnp.sqrt(second / corr_second) + adam_eps)
    part = block // 4
    ranges = [pl.ds(pl.multiple_of(rep * (block // 2) + c * part, 8), part) for c in range(2)]
    inner = jnp.logical_and(layer > 0, layer < depth - 1)
    low = layer < 2
    mirrored = jnp.where(low, layer, depth - 1 - layer)
    origins = [jnp.where(low, k, depth - 1 - k) for k in (1 - mirrored, 2, 3)]

    def pass_copy(origin, c, toward, at):
        chip = jnp.clip(layer + toward, 0, depth - 1) * fan + spot
        held = direction.at[origin, ranges[c]]
        return peer_copy(held, held, pass_send.at[at, c], pass_recv.at[origin, c], {"grp": chip})

    def own_pass(act):
        for c in range(2):

            @pl.when(layer < depth - 1)
            def _():
                act(pass_copy(layer, c, 1, 0))

            @pl.when(layer > 0)
            def _():
                act(pass_copy(layer, c, -1, 1))

    own_pass(lambda copy: copy.start())

    def cross_copy(k, c):
        held = direction.at[origins[k], ranges[c]]
        return peer_copy(held, held, cross_send.at[k, c], cross_recv.at[k, c], partner)

    def forward(k, c):
        return pass_copy(origins[k], c, jnp.where(origins[k] < layer, 1, -1), 2 + k)

    def take_pass(k):
        for c in range(2):
            forward(k, c).wait_recv()

            @pl.when(inner)
            def _():
                forward(k, c).start()

            cross_copy(k, c).start()

    blank = jnp.zeros((rest, rank), jnp.float32)

    def paired(tail):
        return jnp.concatenate(
            [jnp.concatenate([tail, blank], axis=1), jnp.concatenate([blank, tail], axis=1)], axis=0
        )

    pair_proj[...] = paired(projected[main:])

    whole = exact_dot(lane_tiles(cols, pl.ds(0, n), half, tiles), projected[:main]).reshape(n, half, rank)
    tail = exact_dot(cols[:, tiles * half :].reshape(-1, 128), pair_proj[...])
    terms[:, : half // 2] = whole[:, : half // 2] + tail[:, :rank].reshape(n, half // 2, rank)
    terms[:, half // 2 :] = whole[:, half // 2 :] + tail[:, rank:].reshape(n, half // 2, rank)

    first_hop = []
    for f in plane:
        for d in range(depth):
            source = d * fan + lax.rem(spot + f, fan)
            first_hop.append(
                peer_copy(
                    terms.at[source],
                    near.at[f * depth + d],
                    near_send.at[f * depth + d],
                    near_recv.at[f * depth + d],
                    {"grp": plane[f]},
                )
            )
            first_hop[-1].start()

    beside = pl.ds(pl.multiple_of(layer * fan, fan), fan)

    def make_update(origin):
        group = pl.ds(pl.multiple_of(origin * fan, fan), fan)
        depths = full[beside].reshape(-1, rank)
        sides = jnp.concatenate(
            [full[beside, : half // 2].reshape(-1, rank), full[beside, half // 2 :].reshape(-1, rank)], axis=1
        )
        wide_part = lanes_dot(depths, direction[origin, :main])
        for t in range(tiles):
            up_out[group, t * half : (t + 1) * half] = wide_part[:, 128 * t : 128 * (t + 1)].reshape(fan, half, 128)
        up_out[group, tiles * half :] = lanes_dot(sides, paired(direction[origin, main:])).reshape(fan, half // 2, 128)
        for f in plane:
            at = origin * fan + lax.rem(spot + f, fan)
            peer_copy(
                up_out.at[at],
                up_in.at[origin * fan + spot],
                up_send.at[at],
                up_recv.at[origin * fan + spot],
                {"grp": plane[f]},
            ).start()
        up_in[pl.ds(origin * fan + spot, 1)] = up_out[pl.ds(origin * fan + spot, 1)]

    def take_update(k):
        for c in range(2):
            cross_copy(k, c).wait_recv()
        make_update(origins[k])

    make_update(layer)
    take_pass(0)
    for copy in first_hop:
        copy.wait()
    for d in range(depth):
        total = terms[d * fan + spot]
        for f in plane:
            total = total + near[f * depth + d]
        sums[d] = total
    second_hop = []
    for d in column:
        source = sums.at[lax.rem(layer + d, depth)]
        second_hop.append(peer_copy(source, far.at[d], far_send.at[d], far_recv.at[d], {"grp": column[d]}))
        second_hop[-1].start()
    take_update(0)
    take_pass(1)
    for copy in second_hop:
        copy.wait()
    total = sums[layer]
    for d in column:
        total = total + far[d]
    rows[pl.ds(me, 1)] = total[None]
    pass_rows = spread(n, me, rows, row_send, row_recv, late)
    take_update(1)
    row_trade = peer_copy(rows.at[me], other_rows, swap_sems.at[0], swap_sems.at[1], partner)
    row_trade.start()

    for load in small[1:4]:
        load.wait()
    gain_trade.wait()
    gain_grad = gain_mine[...] + gain_other[...]
    gain_one = beta_first * gain_in[1] + (1.0 - beta_first) * gain_grad
    gain_two = beta_second * gain_in[2] + (1.0 - beta_second) * gain_grad * gain_grad
    new_gain_first[...] = gain_one
    new_gain_second[...] = gain_two
    new_gains[...] = gain_in[0] - learn_rate * (gain_one / corr_first) / (jnp.sqrt(gain_two / corr_second) + adam_eps)

    pass_rows()
    take_pass(2)
    take_update(2)
    for copy in late:
        copy.wait()
    everything = rows[...].reshape(-1, rank)
    gram[...] = rows_dot(everything, everything)
    gram_trade = peer_copy(gram, other_gram, swap_sems.at[2], swap_sems.at[3], partner)
    gram_trade.start()
    row_trade.wait()
    gram_trade.wait()
    current = gram[...] + other_gram[...]
    scale = jnp.sqrt(jnp.sqrt(jnp.sum(current * current, keepdims=True) + 1e-06))
    current = current / scale / scale
    first_rows = rows[me]
    second_rows = other_rows[...]
    upper_rows = jnp.where(rep == 0, first_rows, second_rows)
    lower_rows = jnp.where(rep == 0, second_rows, first_rows)
    iterate = jnp.concatenate([upper_rows, lower_rows], axis=0) / scale
    for step in range(NS_STEPS):
        iterate = 1.5 * iterate - 0.5 * exact_dot(iterate, current)
        if step + 1 < NS_STEPS:
            beside = 1.5 * current - 0.5 * exact_dot(current, current)
            current = 1.5 * beside - 0.5 * exact_dot(beside, current)
    new_basis[...] = iterate

    small[6].wait()
    rate = learn_rate * galore_scale
    returns = []
    for i, (z, y) in enumerate([(z, y) for z in [layer] + origins for y in (line, 1 - line)]):
        base = (z * 2 + y) * 2
        for x in [1 - side] if i % 2 == 0 else [side, 1 - side]:
            landed(up_in, up_send, up_recv, base + x).wait_recv()
        start = pl.multiple_of((z * 2 + y) * wide, 128)
        top, bottom = exchange_tails(up_in[base, tiles * half :], up_in[base + 1, tiles * half :])
        for t in range(2 * tiles + 1):
            lanes = pl.ds(pl.multiple_of(start + 128 * t, 128), 128)
            if t < tiles:
                change = up_in[base, t * half : (t + 1) * half]
            elif t == tiles:
                change = jnp.concatenate([top, bottom], axis=0)
            else:
                change = up_in[base + 1, (t - tiles - 1) * half : (t - tiles) * half]
            new_weights[own, lanes] = weights_in[:, lanes] - rate * change
        span = pl.ds(start, wide)
        returns.append(
            peer_copy(new_weights.at[own, span], new_weights.at[own, span], out_send.at[i], out_recv.at[i], partner)
        )
        returns[-1].start()
    for source in far_sources + near_sources:
        landed(parts, col_send, col_recv, source).wait_send()
    for origin in [layer] + origins:
        for f in plane:
            landed(up_out, up_send, up_recv, origin * fan + lax.rem(spot + f, fan)).wait_send()
    own_pass(lambda copy: copy.wait_send())
    for k in range(3):
        for c in range(2):
            cross_copy(k, c).wait_send()

            @pl.when(inner)
            def _():
                forward(k, c).wait_send()

    for copy in returns:
        copy.wait()


def call_step(n, *arrays):
    grad, gain_part, weights, basis, moment_first, moment_second, gains, gain_first, gain_second = arrays
    rows, ncol = grad.shape
    half, block, rank = rows // 2, ncol // n, basis.shape[1]
    depth, fan = groups(n)
    message = half * block // 128
    pairs = n // 2

    def held(*shape):
        return pltpu.VMEM(shape, jnp.float32)

    def sems(*shape):
        return pltpu.SemaphoreType.DMA(shape)

    return pl.pallas_call(
        lambda *refs: one_step(n, *refs),
        out_shape=tuple(
            jax.ShapeDtypeStruct(x.shape, jnp.float32)
            for x in (weights, moment_first, moment_second, basis, gains, gain_first, gain_second)
        ),
        in_specs=[pl.BlockSpec(memory_space=pltpu.HBM)] * 9,
        out_specs=tuple(in_vmem(7)),
        scratch_shapes=[
            held(half, ncol),
            held(half, ncol),
            held(n, message, 128),
            held(n, message, 128),
            held(n, half, rank),
            held(block, rank),
            held(block, rank),
            held(block, rank),
            held(depth, block, rank),
            held(128, 2 * rank),
            held(block, rank),
            held(block, rank),
            held(half, ncol),
            held(rows, rank),
            held(3, 2, rows),
            held(2, rows),
            held(2, rows),
            held(n, half, rank),
            held(n, half, rank),
            held(depth, half, rank),
            held(depth, half, rank),
            held(n, half, rank),
            held(half, rank),
            held(rank, rank),
            held(rank, rank),
            held(n, message, 128),
            held(n, message, 128),
            sems(pairs),
            sems(pairs),
            sems(pairs),
            sems(8),
            sems(2),
            sems(n),
            sems(n),
            sems(n),
            sems(n),
            sems(3),
            sems(3),
            sems(n),
            sems(n),
            sems(n),
            sems(n),
            sems(n),
            sems(n),
            sems(4),
            sems(5, 2),
            sems(depth, 2),
            sems(3, 2),
            sems(3, 2),
            sems(n),
            sems(n),
            sems(pairs),
            sems(pairs),
        ],
        compiler_params=pltpu.CompilerParams(collective_id=2, has_side_effects=True, vmem_limit_bytes=WIDE_GRANT),
        name="one_step",
    )(*arrays)


def place(count, *refs):
    copies = [
        pltpu.make_async_copy(refs[i], refs[count + i], refs[2 * count].at[i]) for i in range(count)
    ]
    for copy in copies:
        copy.start()
    for copy in copies:
        copy.wait()


def call_place(arrays):
    count = len(arrays)
    return pl.pallas_call(
        lambda *refs: place(count, *refs),
        out_shape=tuple(jax.ShapeDtypeStruct(x.shape, x.dtype) for x in arrays),
        in_specs=in_vmem(count),
        out_specs=tuple([pl.BlockSpec(memory_space=pltpu.HBM)] * count),
        scratch_shapes=[pltpu.SemaphoreType.DMA((count,))],
        name="place",
    )(*arrays)


def body(grad_parts, *rest):
    n = lax.axis_size("grp")
    rows, ncol = grad_parts.shape[1:]
    half, block = rows // 2, ncol // n
    if n == 16 and half == 32 and block % 128 == 64:
        return call_place(call_step(n, grad_parts[0], *rest))
    return split_body(grad_parts, *rest)


def solution(mesh):
    in_specs = (
        P("rep", "grp", None),
        P("rep", None, "grp"),
        P("grp", None),
        P("grp", None),
        P("grp", None),
        P("grp", None),
        P(None, "grp"),
        P(None, "grp"),
        P(None, "grp"),
    )
    out_specs = (
        P("grp", None),
        P("grp", None),
        P("grp", None),
        P("grp", None),
        P(None, "grp"),
        P(None, "grp"),
        P(None, "grp"),
    )
    return jax.shard_map(body, mesh=mesh, in_specs=in_specs, out_specs=out_specs, check_vma=False)
```

```python
import jax
import jax.numpy as jnp
from jax import lax
from jax.experimental import pallas as pl
from jax.experimental.pallas import tpu as pltpu
from jax.sharding import PartitionSpec as P

NS_STEPS = 3
GRANT = 24 << 20
WIDE_GRANT = 60 << 20


beta_first = 0.9
beta_second = 0.999
learn_rate = 0.1
galore_scale = 0.25
adam_eps = 1e-08


def exact_dot(left, right):
    return jnp.dot(left, right, precision=lax.Precision.HIGHEST, preferred_element_type=jnp.float32)


def far_first(n):
    return sorted(range(1, n), key=lambda k: abs(k - n // 2))


def peer_copy(src, dst, send_sem, recv_sem, where):
    return pltpu.make_async_remote_copy(
        src_ref=src,
        dst_ref=dst,
        send_sem=send_sem,
        recv_sem=recv_sem,
        device_id=where,
        device_id_type=pl.DeviceIdType.MESH,
    )


def greet(others):
    barrier = pltpu.get_barrier_semaphore()
    for other in others:
        pl.semaphore_signal(barrier, inc=1, device_id=other, device_id_type=pl.DeviceIdType.MESH)
    pl.semaphore_wait(barrier, len(others))


def groups(n):
    fan = 4 if n % 4 == 0 else 1
    return n // fan, fan


def peer_maps(n, me):
    depth, fan = groups(n)
    layer, spot = me // fan, lax.rem(me, fan)
    column = {d: lax.rem(layer + d, depth) * fan + spot for d in range(1, depth)}
    plane = {f: layer * fan + lax.rem(spot + f, fan) for f in range(1, fan)}
    return layer, spot, column, plane


def spread(n, me, ref, send, recv, sent):
    depth, fan = groups(n)
    layer, spot, column, plane = peer_maps(n, me)
    down = []
    for d in sorted(column, key=lambda d: abs(d - depth // 2)):
        down.append((d, peer_copy(ref.at[me], ref.at[me], send.at[d * fan], recv.at[d * fan], {"grp": column[d]})))
        down[-1][1].start()
    for f in plane:
        sent.append(peer_copy(ref.at[me], ref.at[me], send.at[f], recv.at[f], {"grp": plane[f]}))
        sent[-1].start()

    def pass_on():
        for d, copy in down:
            copy.wait()
            slot = lax.rem(layer - d + depth, depth) * fan + spot
            for f in plane:
                at = d * fan + f
                sent.append(peer_copy(ref.at[slot], ref.at[slot], send.at[at], recv.at[at], {"grp": plane[f]}))
                sent[-1].start()

    return pass_on


def split_of(half, block):
    rest = block % 128
    return (block - rest, rest) if 2 * rest == 128 and half % 16 == 0 else (block, 0)


def tails_of(n, half, block):
    rest = split_of(half, block)[1]
    return pltpu.VMEM((n, half // 2, 128) if rest else (1, 8, 128), jnp.float32)


def pack_tails(ref, tails):
    half = ref.shape[1]
    main, rest = split_of(half, ref.shape[2])
    if rest:
        tails[:, :, :rest] = ref[:, : half // 2, main:]
        tails[:, :, rest:] = ref[:, half // 2 :, main:]


def unpack_tails(tails, ref):
    half = ref.shape[1]
    main, rest = split_of(half, ref.shape[2])
    if rest:
        ref[:, : half // 2, main:] = tails[:, :, :rest]
        ref[:, half // 2 :, main:] = tails[:, :, rest:]


def keep_own(me, source, target, tails_out, tails_in):
    target[pl.ds(me, 1)] = source[pl.ds(me, 1)]
    if split_of(*source.shape[1:])[1]:
        tails_in[pl.ds(me, 1)] = tails_out[pl.ds(me, 1)]


def send_block(me, k, where, source, target, tails_out, tails_in, send, recv):
    main, rest = split_of(*source.shape[1:])
    peer = where["grp"]
    copies = [peer_copy(source.at[peer, :, :main], target.at[me, :, :main], send.at[0, k], recv.at[0, k], where)]
    if rest:
        copies.append(peer_copy(tails_out.at[peer], tails_in.at[me], send.at[1, k], recv.at[1, k], where))
    for copy in copies:
        copy.start()
    return copies


def scatter_grad(n, grad, basis, cols, full, mine, swap, parts, tails_out, tails_in, load_sem, swap_sems, basis_send, basis_recv, col_send, col_recv):
    me, rep = lax.axis_index("grp"), lax.axis_index("rep")
    half = swap.shape[0]
    block = cols.shape[2]
    offsets = far_first(n)
    peers = {k: {"grp": lax.rem(me + k, n)} for k in offsets}
    own = pl.ds(pl.multiple_of(rep * half, half), half)
    other = pl.ds(pl.multiple_of((1 - rep) * half, half), half)
    load = pltpu.make_async_copy(grad.at[own], mine, load_sem)
    load.start()
    full[pl.ds(me, 1)] = basis[own][None]
    greet([{"rep": 1 - rep}] + [peers[k] for k in offsets])
    trade = peer_copy(grad.at[other], swap, swap_sems.at[0], swap_sems.at[1], {"rep": 1 - rep})
    trade.start()
    copies = []
    pass_on = spread(n, me, full, basis_send, basis_recv, copies)
    load.wait()
    trade.wait()
    for j in range(n):
        parts[j] = mine[:, j * block : (j + 1) * block] + swap[:, j * block : (j + 1) * block]
    pack_tails(parts, tails_out)
    keep_own(me, parts, cols, tails_out, tails_in)
    late = n // 4
    for at, k in enumerate(offsets):
        if at == late:
            pass_on()
        copies += send_block(me, k, peers[k], parts, cols, tails_out, tails_in, col_send, col_recv)
    for copy in copies:
        copy.wait()
    unpack_tails(tails_in, cols)


def reduce_and_return(
    n, terms, moved, rows, update, near, sums, far, tails_out, tails_in, near_send, near_recv, far_send, far_recv, row_send, row_recv, up_send, up_recv
):
    me = lax.axis_index("grp")
    depth, fan = groups(n)
    layer, spot, column, plane = peer_maps(n, me)
    offsets = far_first(n)
    peers = {k: {"grp": lax.rem(me + k, n)} for k in offsets}
    greet([peers[k] for k in offsets])
    late = []
    waiting = list(offsets)

    def send_update(count):
        for k in waiting[:count]:
            late.extend(send_block(me, k, peers[k], moved, update, tails_out, tails_in, up_send, up_recv))
        del waiting[:count]

    first = []
    for f in plane:
        source = terms.at[:, lax.rem(spot + f, fan)]
        first.append(peer_copy(source, near.at[f], near_send.at[f], near_recv.at[f], {"grp": plane[f]}))
        first[-1].start()
    pack_tails(moved, tails_out)
    send_update(n // 4)
    keep_own(me, moved, update, tails_out, tails_in)
    near[0] = terms[:, pl.ds(spot, 1)][:, 0]
    for copy in first:
        copy.wait()
    partial = near[0]
    for f in plane:
        partial = partial + near[f]
    sums[...] = partial
    second = []
    for d in column:
        source = sums.at[lax.rem(layer + d, depth)]
        second.append(peer_copy(source, far.at[d], far_send.at[d], far_recv.at[d], {"grp": column[d]}))
        second[-1].start()
    send_update(n // 8)
    far[0] = sums[pl.ds(layer, 1)][0]
    for copy in second:
        copy.wait()
    total = far[0]
    for d in column:
        total = total + far[d]
    rows[pl.ds(me, 1)] = total[None]
    pass_on = spread(n, me, rows, row_send, row_recv, late)
    send_update(n // 4)
    pass_on()
    send_update(n)
    for copy in late:
        copy.wait()
    unpack_tails(tails_in, update)


def in_vmem(count):
    return [pl.BlockSpec(memory_space=pltpu.VMEM)] * count


def call_scatter(n, grad, basis):
    rows, ncol = grad.shape
    half, block, rank = rows // 2, ncol // n, basis.shape[1]
    sems = pltpu.SemaphoreType.DMA((n,))
    return pl.pallas_call(
        lambda *refs: scatter_grad(n, *refs),
        out_shape=(
            jax.ShapeDtypeStruct((n, half, block), jnp.float32),
            jax.ShapeDtypeStruct((n, half, rank), jnp.float32),
        ),
        in_specs=[pl.BlockSpec(memory_space=pltpu.HBM)] + in_vmem(1),
        out_specs=tuple(in_vmem(2)),
        scratch_shapes=[
            pltpu.VMEM((half, ncol), jnp.float32),
            pltpu.VMEM((half, ncol), jnp.float32),
            pltpu.VMEM((n, half, block), jnp.float32),
            tails_of(n, half, block),
            tails_of(n, half, block),
            pltpu.SemaphoreType.DMA,
            pltpu.SemaphoreType.DMA((2,)),
            sems,
            sems,
            pltpu.SemaphoreType.DMA((2, n)),
            pltpu.SemaphoreType.DMA((2, n)),
        ],
        compiler_params=pltpu.CompilerParams(collective_id=0, has_side_effects=True, vmem_limit_bytes=GRANT),
        name="scatter_grad",
    )(grad, basis)


def call_return(n, terms, moved):
    half, rank = terms.shape[2:]
    depth, fan = groups(n)
    sems = pltpu.SemaphoreType.DMA((n,))
    return pl.pallas_call(
        lambda *refs: reduce_and_return(n, *refs),
        out_shape=(
            jax.ShapeDtypeStruct((n, half, rank), jnp.float32),
            jax.ShapeDtypeStruct(moved.shape, jnp.float32),
        ),
        in_specs=in_vmem(2),
        out_specs=tuple(in_vmem(2)),
        scratch_shapes=[
            pltpu.VMEM((fan, depth, half, rank), jnp.float32),
            pltpu.VMEM((depth, half, rank), jnp.float32),
            pltpu.VMEM((depth, half, rank), jnp.float32),
            tails_of(*moved.shape),
            tails_of(*moved.shape),
        ]
        + [sems] * 6
        + [pltpu.SemaphoreType.DMA((2, n))] * 2,
        compiler_params=pltpu.CompilerParams(collective_id=1, has_side_effects=True, vmem_limit_bytes=GRANT),
        name="reduce_and_return",
    )(terms, moved)


def split_body(
    grad_parts,
    gain_grad_parts,
    weights,
    basis,
    moment_first,
    moment_second,
    gains,
    gain_first,
    gain_second,
):
    corr_first = 1.0 - beta_first**10
    corr_second = 1.0 - beta_second**10
    n = lax.axis_size("grp")
    rep = lax.axis_index("rep")
    swap = [(0, 1), (1, 0)]
    local_grad = grad_parts[0]
    local_gain = gain_grad_parts[0]
    rows, ncol = local_grad.shape
    half = rows // 2
    block = ncol // n
    rank = basis.shape[1]

    def own_half(x):
        return lax.dynamic_slice_in_dim(x, rep * half, half, 0)

    def swapped(x):
        return lax.ppermute(x, "rep", swap)

    def joined(mine, other):
        return jnp.where(rep == 0, jnp.concatenate([mine, other], 0), jnp.concatenate([other, mine], 0))

    gain_grad = local_gain + swapped(local_gain)
    col_block, half_basis = call_scatter(n, local_grad, basis)
    col_block = col_block.reshape(n * half, block)
    half_basis = half_basis.reshape(n * half, rank)
    partial = exact_dot(col_block.T, half_basis)
    projected = partial + swapped(partial)
    new_first = beta_first * moment_first + (1.0 - beta_first) * projected
    new_second = beta_second * moment_second + (1.0 - beta_second) * projected * projected
    direction = new_first / corr_first / (jnp.sqrt(new_second / corr_second) + adam_eps)
    terms = exact_dot(col_block, projected).reshape(*groups(n), half, rank)
    update_cols = exact_dot(half_basis, direction.T).reshape(n, half, block)
    sub_all, update = call_return(n, terms, update_cols)
    sub_half = lax.dynamic_index_in_dim(sub_all, lax.axis_index("grp"), 0, keepdims=False)
    sub_all = sub_all.reshape(n * half, rank)
    update = jnp.swapaxes(update, 0, 1).reshape(half, ncol)
    gram_half = exact_dot(sub_all.T, sub_all)
    gram = gram_half + swapped(gram_half)
    subspace = joined(sub_half, swapped(sub_half))
    new_half = own_half(weights) - learn_rate * galore_scale * update
    new_weights = joined(new_half, swapped(new_half))
    scale = jnp.sqrt(jnp.sqrt(jnp.sum(gram * gram) + 1e-06))
    iterate = subspace / scale
    current = gram / scale / scale
    for step in range(NS_STEPS):
        iterate = 1.5 * iterate - 0.5 * exact_dot(iterate, current)
        if step + 1 < NS_STEPS:
            side = 1.5 * current - 0.5 * exact_dot(current, current)
            current = 1.5 * side - 0.5 * exact_dot(side, current)
    new_gain_first = beta_first * gain_first + (1.0 - beta_first) * gain_grad
    new_gain_second = beta_second * gain_second + (1.0 - beta_second) * gain_grad * gain_grad
    new_gains = gains - learn_rate * (new_gain_first / corr_first) / (
        jnp.sqrt(new_gain_second / corr_second) + adam_eps
    )
    return (new_weights, new_first, new_second, iterate, new_gains, new_gain_first, new_gain_second)


def halves(x):
    high = x.astype(jnp.bfloat16)
    return high, (x - high.astype(jnp.float32)).astype(jnp.bfloat16)


def three_dots(left, right, dims):
    left_high, left_low = halves(left)
    right_high, right_low = halves(right)

    def product(a, b):
        return lax.dot_general(a, b, (dims, ((), ())), preferred_element_type=jnp.float32)

    return product(left_high, right_high) + (product(left_high, right_low) + product(left_low, right_high))


def plain_dot(left, right):
    return three_dots(left, right, ((1,), (0,)))


def rows_dot(left, right):
    return three_dots(left, right, ((0,), (0,)))


def lanes_dot(left, right):
    return three_dots(left, right, ((1,), (1,)))


def exchange_tails(top, bottom):
    low = lax.broadcasted_iota(jnp.int32, top.shape, 1) < 64
    even = jnp.where(low, top, pltpu.roll(bottom, 64, 1))
    odd = jnp.where(low, pltpu.roll(top, 64, 1), bottom)
    return even, odd


def lane_tiles(ref, group, half, tiles):
    return jnp.concatenate(
        [ref[group, t * half : (t + 1) * half].reshape(-1, 128) for t in range(tiles)], axis=1
    )


def one_step(
    n,
    grad,
    gain_part,
    weights,
    basis,
    moment_first,
    moment_second,
    gains,
    gain_first,
    gain_second,
    new_weights,
    new_first,
    new_second,
    new_basis,
    new_gains,
    new_gain_first,
    new_gain_second,
    mine,
    swap,
    parts,
    cols,
    full,
    partial,
    other_partial,
    projected,
    direction,
    pair_proj,
    first_in,
    second_in,
    weights_in,
    basis_in,
    gain_in,
    gain_mine,
    gain_other,
    terms,
    near,
    sums,
    far,
    rows,
    other_rows,
    gram,
    other_gram,
    up_out,
    up_in,
    chunk_sem,
    trade_send,
    trade_recv,
    load_sem,
    gain_sems,
    basis_send,
    basis_recv,
    col_send,
    col_recv,
    part_send,
    part_recv,
    near_send,
    near_recv,
    far_send,
    far_recv,
    row_send,
    row_recv,
    swap_sems,
    pass_send,
    pass_recv,
    cross_send,
    cross_recv,
    up_send,
    up_recv,
    out_send,
    out_recv,
    store_sem,
):
    corr_first = 1.0 - beta_first**10
    corr_second = 1.0 - beta_second**10
    me, rep = lax.axis_index("grp"), lax.axis_index("rep")
    depth, fan = groups(n)
    layer, spot, column, plane = peer_maps(n, me)
    half, ncol = mine.shape
    wide = 2 * ncol // n
    block = ncol // n
    tiles = block // 128
    main = tiles * 128
    rest = block - main
    rank = basis.shape[1]
    upper, deep = layer // 2, lax.rem(layer, 2)
    line, side = spot // 2, lax.rem(spot, 2)
    partner = {"rep": 1 - rep}
    own = pl.ds(pl.multiple_of(rep * half, half), half)
    other = pl.ds(pl.multiple_of((1 - rep) * half, half), half)
    layers = [2 * (1 - upper) + deep, 2 * (1 - upper) + 1 - deep, 2 * upper + 1 - deep, layer]
    order = [(z, y) for z in layers for y in (line, 1 - line)]
    order[-2:] = order[-2:][::-1]
    spans = [pl.ds(pl.multiple_of((z * 2 + y) * wide, 128), wide) for z, y in order]

    loads = [
        pltpu.make_async_copy(grad.at[own, span], mine.at[:, span], chunk_sem.at[i]) for i, span in enumerate(spans)
    ]
    for load in loads:
        load.start()
    basis_load = pltpu.make_async_copy(basis, basis_in, load_sem.at[0])
    basis_load.start()
    small = [
        pltpu.make_async_copy(gain_part.at[0], gain_mine, load_sem.at[1]),
        pltpu.make_async_copy(gains, gain_in.at[0], load_sem.at[2]),
        pltpu.make_async_copy(gain_first, gain_in.at[1], load_sem.at[3]),
        pltpu.make_async_copy(gain_second, gain_in.at[2], load_sem.at[4]),
        pltpu.make_async_copy(moment_first, first_in, load_sem.at[5]),
        pltpu.make_async_copy(moment_second, second_in, load_sem.at[6]),
        pltpu.make_async_copy(weights.at[own], weights_in, load_sem.at[7]),
    ]
    basis_load.wait()
    full[pl.ds(me, 1)] = basis_in[own][None]
    greet([partner] + [{"grp": lax.rem(me + k, n)} for k in far_first(n)])
    late = []
    trades = [
        peer_copy(grad.at[other, span], swap.at[:, span], trade_send.at[i], trade_recv.at[i], partner)
        for i, span in enumerate(spans)
    ]
    for trade in trades:
        trade.start()
    pass_basis = spread(n, me, full, basis_send, basis_recv, late)
    for load in small:
        load.start()

    for i, (z, y) in enumerate(order):
        loads[i].wait()
        trades[i].wait()
        span = spans[i]
        total = mine[:, span] + swap[:, span]
        base = (z * 2 + y) * 2
        even_tail, odd_tail = exchange_tails(total[: half // 2, main : main + 128], total[half // 2 :, main : main + 128])
        packed = [
            [total[:, 128 * t : 128 * (t + 1)] for t in range(tiles)] + [even_tail],
            [total[:, main + 128 * (t + 1) : main + 128 * (t + 2)] for t in range(tiles)] + [odd_tail],
        ]
        last = i + 1 == len(order)
        for x in range(2):
            at = 0
            for piece in packed[x]:
                parts[base + x, at : at + piece.shape[0]] = piece
                at += piece.shape[0]
        for x in [1 - side] if last else [side, 1 - side]:
            copy = peer_copy(
                parts.at[base + x], cols.at[me], col_send.at[base + x], col_recv.at[me], {"grp": base + x}
            )
            copy.start()
        if i == 1:
            pass_basis()
    cols[pl.ds(me, 1)] = parts[pl.ds(me, 1)]
    for copy in late:
        copy.wait()
    late = []
    gain_trade = peer_copy(gain_mine, gain_other, gain_sems.at[0], gain_sems.at[1], partner)
    small[0].wait()
    gain_trade.start()

    def landed(buffer, send, recv, source):
        return peer_copy(buffer.at[source], buffer.at[source], send.at[source], recv.at[source], {"grp": source})

    near_group = pl.ds(pl.multiple_of(upper * (n // 2), n // 2), n // 2)
    far_group = pl.ds(pl.multiple_of((1 - upper) * (n // 2), n // 2), n // 2)
    near_sources = [2 * (2 * z + y) + x for z, y in order[4:] for x in (side, 1 - side)]
    far_sources = [2 * (2 * z + y) + x for z, y in order[:4] for x in (side, 1 - side)]
    del near_sources[-2]

    def products(group):
        depths = full[group].reshape(-1, rank)
        tops = full[group, : half // 2].reshape(-1, rank)
        bottoms = full[group, half // 2 :].reshape(-1, rank)
        left = lane_tiles(cols, group, half, tiles)
        tail = cols[group, tiles * half :].reshape(-1, 128)
        yield rows_dot(left[:, : main // 2], depths)
        yield rows_dot(left[:, main // 2 :], depths)
        yield rows_dot(tail, tops)[:rest] + rows_dot(tail, bottoms)[rest:]

    pieces = [pl.ds(0, main // 2), pl.ds(main // 2, main // 2), pl.ds(main, rest)]
    for source in near_sources:
        landed(cols, col_send, col_recv, source).wait_recv()
    for piece, product in zip(pieces, products(near_group)):
        partial[piece] = product
    for source in far_sources:
        landed(cols, col_send, col_recv, source).wait_recv()
    joins = []
    for i, (piece, product) in enumerate(zip(pieces, products(far_group))):
        partial[piece] += product
        joins.append(peer_copy(partial.at[piece], other_partial.at[piece], part_send.at[i], part_recv.at[i], partner))
        joins[-1].start()
    small[4].wait()
    small[5].wait()
    natural = [
        pl.ds(pl.multiple_of(side * rest, rest), main // 2),
        pl.ds(pl.multiple_of(side * rest + main // 2, rest), main // 2),
        pl.ds(pl.multiple_of((1 - side) * main, rest), rest),
    ]
    for piece, place, join in zip(pieces, natural, joins):
        join.wait()
        proj = partial[piece] + other_partial[piece]
        projected[piece] = proj
        first = beta_first * first_in[place] + (1.0 - beta_first) * proj
        second = beta_second * second_in[place] + (1.0 - beta_second) * proj * proj
        first_in[place] = first
        second_in[place] = second
        direction[layer, piece] = first / corr_first / (jnp.sqrt(second / corr_second) + adam_eps)
    stores = []

    def store(source, target):
        stores.append(pltpu.make_async_copy(source, target, store_sem.at[len(stores)]))
        stores[-1].start()

    store(first_in, new_first)
    store(second_in, new_second)
    part = block // 4
    ranges = [pl.ds(pl.multiple_of(rep * (block // 2) + c * part, 8), part) for c in range(2)]
    inner = jnp.logical_and(layer > 0, layer < depth - 1)
    low = layer < 2
    mirrored = jnp.where(low, layer, depth - 1 - layer)
    origins = [jnp.where(low, k, depth - 1 - k) for k in (1 - mirrored, 2, 3)]

    def pass_copy(origin, c, toward, at):
        chip = jnp.clip(layer + toward, 0, depth - 1) * fan + spot
        held = direction.at[origin, ranges[c]]
        return peer_copy(held, held, pass_send.at[at, c], pass_recv.at[origin, c], {"grp": chip})

    def own_pass(act):
        for c in range(2):

            @pl.when(layer < depth - 1)
            def _():
                act(pass_copy(layer, c, 1, 0))

            @pl.when(layer > 0)
            def _():
                act(pass_copy(layer, c, -1, 1))

    own_pass(lambda copy: copy.start())

    def cross_copy(k, c):
        held = direction.at[origins[k], ranges[c]]
        return peer_copy(held, held, cross_send.at[k, c], cross_recv.at[k, c], partner)

    def forward(k, c):
        return pass_copy(origins[k], c, jnp.where(origins[k] < layer, 1, -1), 2 + k)

    def take_pass(k):
        for c in range(2):
            forward(k, c).wait_recv()

            @pl.when(inner)
            def _():
                forward(k, c).start()

            cross_copy(k, c).start()

    blank = jnp.zeros((rest, rank), jnp.float32)

    def paired(tail):
        return jnp.concatenate(
            [jnp.concatenate([tail, blank], axis=1), jnp.concatenate([blank, tail], axis=1)], axis=0
        )

    pair_proj[...] = paired(projected[main:])

    whole = plain_dot(lane_tiles(cols, pl.ds(0, n), half, tiles), projected[:main]).reshape(n, half, rank)
    tail = plain_dot(cols[:, tiles * half :].reshape(-1, 128), pair_proj[...])
    terms[:, : half // 2] = whole[:, : half // 2] + tail[:, :rank].reshape(n, half // 2, rank)
    terms[:, half // 2 :] = whole[:, half // 2 :] + tail[:, rank:].reshape(n, half // 2, rank)

    first_hop = []
    for f in plane:
        for d in range(depth):
            source = d * fan + lax.rem(spot + f, fan)
            first_hop.append(
                peer_copy(
                    terms.at[source],
                    near.at[f * depth + d],
                    near_send.at[f * depth + d],
                    near_recv.at[f * depth + d],
                    {"grp": plane[f]},
                )
            )
            first_hop[-1].start()

    beside = pl.ds(pl.multiple_of(layer * fan, fan), fan)

    def make_update(origin):
        group = pl.ds(pl.multiple_of(origin * fan, fan), fan)
        depths = full[beside].reshape(-1, rank)
        sides = jnp.concatenate(
            [full[beside, : half // 2].reshape(-1, rank), full[beside, half // 2 :].reshape(-1, rank)], axis=1
        )
        wide_part = lanes_dot(depths, direction[origin, :main])
        for t in range(tiles):
            up_out[group, t * half : (t + 1) * half] = wide_part[:, 128 * t : 128 * (t + 1)].reshape(fan, half, 128)
        up_out[group, tiles * half :] = lanes_dot(sides, paired(direction[origin, main:])).reshape(fan, half // 2, 128)
        for f in plane:
            at = origin * fan + lax.rem(spot + f, fan)
            peer_copy(
                up_out.at[at],
                up_in.at[origin * fan + spot],
                up_send.at[at],
                up_recv.at[origin * fan + spot],
                {"grp": plane[f]},
            ).start()
        up_in[pl.ds(origin * fan + spot, 1)] = up_out[pl.ds(origin * fan + spot, 1)]

    def take_update(k):
        for c in range(2):
            cross_copy(k, c).wait_recv()
        make_update(origins[k])

    rate = learn_rate * galore_scale
    returns = []

    def take_weights(k):
        z = ([layer] + origins)[k]
        for j, y in enumerate((line, 1 - line)):
            base = (z * 2 + y) * 2
            for x in [1 - side] if j == 0 else [side, 1 - side]:
                landed(up_in, up_send, up_recv, base + x).wait_recv()
            start = pl.multiple_of((z * 2 + y) * wide, 128)
            top, bottom = exchange_tails(up_in[base, tiles * half :], up_in[base + 1, tiles * half :])
            for t in range(2 * tiles + 1):
                lanes = pl.ds(pl.multiple_of(start + 128 * t, 128), 128)
                if t < tiles:
                    change = up_in[base, t * half : (t + 1) * half]
                elif t == tiles:
                    change = jnp.concatenate([top, bottom], axis=0)
                else:
                    change = up_in[base + 1, (t - tiles - 1) * half : (t - tiles) * half]
                weights_in[:, lanes] = weights_in[:, lanes] - rate * change
            ready = weights_in.at[:, pl.ds(start, wide)]
            target = new_weights.at[own, pl.ds(start, wide)]
            i = len(returns)
            returns.append(peer_copy(ready, target, out_send.at[i], out_recv.at[i], partner))
            returns[-1].start()
            store(ready, target)

    take_pass(0)
    for copy in first_hop:
        copy.wait()
    for d in range(depth):
        total = terms[d * fan + spot]
        for f in plane:
            total = total + near[f * depth + d]
        sums[d] = total
    second_hop = []
    for d in column:
        source = sums.at[lax.rem(layer + d, depth)]
        second_hop.append(peer_copy(source, far.at[d], far_send.at[d], far_recv.at[d], {"grp": column[d]}))
        second_hop[-1].start()
    make_update(layer)
    take_update(0)
    take_pass(1)
    for copy in second_hop:
        copy.wait()
    total = sums[layer]
    for d in column:
        total = total + far[d]
    rows[pl.ds(me, 1)] = total[None]
    pass_rows = spread(n, me, rows, row_send, row_recv, late)
    take_update(1)
    row_trade = peer_copy(rows.at[me], other_rows, swap_sems.at[0], swap_sems.at[1], partner)
    row_trade.start()

    for load in small[1:4]:
        load.wait()
    gain_trade.wait()
    gain_grad = gain_mine[...] + gain_other[...]
    gain_one = beta_first * gain_in[1] + (1.0 - beta_first) * gain_grad
    gain_two = beta_second * gain_in[2] + (1.0 - beta_second) * gain_grad * gain_grad
    gain_in[0] = gain_in[0] - learn_rate * (gain_one / corr_first) / (jnp.sqrt(gain_two / corr_second) + adam_eps)
    gain_in[1] = gain_one
    gain_in[2] = gain_two
    store(gain_in.at[0], new_gains)
    store(gain_in.at[1], new_gain_first)
    store(gain_in.at[2], new_gain_second)

    pass_rows()
    take_pass(2)
    small[6].wait()
    take_weights(0)
    take_weights(1)
    take_update(2)
    for copy in late:
        copy.wait()
    everything = rows[...].reshape(-1, rank)
    gram[...] = rows_dot(everything, everything)
    gram_trade = peer_copy(gram, other_gram, swap_sems.at[2], swap_sems.at[3], partner)
    gram_trade.start()
    take_weights(2)
    row_trade.wait()
    gram_trade.wait()
    current = gram[...] + other_gram[...]
    scale = jnp.sqrt(jnp.sqrt(jnp.sum(current * current, keepdims=True) + 1e-06))
    current = current / scale / scale
    first_rows = rows[me]
    second_rows = other_rows[...]
    upper_rows = jnp.where(rep == 0, first_rows, second_rows)
    lower_rows = jnp.where(rep == 0, second_rows, first_rows)
    iterate = jnp.concatenate([upper_rows, lower_rows], axis=0) / scale
    for step in range(NS_STEPS):
        iterate = 1.5 * iterate - 0.5 * plain_dot(iterate, current)
        if step + 1 < NS_STEPS:
            beside = 1.5 * current - 0.5 * plain_dot(current, current)
            current = 1.5 * beside - 0.5 * plain_dot(beside, current)
    basis_in[...] = iterate
    store(basis_in, new_basis)

    take_weights(3)
    for source in far_sources + near_sources:
        landed(parts, col_send, col_recv, source).wait_send()
    for origin in [layer] + origins:
        for f in plane:
            landed(up_out, up_send, up_recv, origin * fan + lax.rem(spot + f, fan)).wait_send()
    own_pass(lambda copy: copy.wait_send())
    for k in range(3):
        for c in range(2):
            cross_copy(k, c).wait_send()

            @pl.when(inner)
            def _():
                forward(k, c).wait_send()

    for copy in returns + stores:
        copy.wait()


def call_step(n, *arrays):
    grad, gain_part, weights, basis, moment_first, moment_second, gains, gain_first, gain_second = arrays
    rows, ncol = grad.shape
    half, block, rank = rows // 2, ncol // n, basis.shape[1]
    depth, fan = groups(n)
    message = half * block // 128
    pairs = n // 2

    def held(*shape):
        return pltpu.VMEM(shape, jnp.float32)

    def sems(*shape):
        return pltpu.SemaphoreType.DMA(shape)

    return pl.pallas_call(
        lambda *refs: one_step(n, *refs),
        out_shape=tuple(
            jax.ShapeDtypeStruct(x.shape, jnp.float32)
            for x in (weights, moment_first, moment_second, basis, gains, gain_first, gain_second)
        ),
        in_specs=[pl.BlockSpec(memory_space=pltpu.HBM)] * 9,
        out_specs=tuple([pl.BlockSpec(memory_space=pltpu.HBM)] * 7),
        scratch_shapes=[
            held(half, ncol),
            held(half, ncol),
            held(n, message, 128),
            held(n, message, 128),
            held(n, half, rank),
            held(block, rank),
            held(block, rank),
            held(block, rank),
            held(depth, block, rank),
            held(128, 2 * rank),
            held(block, rank),
            held(block, rank),
            held(half, ncol),
            held(rows, rank),
            held(3, 2, rows),
            held(2, rows),
            held(2, rows),
            held(n, half, rank),
            held(n, half, rank),
            held(depth, half, rank),
            held(depth, half, rank),
            held(n, half, rank),
            held(half, rank),
            held(rank, rank),
            held(rank, rank),
            held(n, message, 128),
            held(n, message, 128),
            sems(pairs),
            sems(pairs),
            sems(pairs),
            sems(8),
            sems(2),
            sems(n),
            sems(n),
            sems(n),
            sems(n),
            sems(3),
            sems(3),
            sems(n),
            sems(n),
            sems(n),
            sems(n),
            sems(n),
            sems(n),
            sems(4),
            sems(5, 2),
            sems(depth, 2),
            sems(3, 2),
            sems(3, 2),
            sems(n),
            sems(n),
            sems(pairs),
            sems(pairs),
            sems(pairs + 6),
        ],
        compiler_params=pltpu.CompilerParams(collective_id=2, has_side_effects=True, vmem_limit_bytes=WIDE_GRANT),
        name="one_step",
    )(*arrays)


def pieces_of(shape):
    count = 1
    while shape[0] % (16 * count) == 0 and shape[0] * shape[1] // count > 1 << 17:
        count *= 2
    size = shape[0] // count
    return [pl.ds(i * size, size) for i in range(count)]


def place(count, *refs):
    sources, targets, held, sems = refs[:count], refs[count : 2 * count], refs[2 * count : 3 * count], refs[-1]
    loads, stores = [], []
    for source, target, buffer in zip(sources, targets, held):
        for piece in pieces_of(source.shape):
            at = len(loads)
            loads.append(pltpu.make_async_copy(source.at[piece], buffer.at[piece], sems.at[0, at]))
            stores.append(pltpu.make_async_copy(buffer.at[piece], target.at[piece], sems.at[1, at]))
            loads[-1].start()
    for load, store in zip(loads, stores):
        load.wait()
        store.start()
    for store in stores:
        store.wait()


def call_place(arrays):
    count = len(arrays)
    space = [pl.BlockSpec(memory_space=pltpu.HBM)] * count
    return pl.pallas_call(
        lambda *refs: place(count, *refs),
        out_shape=tuple(jax.ShapeDtypeStruct(x.shape, x.dtype) for x in arrays),
        in_specs=space,
        out_specs=tuple(space),
        scratch_shapes=[pltpu.VMEM(x.shape, x.dtype) for x in arrays]
        + [pltpu.SemaphoreType.DMA((2, sum(len(pieces_of(x.shape)) for x in arrays)))],
        compiler_params=pltpu.CompilerParams(vmem_limit_bytes=WIDE_GRANT),
        name="place",
    )(*arrays)


def body(grad_parts, *rest):
    n = lax.axis_size("grp")
    rows, ncol = grad_parts.shape[1:]
    half, block = rows // 2, ncol // n
    if n == 16 and half == 32 and block % 128 == 64:
        return call_place(call_step(n, grad_parts[0], *rest))
    return split_body(grad_parts, *rest)


def solution(mesh):
    in_specs = (
        P("rep", "grp", None),
        P("rep", None, "grp"),
        P("grp", None),
        P("grp", None),
        P("grp", None),
        P("grp", None),
        P(None, "grp"),
        P(None, "grp"),
        P(None, "grp"),
    )
    out_specs = (
        P("grp", None),
        P("grp", None),
        P("grp", None),
        P("grp", None),
        P(None, "grp"),
        P(None, "grp"),
        P(None, "grp"),
    )
    return jax.shard_map(body, mesh=mesh, in_specs=in_specs, out_specs=out_specs, check_vma=False)
```

```python
import jax
import jax.numpy as jnp
from jax import lax
from jax.experimental import pallas as pl
from jax.experimental.pallas import tpu as pltpu
from jax.sharding import PartitionSpec as P

NS_STEPS = 3
GRANT = 24 << 20
WIDE_GRANT = 60 << 20


beta_first = 0.9
beta_second = 0.999
learn_rate = 0.1
galore_scale = 0.25
adam_eps = 1e-08


def exact_dot(left, right):
    return jnp.dot(left, right, precision=lax.Precision.HIGHEST, preferred_element_type=jnp.float32)


def far_first(n):
    return sorted(range(1, n), key=lambda k: abs(k - n // 2))


def peer_copy(src, dst, send_sem, recv_sem, where):
    return pltpu.make_async_remote_copy(
        src_ref=src,
        dst_ref=dst,
        send_sem=send_sem,
        recv_sem=recv_sem,
        device_id=where,
        device_id_type=pl.DeviceIdType.MESH,
    )


def greet(others):
    barrier = pltpu.get_barrier_semaphore()
    for other in others:
        pl.semaphore_signal(barrier, inc=1, device_id=other, device_id_type=pl.DeviceIdType.MESH)
    pl.semaphore_wait(barrier, len(others))


def groups(n):
    fan = 4 if n % 4 == 0 else 1
    return n // fan, fan


def peer_maps(n, me):
    depth, fan = groups(n)
    layer, spot = me // fan, lax.rem(me, fan)
    column = {d: lax.rem(layer + d, depth) * fan + spot for d in range(1, depth)}
    plane = {f: layer * fan + lax.rem(spot + f, fan) for f in range(1, fan)}
    return layer, spot, column, plane


def spread(n, me, ref, send, recv, sent):
    depth, fan = groups(n)
    layer, spot, column, plane = peer_maps(n, me)
    down = []
    for d in sorted(column, key=lambda d: abs(d - depth // 2)):
        down.append((d, peer_copy(ref.at[me], ref.at[me], send.at[d * fan], recv.at[d * fan], {"grp": column[d]})))
        down[-1][1].start()
    for f in plane:
        sent.append(peer_copy(ref.at[me], ref.at[me], send.at[f], recv.at[f], {"grp": plane[f]}))
        sent[-1].start()

    def pass_on():
        for d, copy in down:
            copy.wait()
            slot = lax.rem(layer - d + depth, depth) * fan + spot
            for f in plane:
                at = d * fan + f
                sent.append(peer_copy(ref.at[slot], ref.at[slot], send.at[at], recv.at[at], {"grp": plane[f]}))
                sent[-1].start()

    return pass_on


def split_of(half, block):
    rest = block % 128
    return (block - rest, rest) if 2 * rest == 128 and half % 16 == 0 else (block, 0)


def tails_of(n, half, block):
    rest = split_of(half, block)[1]
    return pltpu.VMEM((n, half // 2, 128) if rest else (1, 8, 128), jnp.float32)


def pack_tails(ref, tails):
    half = ref.shape[1]
    main, rest = split_of(half, ref.shape[2])
    if rest:
        tails[:, :, :rest] = ref[:, : half // 2, main:]
        tails[:, :, rest:] = ref[:, half // 2 :, main:]


def unpack_tails(tails, ref):
    half = ref.shape[1]
    main, rest = split_of(half, ref.shape[2])
    if rest:
        ref[:, : half // 2, main:] = tails[:, :, :rest]
        ref[:, half // 2 :, main:] = tails[:, :, rest:]


def keep_own(me, source, target, tails_out, tails_in):
    target[pl.ds(me, 1)] = source[pl.ds(me, 1)]
    if split_of(*source.shape[1:])[1]:
        tails_in[pl.ds(me, 1)] = tails_out[pl.ds(me, 1)]


def send_block(me, k, where, source, target, tails_out, tails_in, send, recv):
    main, rest = split_of(*source.shape[1:])
    peer = where["grp"]
    copies = [peer_copy(source.at[peer, :, :main], target.at[me, :, :main], send.at[0, k], recv.at[0, k], where)]
    if rest:
        copies.append(peer_copy(tails_out.at[peer], tails_in.at[me], send.at[1, k], recv.at[1, k], where))
    for copy in copies:
        copy.start()
    return copies


def scatter_grad(n, grad, basis, cols, full, mine, swap, parts, tails_out, tails_in, load_sem, swap_sems, basis_send, basis_recv, col_send, col_recv):
    me, rep = lax.axis_index("grp"), lax.axis_index("rep")
    half = swap.shape[0]
    block = cols.shape[2]
    offsets = far_first(n)
    peers = {k: {"grp": lax.rem(me + k, n)} for k in offsets}
    own = pl.ds(pl.multiple_of(rep * half, half), half)
    other = pl.ds(pl.multiple_of((1 - rep) * half, half), half)
    load = pltpu.make_async_copy(grad.at[own], mine, load_sem)
    load.start()
    full[pl.ds(me, 1)] = basis[own][None]
    greet([{"rep": 1 - rep}] + [peers[k] for k in offsets])
    trade = peer_copy(grad.at[other], swap, swap_sems.at[0], swap_sems.at[1], {"rep": 1 - rep})
    trade.start()
    copies = []
    pass_on = spread(n, me, full, basis_send, basis_recv, copies)
    load.wait()
    trade.wait()
    for j in range(n):
        parts[j] = mine[:, j * block : (j + 1) * block] + swap[:, j * block : (j + 1) * block]
    pack_tails(parts, tails_out)
    keep_own(me, parts, cols, tails_out, tails_in)
    late = n // 4
    for at, k in enumerate(offsets):
        if at == late:
            pass_on()
        copies += send_block(me, k, peers[k], parts, cols, tails_out, tails_in, col_send, col_recv)
    for copy in copies:
        copy.wait()
    unpack_tails(tails_in, cols)


def reduce_and_return(
    n, terms, moved, rows, update, near, sums, far, tails_out, tails_in, near_send, near_recv, far_send, far_recv, row_send, row_recv, up_send, up_recv
):
    me = lax.axis_index("grp")
    depth, fan = groups(n)
    layer, spot, column, plane = peer_maps(n, me)
    offsets = far_first(n)
    peers = {k: {"grp": lax.rem(me + k, n)} for k in offsets}
    greet([peers[k] for k in offsets])
    late = []
    waiting = list(offsets)

    def send_update(count):
        for k in waiting[:count]:
            late.extend(send_block(me, k, peers[k], moved, update, tails_out, tails_in, up_send, up_recv))
        del waiting[:count]

    first = []
    for f in plane:
        source = terms.at[:, lax.rem(spot + f, fan)]
        first.append(peer_copy(source, near.at[f], near_send.at[f], near_recv.at[f], {"grp": plane[f]}))
        first[-1].start()
    pack_tails(moved, tails_out)
    send_update(n // 4)
    keep_own(me, moved, update, tails_out, tails_in)
    near[0] = terms[:, pl.ds(spot, 1)][:, 0]
    for copy in first:
        copy.wait()
    partial = near[0]
    for f in plane:
        partial = partial + near[f]
    sums[...] = partial
    second = []
    for d in column:
        source = sums.at[lax.rem(layer + d, depth)]
        second.append(peer_copy(source, far.at[d], far_send.at[d], far_recv.at[d], {"grp": column[d]}))
        second[-1].start()
    send_update(n // 8)
    far[0] = sums[pl.ds(layer, 1)][0]
    for copy in second:
        copy.wait()
    total = far[0]
    for d in column:
        total = total + far[d]
    rows[pl.ds(me, 1)] = total[None]
    pass_on = spread(n, me, rows, row_send, row_recv, late)
    send_update(n // 4)
    pass_on()
    send_update(n)
    for copy in late:
        copy.wait()
    unpack_tails(tails_in, update)


def in_vmem(count):
    return [pl.BlockSpec(memory_space=pltpu.VMEM)] * count


def call_scatter(n, grad, basis):
    rows, ncol = grad.shape
    half, block, rank = rows // 2, ncol // n, basis.shape[1]
    sems = pltpu.SemaphoreType.DMA((n,))
    return pl.pallas_call(
        lambda *refs: scatter_grad(n, *refs),
        out_shape=(
            jax.ShapeDtypeStruct((n, half, block), jnp.float32),
            jax.ShapeDtypeStruct((n, half, rank), jnp.float32),
        ),
        in_specs=[pl.BlockSpec(memory_space=pltpu.HBM)] + in_vmem(1),
        out_specs=tuple(in_vmem(2)),
        scratch_shapes=[
            pltpu.VMEM((half, ncol), jnp.float32),
            pltpu.VMEM((half, ncol), jnp.float32),
            pltpu.VMEM((n, half, block), jnp.float32),
            tails_of(n, half, block),
            tails_of(n, half, block),
            pltpu.SemaphoreType.DMA,
            pltpu.SemaphoreType.DMA((2,)),
            sems,
            sems,
            pltpu.SemaphoreType.DMA((2, n)),
            pltpu.SemaphoreType.DMA((2, n)),
        ],
        compiler_params=pltpu.CompilerParams(collective_id=0, has_side_effects=True, vmem_limit_bytes=GRANT),
        name="scatter_grad",
    )(grad, basis)


def call_return(n, terms, moved):
    half, rank = terms.shape[2:]
    depth, fan = groups(n)
    sems = pltpu.SemaphoreType.DMA((n,))
    return pl.pallas_call(
        lambda *refs: reduce_and_return(n, *refs),
        out_shape=(
            jax.ShapeDtypeStruct((n, half, rank), jnp.float32),
            jax.ShapeDtypeStruct(moved.shape, jnp.float32),
        ),
        in_specs=in_vmem(2),
        out_specs=tuple(in_vmem(2)),
        scratch_shapes=[
            pltpu.VMEM((fan, depth, half, rank), jnp.float32),
            pltpu.VMEM((depth, half, rank), jnp.float32),
            pltpu.VMEM((depth, half, rank), jnp.float32),
            tails_of(*moved.shape),
            tails_of(*moved.shape),
        ]
        + [sems] * 6
        + [pltpu.SemaphoreType.DMA((2, n))] * 2,
        compiler_params=pltpu.CompilerParams(collective_id=1, has_side_effects=True, vmem_limit_bytes=GRANT),
        name="reduce_and_return",
    )(terms, moved)


def split_body(
    grad_parts,
    gain_grad_parts,
    weights,
    basis,
    moment_first,
    moment_second,
    gains,
    gain_first,
    gain_second,
):
    corr_first = 1.0 - beta_first**10
    corr_second = 1.0 - beta_second**10
    n = lax.axis_size("grp")
    rep = lax.axis_index("rep")
    swap = [(0, 1), (1, 0)]
    local_grad = grad_parts[0]
    local_gain = gain_grad_parts[0]
    rows, ncol = local_grad.shape
    half = rows // 2
    block = ncol // n
    rank = basis.shape[1]

    def own_half(x):
        return lax.dynamic_slice_in_dim(x, rep * half, half, 0)

    def swapped(x):
        return lax.ppermute(x, "rep", swap)

    def joined(mine, other):
        return jnp.where(rep == 0, jnp.concatenate([mine, other], 0), jnp.concatenate([other, mine], 0))

    gain_grad = local_gain + swapped(local_gain)
    col_block, half_basis = call_scatter(n, local_grad, basis)
    col_block = col_block.reshape(n * half, block)
    half_basis = half_basis.reshape(n * half, rank)
    partial = exact_dot(col_block.T, half_basis)
    projected = partial + swapped(partial)
    new_first = beta_first * moment_first + (1.0 - beta_first) * projected
    new_second = beta_second * moment_second + (1.0 - beta_second) * projected * projected
    direction = new_first / corr_first / (jnp.sqrt(new_second / corr_second) + adam_eps)
    terms = exact_dot(col_block, projected).reshape(*groups(n), half, rank)
    update_cols = exact_dot(half_basis, direction.T).reshape(n, half, block)
    sub_all, update = call_return(n, terms, update_cols)
    sub_half = lax.dynamic_index_in_dim(sub_all, lax.axis_index("grp"), 0, keepdims=False)
    sub_all = sub_all.reshape(n * half, rank)
    update = jnp.swapaxes(update, 0, 1).reshape(half, ncol)
    gram_half = exact_dot(sub_all.T, sub_all)
    gram = gram_half + swapped(gram_half)
    subspace = joined(sub_half, swapped(sub_half))
    new_half = own_half(weights) - learn_rate * galore_scale * update
    new_weights = joined(new_half, swapped(new_half))
    scale = jnp.sqrt(jnp.sqrt(jnp.sum(gram * gram) + 1e-06))
    iterate = subspace / scale
    current = gram / scale / scale
    for step in range(NS_STEPS):
        iterate = 1.5 * iterate - 0.5 * exact_dot(iterate, current)
        if step + 1 < NS_STEPS:
            side = 1.5 * current - 0.5 * exact_dot(current, current)
            current = 1.5 * side - 0.5 * exact_dot(side, current)
    new_gain_first = beta_first * gain_first + (1.0 - beta_first) * gain_grad
    new_gain_second = beta_second * gain_second + (1.0 - beta_second) * gain_grad * gain_grad
    new_gains = gains - learn_rate * (new_gain_first / corr_first) / (
        jnp.sqrt(new_gain_second / corr_second) + adam_eps
    )
    return (new_weights, new_first, new_second, iterate, new_gains, new_gain_first, new_gain_second)


def halves(x):
    high = x.astype(jnp.bfloat16)
    return high, (x - high.astype(jnp.float32)).astype(jnp.bfloat16)


def three_dots(left, right, dims):
    left_high, left_low = halves(left)
    right_high, right_low = halves(right)

    def product(a, b):
        return lax.dot_general(a, b, (dims, ((), ())), preferred_element_type=jnp.float32)

    return product(left_high, right_high) + (product(left_high, right_low) + product(left_low, right_high))


def plain_dot(left, right):
    return three_dots(left, right, ((1,), (0,)))


def rows_dot(left, right):
    return three_dots(left, right, ((0,), (0,)))


def lanes_dot(left, right):
    return three_dots(left, right, ((1,), (1,)))


def exchange_tails(top, bottom):
    low = lax.broadcasted_iota(jnp.int32, top.shape, 1) < 64
    even = jnp.where(low, top, pltpu.roll(bottom, 64, 1))
    odd = jnp.where(low, pltpu.roll(top, 64, 1), bottom)
    return even, odd


def lane_tiles(ref, group, half, tiles):
    return jnp.concatenate(
        [ref[group, t * half : (t + 1) * half].reshape(-1, 128) for t in range(tiles)], axis=1
    )


def one_step(
    n,
    grad,
    gain_part,
    weights,
    basis,
    moment_first,
    moment_second,
    gains,
    gain_first,
    gain_second,
    new_weights,
    new_first,
    new_second,
    new_basis,
    new_gains,
    new_gain_first,
    new_gain_second,
    mine,
    swap,
    parts,
    cols,
    full,
    partial,
    other_partial,
    projected,
    direction,
    pair_proj,
    first_in,
    second_in,
    weights_in,
    basis_in,
    gain_in,
    gain_mine,
    gain_other,
    terms,
    near,
    sums,
    far,
    rows,
    other_rows,
    gram,
    other_gram,
    up_out,
    up_in,
    chunk_sem,
    trade_send,
    trade_recv,
    load_sem,
    gain_sems,
    basis_send,
    basis_recv,
    col_send,
    col_recv,
    part_send,
    part_recv,
    near_send,
    near_recv,
    far_send,
    far_recv,
    row_send,
    row_recv,
    swap_sems,
    pass_send,
    pass_recv,
    cross_send,
    cross_recv,
    up_send,
    up_recv,
    out_send,
    out_recv,
    store_sem,
):
    corr_first = 1.0 - beta_first**10
    corr_second = 1.0 - beta_second**10
    me, rep = lax.axis_index("grp"), lax.axis_index("rep")
    depth, fan = groups(n)
    layer, spot, column, plane = peer_maps(n, me)
    half, ncol = mine.shape
    wide = 2 * ncol // n
    block = ncol // n
    tiles = block // 128
    main = tiles * 128
    rest = block - main
    rank = basis.shape[1]
    upper, deep = layer // 2, lax.rem(layer, 2)
    line, side = spot // 2, lax.rem(spot, 2)
    partner = {"rep": 1 - rep}
    own = pl.ds(pl.multiple_of(rep * half, half), half)
    other = pl.ds(pl.multiple_of((1 - rep) * half, half), half)
    layers = [2 * (1 - upper) + deep, 2 * (1 - upper) + 1 - deep, 2 * upper + 1 - deep, layer]
    order = [(z, y) for z in layers for y in (line, 1 - line)]
    order[-2:] = order[-2:][::-1]
    spans = [pl.ds(pl.multiple_of((z * 2 + y) * wide, 128), wide) for z, y in order]

    loads = [
        pltpu.make_async_copy(grad.at[own, span], mine.at[:, span], chunk_sem.at[i]) for i, span in enumerate(spans)
    ]
    for load in loads:
        load.start()
    basis_load = pltpu.make_async_copy(basis, basis_in, load_sem.at[0])
    basis_load.start()
    small = [
        pltpu.make_async_copy(gain_part.at[0], gain_mine, load_sem.at[1]),
        pltpu.make_async_copy(gains, gain_in.at[0], load_sem.at[2]),
        pltpu.make_async_copy(gain_first, gain_in.at[1], load_sem.at[3]),
        pltpu.make_async_copy(gain_second, gain_in.at[2], load_sem.at[4]),
        pltpu.make_async_copy(moment_first, first_in, load_sem.at[5]),
        pltpu.make_async_copy(moment_second, second_in, load_sem.at[6]),
        pltpu.make_async_copy(weights.at[own], weights_in, load_sem.at[7]),
    ]
    greet([partner] + [{"grp": lax.rem(me + k, n)} for k in far_first(n)])
    late = []
    trades = [
        peer_copy(grad.at[other, span], swap.at[:, span], trade_send.at[i], trade_recv.at[i], partner)
        for i, span in enumerate(spans)
    ]
    for trade in trades:
        trade.start()
    basis_load.wait()
    full[pl.ds(me, 1)] = basis_in[own][None]
    pass_basis = spread(n, me, full, basis_send, basis_recv, late)
    for load in small:
        load.start()

    for i, (z, y) in enumerate(order):
        loads[i].wait()
        trades[i].wait()
        span = spans[i]
        total = mine[:, span] + swap[:, span]
        base = (z * 2 + y) * 2
        even_tail, odd_tail = exchange_tails(total[: half // 2, main : main + 128], total[half // 2 :, main : main + 128])
        packed = [
            [total[:, 128 * t : 128 * (t + 1)] for t in range(tiles)] + [even_tail],
            [total[:, main + 128 * (t + 1) : main + 128 * (t + 2)] for t in range(tiles)] + [odd_tail],
        ]
        last = i + 1 == len(order)
        for x in range(2):
            at = 0
            for piece in packed[x]:
                parts[base + x, at : at + piece.shape[0]] = piece
                at += piece.shape[0]
        for x in [1 - side] if last else [side, 1 - side]:
            copy = peer_copy(
                parts.at[base + x], cols.at[me], col_send.at[base + x], col_recv.at[me], {"grp": base + x}
            )
            copy.start()
        if i == 1:
            pass_basis()
    cols[pl.ds(me, 1)] = parts[pl.ds(me, 1)]
    for copy in late:
        copy.wait()
    late = []
    gain_trade = peer_copy(gain_mine, gain_other, gain_sems.at[0], gain_sems.at[1], partner)
    small[0].wait()
    gain_trade.start()

    def landed(buffer, send, recv, source):
        return peer_copy(buffer.at[source], buffer.at[source], send.at[source], recv.at[source], {"grp": source})

    near_group = pl.ds(pl.multiple_of(upper * (n // 2), n // 2), n // 2)
    far_group = pl.ds(pl.multiple_of((1 - upper) * (n // 2), n // 2), n // 2)
    near_sources = [2 * (2 * z + y) + x for z, y in order[4:] for x in (side, 1 - side)]
    far_sources = [2 * (2 * z + y) + x for z, y in order[:4] for x in (side, 1 - side)]
    del near_sources[-2]

    def products(group):
        depths = full[group].reshape(-1, rank)
        tops = full[group, : half // 2].reshape(-1, rank)
        bottoms = full[group, half // 2 :].reshape(-1, rank)
        left = lane_tiles(cols, group, half, tiles)
        tail = cols[group, tiles * half :].reshape(-1, 128)
        yield rows_dot(left[:, : main // 2], depths)
        yield rows_dot(left[:, main // 2 :], depths)
        yield rows_dot(tail, tops)[:rest] + rows_dot(tail, bottoms)[rest:]

    pieces = [pl.ds(0, main // 2), pl.ds(main // 2, main // 2), pl.ds(main, rest)]
    for source in near_sources:
        landed(cols, col_send, col_recv, source).wait_recv()
    for piece, product in zip(pieces, products(near_group)):
        partial[piece] = product
    for source in far_sources:
        landed(cols, col_send, col_recv, source).wait_recv()
    joins = []
    for i, (piece, product) in enumerate(zip(pieces, products(far_group))):
        partial[piece] += product
        joins.append(peer_copy(partial.at[piece], other_partial.at[piece], part_send.at[i], part_recv.at[i], partner))
        joins[-1].start()
    small[4].wait()
    small[5].wait()
    natural = [
        pl.ds(pl.multiple_of(side * rest, rest), main // 2),
        pl.ds(pl.multiple_of(side * rest + main // 2, rest), main // 2),
        pl.ds(pl.multiple_of((1 - side) * main, rest), rest),
    ]
    for piece, place, join in zip(pieces, natural, joins):
        join.wait()
        proj = partial[piece] + other_partial[piece]
        projected[piece] = proj
        first = beta_first * first_in[place] + (1.0 - beta_first) * proj
        second = beta_second * second_in[place] + (1.0 - beta_second) * proj * proj
        first_in[place] = first
        second_in[place] = second
        direction[layer, piece] = first / corr_first / (jnp.sqrt(second / corr_second) + adam_eps)
    stores = []

    def store(source, target):
        stores.append(pltpu.make_async_copy(source, target, store_sem.at[len(stores)]))
        stores[-1].start()

    store(first_in, new_first)
    store(second_in, new_second)
    part = block // 4
    ranges = [pl.ds(pl.multiple_of(rep * (block // 2) + c * part, 8), part) for c in range(2)]
    inner = jnp.logical_and(layer > 0, layer < depth - 1)
    low = layer < 2
    mirrored = jnp.where(low, layer, depth - 1 - layer)
    origins = [jnp.where(low, k, depth - 1 - k) for k in (1 - mirrored, 2, 3)]

    def pass_copy(origin, c, toward, at):
        chip = jnp.clip(layer + toward, 0, depth - 1) * fan + spot
        held = direction.at[origin, ranges[c]]
        return peer_copy(held, held, pass_send.at[at, c], pass_recv.at[origin, c], {"grp": chip})

    def own_pass(act):
        for c in range(2):

            @pl.when(layer < depth - 1)
            def _():
                act(pass_copy(layer, c, 1, 0))

            @pl.when(layer > 0)
            def _():
                act(pass_copy(layer, c, -1, 1))

    own_pass(lambda copy: copy.start())

    def cross_copy(k, c):
        held = direction.at[origins[k], ranges[c]]
        return peer_copy(held, held, cross_send.at[k, c], cross_recv.at[k, c], partner)

    def forward(k, c):
        return pass_copy(origins[k], c, jnp.where(origins[k] < layer, 1, -1), 2 + k)

    def take_pass(k):
        for c in range(2):
            forward(k, c).wait_recv()

            @pl.when(inner)
            def _():
                forward(k, c).start()

            cross_copy(k, c).start()

    def take_pass_if(chosen, k):
        @pl.when(chosen)
        def _():
            take_pass(k)

    blank = jnp.zeros((rest, rank), jnp.float32)

    def paired(tail):
        return jnp.concatenate(
            [jnp.concatenate([tail, blank], axis=1), jnp.concatenate([blank, tail], axis=1)], axis=0
        )

    pair_proj[...] = paired(projected[main:])

    whole = plain_dot(lane_tiles(cols, pl.ds(0, n), half, tiles), projected[:main]).reshape(n, half, rank)
    tail = plain_dot(cols[:, tiles * half :].reshape(-1, 128), pair_proj[...])
    terms[:, : half // 2] = whole[:, : half // 2] + tail[:, :rank].reshape(n, half // 2, rank)
    terms[:, half // 2 :] = whole[:, half // 2 :] + tail[:, rank:].reshape(n, half // 2, rank)

    first_hop = []
    for f in plane:
        for d in range(depth):
            source = d * fan + lax.rem(spot + f, fan)
            first_hop.append(
                peer_copy(
                    terms.at[source],
                    near.at[f * depth + d],
                    near_send.at[f * depth + d],
                    near_recv.at[f * depth + d],
                    {"grp": plane[f]},
                )
            )
            first_hop[-1].start()

    beside = pl.ds(pl.multiple_of(layer * fan, fan), fan)

    def make_update(origin):
        group = pl.ds(pl.multiple_of(origin * fan, fan), fan)
        depths = full[beside].reshape(-1, rank)
        sides = jnp.concatenate(
            [full[beside, : half // 2].reshape(-1, rank), full[beside, half // 2 :].reshape(-1, rank)], axis=1
        )
        wide_part = lanes_dot(depths, direction[origin, :main])
        for t in range(tiles):
            up_out[group, t * half : (t + 1) * half] = wide_part[:, 128 * t : 128 * (t + 1)].reshape(fan, half, 128)
        up_out[group, tiles * half :] = lanes_dot(sides, paired(direction[origin, main:])).reshape(fan, half // 2, 128)

    def send_update(origin):
        for f in plane:
            at = origin * fan + lax.rem(spot + f, fan)
            peer_copy(
                up_out.at[at],
                up_in.at[origin * fan + spot],
                up_send.at[at],
                up_recv.at[origin * fan + spot],
                {"grp": plane[f]},
            ).start()
        up_in[pl.ds(origin * fan + spot, 1)] = up_out[pl.ds(origin * fan + spot, 1)]

    def take_update(k):
        for c in range(2):
            cross_copy(k, c).wait_recv()
        make_update(origins[k])
        send_update(origins[k])

    rate = learn_rate * galore_scale
    returns = []

    def take_weights(k):
        z = ([layer] + origins)[k]
        for j, y in enumerate((line, 1 - line)):
            base = (z * 2 + y) * 2
            for x in [1 - side] if j == 0 else [side, 1 - side]:
                landed(up_in, up_send, up_recv, base + x).wait_recv()
            start = pl.multiple_of((z * 2 + y) * wide, 128)
            top, bottom = exchange_tails(up_in[base, tiles * half :], up_in[base + 1, tiles * half :])
            for t in range(2 * tiles + 1):
                lanes = pl.ds(pl.multiple_of(start + 128 * t, 128), 128)
                if t < tiles:
                    change = up_in[base, t * half : (t + 1) * half]
                elif t == tiles:
                    change = jnp.concatenate([top, bottom], axis=0)
                else:
                    change = up_in[base + 1, (t - tiles - 1) * half : (t - tiles) * half]
                weights_in[:, lanes] = weights_in[:, lanes] - rate * change
            ready = weights_in.at[:, pl.ds(start, wide)]
            target = new_weights.at[own, pl.ds(start, wide)]
            i = len(returns)
            returns.append(peer_copy(ready, target, out_send.at[i], out_recv.at[i], partner))
            returns[-1].start()
            store(ready, target)

    make_update(layer)
    for copy in first_hop:
        copy.wait()
    for d in range(depth):
        total = terms[d * fan + spot]
        for f in plane:
            total = total + near[f * depth + d]
        sums[d] = total
    second_hop = []
    for d in column:
        source = sums.at[lax.rem(layer + d, depth)]
        second_hop.append(peer_copy(source, far.at[d], far_send.at[d], far_recv.at[d], {"grp": column[d]}))
        second_hop[-1].start()
    send_update(layer)
    take_pass(0)
    take_pass_if(inner, 1)
    for copy in second_hop:
        copy.wait()
    total = sums[layer]
    for d in column:
        total = total + far[d]
    rows[pl.ds(me, 1)] = total[None]
    pass_rows = spread(n, me, rows, row_send, row_recv, late)
    row_trade = peer_copy(rows.at[me], other_rows, swap_sems.at[0], swap_sems.at[1], partner)
    row_trade.start()
    take_update(0)

    for load in small[1:4]:
        load.wait()
    gain_trade.wait()
    gain_grad = gain_mine[...] + gain_other[...]
    gain_one = beta_first * gain_in[1] + (1.0 - beta_first) * gain_grad
    gain_two = beta_second * gain_in[2] + (1.0 - beta_second) * gain_grad * gain_grad
    gain_in[0] = gain_in[0] - learn_rate * (gain_one / corr_first) / (jnp.sqrt(gain_two / corr_second) + adam_eps)
    gain_in[1] = gain_one
    gain_in[2] = gain_two
    store(gain_in.at[0], new_gains)
    store(gain_in.at[1], new_gain_first)
    store(gain_in.at[2], new_gain_second)

    take_pass_if(inner, 2)
    pass_rows()
    take_pass_if(jnp.logical_not(inner), 1)
    take_update(1)
    small[6].wait()
    take_weights(0)
    for copy in late:
        copy.wait()
    everything = rows[...].reshape(-1, rank)
    gram[...] = rows_dot(everything, everything)
    gram_trade = peer_copy(gram, other_gram, swap_sems.at[2], swap_sems.at[3], partner)
    gram_trade.start()
    take_pass_if(jnp.logical_not(inner), 2)
    take_weights(1)
    row_trade.wait()
    gram_trade.wait()
    take_update(2)
    take_weights(2)
    current = gram[...] + other_gram[...]
    scale = jnp.sqrt(jnp.sqrt(jnp.sum(current * current, keepdims=True) + 1e-06))
    current = current / scale / scale
    first_rows = rows[me]
    second_rows = other_rows[...]
    upper_rows = jnp.where(rep == 0, first_rows, second_rows)
    lower_rows = jnp.where(rep == 0, second_rows, first_rows)
    iterate = jnp.concatenate([upper_rows, lower_rows], axis=0) / scale
    for step in range(NS_STEPS):
        iterate = 1.5 * iterate - 0.5 * plain_dot(iterate, current)
        if step + 1 < NS_STEPS:
            factor = 1.5 * current - 0.5 * plain_dot(current, current)
            current = 1.5 * factor - 0.5 * plain_dot(factor, current)
    basis_in[...] = iterate
    store(basis_in, new_basis)

    take_weights(3)
    for source in far_sources + near_sources:
        landed(parts, col_send, col_recv, source).wait_send()
    for origin in [layer] + origins:
        for f in plane:
            landed(up_out, up_send, up_recv, origin * fan + lax.rem(spot + f, fan)).wait_send()
    own_pass(lambda copy: copy.wait_send())
    for k in range(3):
        for c in range(2):
            cross_copy(k, c).wait_send()

            @pl.when(inner)
            def _():
                forward(k, c).wait_send()

    for copy in returns + stores:
        copy.wait()


def call_step(n, *arrays):
    grad, gain_part, weights, basis, moment_first, moment_second, gains, gain_first, gain_second = arrays
    rows, ncol = grad.shape
    half, block, rank = rows // 2, ncol // n, basis.shape[1]
    depth, fan = groups(n)
    message = half * block // 128
    pairs = n // 2

    def held(*shape):
        return pltpu.VMEM(shape, jnp.float32)

    def sems(*shape):
        return pltpu.SemaphoreType.DMA(shape)

    return pl.pallas_call(
        lambda *refs: one_step(n, *refs),
        out_shape=tuple(
            jax.ShapeDtypeStruct(x.shape, jnp.float32)
            for x in (weights, moment_first, moment_second, basis, gains, gain_first, gain_second)
        ),
        in_specs=[pl.BlockSpec(memory_space=pltpu.HBM)] * 9,
        out_specs=tuple([pl.BlockSpec(memory_space=pltpu.HBM)] * 7),
        scratch_shapes=[
            held(half, ncol),
            held(half, ncol),
            held(n, message, 128),
            held(n, message, 128),
            held(n, half, rank),
            held(block, rank),
            held(block, rank),
            held(block, rank),
            held(depth, block, rank),
            held(128, 2 * rank),
            held(block, rank),
            held(block, rank),
            held(half, ncol),
            held(rows, rank),
            held(3, 2, rows),
            held(2, rows),
            held(2, rows),
            held(n, half, rank),
            held(n, half, rank),
            held(depth, half, rank),
            held(depth, half, rank),
            held(n, half, rank),
            held(half, rank),
            held(rank, rank),
            held(rank, rank),
            held(n, message, 128),
            held(n, message, 128),
            sems(pairs),
            sems(pairs),
            sems(pairs),
            sems(8),
            sems(2),
            sems(n),
            sems(n),
            sems(n),
            sems(n),
            sems(3),
            sems(3),
            sems(n),
            sems(n),
            sems(n),
            sems(n),
            sems(n),
            sems(n),
            sems(4),
            sems(5, 2),
            sems(depth, 2),
            sems(3, 2),
            sems(3, 2),
            sems(n),
            sems(n),
            sems(pairs),
            sems(pairs),
            sems(pairs + 6),
        ],
        compiler_params=pltpu.CompilerParams(collective_id=2, has_side_effects=True, vmem_limit_bytes=WIDE_GRANT),
        name="one_step",
    )(*arrays)


def pieces_of(shape):
    count = 1
    while shape[0] % (16 * count) == 0 and shape[0] * shape[1] // count > 1 << 17:
        count *= 2
    size = shape[0] // count
    return [pl.ds(i * size, size) for i in range(count)]


def place(count, *refs):
    sources, targets, held, sems = refs[:count], refs[count : 2 * count], refs[2 * count : 3 * count], refs[-1]
    loads, stores = [], []
    for source, target, buffer in zip(sources, targets, held):
        for piece in pieces_of(source.shape):
            at = len(loads)
            loads.append(pltpu.make_async_copy(source.at[piece], buffer.at[piece], sems.at[0, at]))
            stores.append(pltpu.make_async_copy(buffer.at[piece], target.at[piece], sems.at[1, at]))
            loads[-1].start()
    for load, store in zip(loads, stores):
        load.wait()
        store.start()
    for store in stores:
        store.wait()


def call_place(arrays):
    count = len(arrays)
    space = [pl.BlockSpec(memory_space=pltpu.HBM)] * count
    return pl.pallas_call(
        lambda *refs: place(count, *refs),
        out_shape=tuple(jax.ShapeDtypeStruct(x.shape, x.dtype) for x in arrays),
        in_specs=space,
        out_specs=tuple(space),
        scratch_shapes=[pltpu.VMEM(x.shape, x.dtype) for x in arrays]
        + [pltpu.SemaphoreType.DMA((2, sum(len(pieces_of(x.shape)) for x in arrays)))],
        compiler_params=pltpu.CompilerParams(vmem_limit_bytes=WIDE_GRANT),
        name="place",
    )(*arrays)


def body(grad_parts, *rest):
    n = lax.axis_size("grp")
    rows, ncol = grad_parts.shape[1:]
    half, block = rows // 2, ncol // n
    if n == 16 and half == 32 and block % 128 == 64:
        return call_place(call_step(n, grad_parts[0], *rest))
    return split_body(grad_parts, *rest)


def solution(mesh):
    in_specs = (
        P("rep", "grp", None),
        P("rep", None, "grp"),
        P("grp", None),
        P("grp", None),
        P("grp", None),
        P("grp", None),
        P(None, "grp"),
        P(None, "grp"),
        P(None, "grp"),
    )
    out_specs = (
        P("grp", None),
        P("grp", None),
        P("grp", None),
        P("grp", None),
        P(None, "grp"),
        P(None, "grp"),
        P(None, "grp"),
    )
    return jax.shard_map(body, mesh=mesh, in_specs=in_specs, out_specs=out_specs, check_vma=False)
```

```python
import jax
import jax.numpy as jnp
from jax import lax
from jax.experimental import pallas as pl
from jax.experimental.pallas import tpu as pltpu
from jax.sharding import PartitionSpec as P

NS_STEPS = 3
GRANT = 24 << 20
WIDE_GRANT = 60 << 20


beta_first = 0.9
beta_second = 0.999
learn_rate = 0.1
galore_scale = 0.25
adam_eps = 1e-08


def exact_dot(left, right):
    return jnp.dot(left, right, precision=lax.Precision.HIGHEST, preferred_element_type=jnp.float32)


def far_first(n):
    return sorted(range(1, n), key=lambda k: abs(k - n // 2))


def peer_copy(src, dst, send_sem, recv_sem, where):
    return pltpu.make_async_remote_copy(
        src_ref=src,
        dst_ref=dst,
        send_sem=send_sem,
        recv_sem=recv_sem,
        device_id=where,
        device_id_type=pl.DeviceIdType.MESH,
    )


def greet(others):
    barrier = pltpu.get_barrier_semaphore()
    for other in others:
        pl.semaphore_signal(barrier, inc=1, device_id=other, device_id_type=pl.DeviceIdType.MESH)
    pl.semaphore_wait(barrier, len(others))


def groups(n):
    fan = 4 if n % 4 == 0 else 1
    return n // fan, fan


def peer_maps(n, me):
    depth, fan = groups(n)
    layer, spot = me // fan, lax.rem(me, fan)
    column = {d: lax.rem(layer + d, depth) * fan + spot for d in range(1, depth)}
    plane = {f: layer * fan + lax.rem(spot + f, fan) for f in range(1, fan)}
    return layer, spot, column, plane


def spread(n, me, ref, send, recv, sent):
    depth, fan = groups(n)
    layer, spot, column, plane = peer_maps(n, me)
    down = []
    for d in sorted(column, key=lambda d: abs(d - depth // 2)):
        down.append((d, peer_copy(ref.at[me], ref.at[me], send.at[d * fan], recv.at[d * fan], {"grp": column[d]})))
        down[-1][1].start()
    for f in plane:
        sent.append(peer_copy(ref.at[me], ref.at[me], send.at[f], recv.at[f], {"grp": plane[f]}))
        sent[-1].start()

    def pass_on():
        for d, copy in down:
            copy.wait()
            slot = lax.rem(layer - d + depth, depth) * fan + spot
            for f in plane:
                at = d * fan + f
                sent.append(peer_copy(ref.at[slot], ref.at[slot], send.at[at], recv.at[at], {"grp": plane[f]}))
                sent[-1].start()

    return pass_on


def split_of(half, block):
    rest = block % 128
    return (block - rest, rest) if 2 * rest == 128 and half % 16 == 0 else (block, 0)


def tails_of(n, half, block):
    rest = split_of(half, block)[1]
    return pltpu.VMEM((n, half // 2, 128) if rest else (1, 8, 128), jnp.float32)


def pack_tails(ref, tails):
    half = ref.shape[1]
    main, rest = split_of(half, ref.shape[2])
    if rest:
        tails[:, :, :rest] = ref[:, : half // 2, main:]
        tails[:, :, rest:] = ref[:, half // 2 :, main:]


def unpack_tails(tails, ref):
    half = ref.shape[1]
    main, rest = split_of(half, ref.shape[2])
    if rest:
        ref[:, : half // 2, main:] = tails[:, :, :rest]
        ref[:, half // 2 :, main:] = tails[:, :, rest:]


def keep_own(me, source, target, tails_out, tails_in):
    target[pl.ds(me, 1)] = source[pl.ds(me, 1)]
    if split_of(*source.shape[1:])[1]:
        tails_in[pl.ds(me, 1)] = tails_out[pl.ds(me, 1)]


def send_block(me, k, where, source, target, tails_out, tails_in, send, recv):
    main, rest = split_of(*source.shape[1:])
    peer = where["grp"]
    copies = [peer_copy(source.at[peer, :, :main], target.at[me, :, :main], send.at[0, k], recv.at[0, k], where)]
    if rest:
        copies.append(peer_copy(tails_out.at[peer], tails_in.at[me], send.at[1, k], recv.at[1, k], where))
    for copy in copies:
        copy.start()
    return copies


def scatter_grad(n, grad, basis, cols, full, mine, swap, parts, tails_out, tails_in, load_sem, swap_sems, basis_send, basis_recv, col_send, col_recv):
    me, rep = lax.axis_index("grp"), lax.axis_index("rep")
    half = swap.shape[0]
    block = cols.shape[2]
    offsets = far_first(n)
    peers = {k: {"grp": lax.rem(me + k, n)} for k in offsets}
    own = pl.ds(pl.multiple_of(rep * half, half), half)
    other = pl.ds(pl.multiple_of((1 - rep) * half, half), half)
    load = pltpu.make_async_copy(grad.at[own], mine, load_sem)
    load.start()
    full[pl.ds(me, 1)] = basis[own][None]
    greet([{"rep": 1 - rep}] + [peers[k] for k in offsets])
    trade = peer_copy(grad.at[other], swap, swap_sems.at[0], swap_sems.at[1], {"rep": 1 - rep})
    trade.start()
    copies = []
    pass_on = spread(n, me, full, basis_send, basis_recv, copies)
    load.wait()
    trade.wait()
    for j in range(n):
        parts[j] = mine[:, j * block : (j + 1) * block] + swap[:, j * block : (j + 1) * block]
    pack_tails(parts, tails_out)
    keep_own(me, parts, cols, tails_out, tails_in)
    late = n // 4
    for at, k in enumerate(offsets):
        if at == late:
            pass_on()
        copies += send_block(me, k, peers[k], parts, cols, tails_out, tails_in, col_send, col_recv)
    for copy in copies:
        copy.wait()
    unpack_tails(tails_in, cols)


def reduce_and_return(
    n, terms, moved, rows, update, near, sums, far, tails_out, tails_in, near_send, near_recv, far_send, far_recv, row_send, row_recv, up_send, up_recv
):
    me = lax.axis_index("grp")
    depth, fan = groups(n)
    layer, spot, column, plane = peer_maps(n, me)
    offsets = far_first(n)
    peers = {k: {"grp": lax.rem(me + k, n)} for k in offsets}
    greet([peers[k] for k in offsets])
    late = []
    waiting = list(offsets)

    def send_update(count):
        for k in waiting[:count]:
            late.extend(send_block(me, k, peers[k], moved, update, tails_out, tails_in, up_send, up_recv))
        del waiting[:count]

    first = []
    for f in plane:
        source = terms.at[:, lax.rem(spot + f, fan)]
        first.append(peer_copy(source, near.at[f], near_send.at[f], near_recv.at[f], {"grp": plane[f]}))
        first[-1].start()
    pack_tails(moved, tails_out)
    send_update(n // 4)
    keep_own(me, moved, update, tails_out, tails_in)
    near[0] = terms[:, pl.ds(spot, 1)][:, 0]
    for copy in first:
        copy.wait()
    partial = near[0]
    for f in plane:
        partial = partial + near[f]
    sums[...] = partial
    second = []
    for d in column:
        source = sums.at[lax.rem(layer + d, depth)]
        second.append(peer_copy(source, far.at[d], far_send.at[d], far_recv.at[d], {"grp": column[d]}))
        second[-1].start()
    send_update(n // 8)
    far[0] = sums[pl.ds(layer, 1)][0]
    for copy in second:
        copy.wait()
    total = far[0]
    for d in column:
        total = total + far[d]
    rows[pl.ds(me, 1)] = total[None]
    pass_on = spread(n, me, rows, row_send, row_recv, late)
    send_update(n // 4)
    pass_on()
    send_update(n)
    for copy in late:
        copy.wait()
    unpack_tails(tails_in, update)


def in_vmem(count):
    return [pl.BlockSpec(memory_space=pltpu.VMEM)] * count


def call_scatter(n, grad, basis):
    rows, ncol = grad.shape
    half, block, rank = rows // 2, ncol // n, basis.shape[1]
    sems = pltpu.SemaphoreType.DMA((n,))
    return pl.pallas_call(
        lambda *refs: scatter_grad(n, *refs),
        out_shape=(
            jax.ShapeDtypeStruct((n, half, block), jnp.float32),
            jax.ShapeDtypeStruct((n, half, rank), jnp.float32),
        ),
        in_specs=[pl.BlockSpec(memory_space=pltpu.HBM)] + in_vmem(1),
        out_specs=tuple(in_vmem(2)),
        scratch_shapes=[
            pltpu.VMEM((half, ncol), jnp.float32),
            pltpu.VMEM((half, ncol), jnp.float32),
            pltpu.VMEM((n, half, block), jnp.float32),
            tails_of(n, half, block),
            tails_of(n, half, block),
            pltpu.SemaphoreType.DMA,
            pltpu.SemaphoreType.DMA((2,)),
            sems,
            sems,
            pltpu.SemaphoreType.DMA((2, n)),
            pltpu.SemaphoreType.DMA((2, n)),
        ],
        compiler_params=pltpu.CompilerParams(collective_id=0, has_side_effects=True, vmem_limit_bytes=GRANT),
        name="scatter_grad",
    )(grad, basis)


def call_return(n, terms, moved):
    half, rank = terms.shape[2:]
    depth, fan = groups(n)
    sems = pltpu.SemaphoreType.DMA((n,))
    return pl.pallas_call(
        lambda *refs: reduce_and_return(n, *refs),
        out_shape=(
            jax.ShapeDtypeStruct((n, half, rank), jnp.float32),
            jax.ShapeDtypeStruct(moved.shape, jnp.float32),
        ),
        in_specs=in_vmem(2),
        out_specs=tuple(in_vmem(2)),
        scratch_shapes=[
            pltpu.VMEM((fan, depth, half, rank), jnp.float32),
            pltpu.VMEM((depth, half, rank), jnp.float32),
            pltpu.VMEM((depth, half, rank), jnp.float32),
            tails_of(*moved.shape),
            tails_of(*moved.shape),
        ]
        + [sems] * 6
        + [pltpu.SemaphoreType.DMA((2, n))] * 2,
        compiler_params=pltpu.CompilerParams(collective_id=1, has_side_effects=True, vmem_limit_bytes=GRANT),
        name="reduce_and_return",
    )(terms, moved)


def split_body(
    grad_parts,
    gain_grad_parts,
    weights,
    basis,
    moment_first,
    moment_second,
    gains,
    gain_first,
    gain_second,
):
    corr_first = 1.0 - beta_first**10
    corr_second = 1.0 - beta_second**10
    n = lax.axis_size("grp")
    rep = lax.axis_index("rep")
    swap = [(0, 1), (1, 0)]
    local_grad = grad_parts[0]
    local_gain = gain_grad_parts[0]
    rows, ncol = local_grad.shape
    half = rows // 2
    block = ncol // n
    rank = basis.shape[1]

    def own_half(x):
        return lax.dynamic_slice_in_dim(x, rep * half, half, 0)

    def swapped(x):
        return lax.ppermute(x, "rep", swap)

    def joined(mine, other):
        return jnp.where(rep == 0, jnp.concatenate([mine, other], 0), jnp.concatenate([other, mine], 0))

    gain_grad = local_gain + swapped(local_gain)
    col_block, half_basis = call_scatter(n, local_grad, basis)
    col_block = col_block.reshape(n * half, block)
    half_basis = half_basis.reshape(n * half, rank)
    partial = exact_dot(col_block.T, half_basis)
    projected = partial + swapped(partial)
    new_first = beta_first * moment_first + (1.0 - beta_first) * projected
    new_second = beta_second * moment_second + (1.0 - beta_second) * projected * projected
    direction = new_first / corr_first / (jnp.sqrt(new_second / corr_second) + adam_eps)
    terms = exact_dot(col_block, projected).reshape(*groups(n), half, rank)
    update_cols = exact_dot(half_basis, direction.T).reshape(n, half, block)
    sub_all, update = call_return(n, terms, update_cols)
    sub_half = lax.dynamic_index_in_dim(sub_all, lax.axis_index("grp"), 0, keepdims=False)
    sub_all = sub_all.reshape(n * half, rank)
    update = jnp.swapaxes(update, 0, 1).reshape(half, ncol)
    gram_half = exact_dot(sub_all.T, sub_all)
    gram = gram_half + swapped(gram_half)
    subspace = joined(sub_half, swapped(sub_half))
    new_half = own_half(weights) - learn_rate * galore_scale * update
    new_weights = joined(new_half, swapped(new_half))
    scale = jnp.sqrt(jnp.sqrt(jnp.sum(gram * gram) + 1e-06))
    iterate = subspace / scale
    current = gram / scale / scale
    for step in range(NS_STEPS):
        iterate = 1.5 * iterate - 0.5 * exact_dot(iterate, current)
        if step + 1 < NS_STEPS:
            side = 1.5 * current - 0.5 * exact_dot(current, current)
            current = 1.5 * side - 0.5 * exact_dot(side, current)
    new_gain_first = beta_first * gain_first + (1.0 - beta_first) * gain_grad
    new_gain_second = beta_second * gain_second + (1.0 - beta_second) * gain_grad * gain_grad
    new_gains = gains - learn_rate * (new_gain_first / corr_first) / (
        jnp.sqrt(new_gain_second / corr_second) + adam_eps
    )
    return (new_weights, new_first, new_second, iterate, new_gains, new_gain_first, new_gain_second)


def halves(x):
    high = x.astype(jnp.bfloat16)
    return high, (x - high.astype(jnp.float32)).astype(jnp.bfloat16)


def three_dots(left, right, dims):
    left_high, left_low = halves(left)
    right_high, right_low = halves(right)

    def product(a, b):
        return lax.dot_general(a, b, (dims, ((), ())), preferred_element_type=jnp.float32)

    return product(left_high, right_high) + (product(left_high, right_low) + product(left_low, right_high))


def plain_dot(left, right):
    return three_dots(left, right, ((1,), (0,)))


def rows_dot(left, right):
    return three_dots(left, right, ((0,), (0,)))


def lanes_dot(left, right):
    return three_dots(left, right, ((1,), (1,)))


def exchange_tails(top, bottom):
    low = lax.broadcasted_iota(jnp.int32, top.shape, 1) < 64
    even = jnp.where(low, top, pltpu.roll(bottom, 64, 1))
    odd = jnp.where(low, pltpu.roll(top, 64, 1), bottom)
    return even, odd


def lane_tiles(ref, group, half, tiles):
    return jnp.concatenate(
        [ref[group, t * half : (t + 1) * half].reshape(-1, 128) for t in range(tiles)], axis=1
    )


def one_step(
    n,
    grad,
    gain_part,
    weights,
    basis,
    moment_first,
    moment_second,
    gains,
    gain_first,
    gain_second,
    new_weights,
    new_first,
    new_second,
    new_basis,
    new_gains,
    new_gain_first,
    new_gain_second,
    mine,
    swap,
    parts,
    cols,
    full,
    partial,
    other_partial,
    projected,
    direction,
    pair_proj,
    first_in,
    second_in,
    weights_in,
    basis_in,
    gain_in,
    gain_mine,
    gain_other,
    terms,
    near,
    sums,
    far,
    rows,
    other_rows,
    gram,
    other_gram,
    up_out,
    up_in,
    chunk_sem,
    trade_send,
    trade_recv,
    load_sem,
    gain_sems,
    basis_send,
    basis_recv,
    col_send,
    col_recv,
    part_send,
    part_recv,
    near_send,
    near_recv,
    far_send,
    far_recv,
    row_send,
    row_recv,
    swap_sems,
    pass_send,
    pass_recv,
    cross_send,
    cross_recv,
    up_send,
    up_recv,
    out_send,
    out_recv,
    store_sem,
):
    corr_first = 1.0 - beta_first**10
    corr_second = 1.0 - beta_second**10
    me, rep = lax.axis_index("grp"), lax.axis_index("rep")
    depth, fan = groups(n)
    layer, spot, column, plane = peer_maps(n, me)
    half, ncol = mine.shape
    wide = 2 * ncol // n
    block = ncol // n
    tiles = block // 128
    main = tiles * 128
    rest = block - main
    head = tiles - 1
    early = head * 128
    bands = [pl.ds(0, head * half), pl.ds(head * half, parts.shape[1] - head * half)]
    rank = basis.shape[1]
    upper, deep = layer // 2, lax.rem(layer, 2)
    line, side = spot // 2, lax.rem(spot, 2)
    partner = {"rep": 1 - rep}
    own = pl.ds(pl.multiple_of(rep * half, half), half)
    other = pl.ds(pl.multiple_of((1 - rep) * half, half), half)
    layers = [2 * (1 - upper) + deep, 2 * (1 - upper) + 1 - deep, 2 * upper + 1 - deep, layer]
    order = [(z, y) for z in layers for y in (line, 1 - line)]
    order[-2:] = order[-2:][::-1]
    spans = [pl.ds(pl.multiple_of((z * 2 + y) * wide, 128), wide) for z, y in order]

    loads = [
        pltpu.make_async_copy(grad.at[own, span], mine.at[:, span], chunk_sem.at[i]) for i, span in enumerate(spans)
    ]
    for load in loads:
        load.start()
    basis_load = pltpu.make_async_copy(basis, basis_in, load_sem.at[0])
    basis_load.start()
    small = [
        pltpu.make_async_copy(gain_part.at[0], gain_mine, load_sem.at[1]),
        pltpu.make_async_copy(gains, gain_in.at[0], load_sem.at[2]),
        pltpu.make_async_copy(gain_first, gain_in.at[1], load_sem.at[3]),
        pltpu.make_async_copy(gain_second, gain_in.at[2], load_sem.at[4]),
        pltpu.make_async_copy(moment_first, first_in, load_sem.at[5]),
        pltpu.make_async_copy(moment_second, second_in, load_sem.at[6]),
        pltpu.make_async_copy(weights.at[own], weights_in, load_sem.at[7]),
    ]
    greet([partner] + [{"grp": lax.rem(me + k, n)} for k in far_first(n)])
    late = []
    trades = [
        peer_copy(grad.at[other, span], swap.at[:, span], trade_send.at[i], trade_recv.at[i], partner)
        for i, span in enumerate(spans)
    ]
    for trade in trades:
        trade.start()
    basis_load.wait()
    full[pl.ds(me, 1)] = basis_in[own][None]
    pass_basis = spread(n, me, full, basis_send, basis_recv, late)
    for load in small:
        load.start()

    def col_copy(target, c):
        return peer_copy(
            parts.at[target, bands[c]], cols.at[me, bands[c]], col_send.at[c, target], col_recv.at[c, me], {"grp": target}
        )

    send_order, sent_last = [], []
    pairs = n // 2
    for i, (z, y) in enumerate(order):
        loads[i].wait()
        trades[i].wait()
        span = spans[i]
        total = mine[:, span] + swap[:, span]
        base = (z * 2 + y) * 2
        even_tail, odd_tail = exchange_tails(total[: half // 2, main : main + 128], total[half // 2 :, main : main + 128])
        packed = [
            [total[:, 128 * t : 128 * (t + 1)] for t in range(tiles)] + [even_tail],
            [total[:, main + 128 * (t + 1) : main + 128 * (t + 2)] for t in range(tiles)] + [odd_tail],
        ]
        last = i + 1 == len(order)
        for x in range(2):
            at = 0
            for piece in packed[x]:
                parts[base + x, at : at + piece.shape[0]] = piece
                at += piece.shape[0]
        targets = [base + x for x in ([1 - side] if last else [side, 1 - side])]
        send_order += targets
        for target in targets:
            col_copy(target, 0).start()
        if i >= pairs // 2:
            for target in send_order[len(sent_last) : len(sent_last) + 2]:
                col_copy(target, 1).start()
                sent_last.append(target)
        if i == 1:
            pass_basis()
    for target in send_order[len(sent_last) :]:
        col_copy(target, 1).start()
    cols[pl.ds(me, 1)] = parts[pl.ds(me, 1)]
    for copy in late:
        copy.wait()
    late = []
    gain_trade = peer_copy(gain_mine, gain_other, gain_sems.at[0], gain_sems.at[1], partner)
    small[0].wait()
    gain_trade.start()

    def wait_cols(c):
        for source in send_order[::-1]:
            held = cols.at[source, bands[c]]
            peer_copy(held, held, col_send.at[c, source], col_recv.at[c, source], {"grp": source}).wait_recv()

    pieces = [pl.ds(0, early), pl.ds(early, main - early), pl.ds(main, rest)]
    natural = [
        pl.ds(pl.multiple_of(side * rest, rest), early),
        pl.ds(pl.multiple_of(side * rest + early, rest), main - early),
        pl.ds(pl.multiple_of((1 - side) * main, rest), rest),
    ]

    def join_copy(i):
        return peer_copy(
            partial.at[pieces[i]], other_partial.at[pieces[i]], part_send.at[i], part_recv.at[i], partner
        )

    def finish(i):
        piece, place = pieces[i], natural[i]
        join_copy(i).wait()
        proj = partial[piece] + other_partial[piece]
        projected[piece] = proj
        first = beta_first * first_in[place] + (1.0 - beta_first) * proj
        second = beta_second * second_in[place] + (1.0 - beta_second) * proj * proj
        first_in[place] = first
        second_in[place] = second
        direction[layer, piece] = first / corr_first / (jnp.sqrt(second / corr_second) + adam_eps)

    stores = []

    def store(source, target):
        stores.append(pltpu.make_async_copy(source, target, store_sem.at[len(stores)]))
        stores[-1].start()

    shares = [early // 2, (block - early) // 2]
    ranges = [pl.ds(pl.multiple_of(c * early + rep * shares[c], 8), shares[c]) for c in range(2)]
    inner = jnp.logical_and(layer > 0, layer < depth - 1)
    low = layer < 2
    mirrored = jnp.where(low, layer, depth - 1 - layer)
    origins = [jnp.where(low, k, depth - 1 - k) for k in (1 - mirrored, 2, 3)]

    def pass_copy(origin, c, toward, at):
        chip = jnp.clip(layer + toward, 0, depth - 1) * fan + spot
        held = direction.at[origin, ranges[c]]
        return peer_copy(held, held, pass_send.at[at, c], pass_recv.at[origin, c], {"grp": chip})

    def half_pass(c):
        return pass_copy(layer, c, 1 - 2 * deep, deep)

    def middle_pass(c):
        return pass_copy(layer, c, 2 * deep - 1, 1 - deep)

    def cross_copy(k, c):
        held = direction.at[origins[k], ranges[c]]
        return peer_copy(held, held, cross_send.at[k, c], cross_recv.at[k, c], partner)

    def forward(k, c):
        return pass_copy(origins[k], c, jnp.where(origins[k] < layer, 1, -1), 2 + k)

    def take_pass(k, bands_taken=(0, 1)):
        for c in bands_taken:
            forward(k, c).wait_recv()

            @pl.when(inner)
            def _():
                forward(k, c).start()

            cross_copy(k, c).start()

    def take_pass_if(chosen, k, bands_taken=(0, 1)):
        @pl.when(chosen)
        def _():
            take_pass(k, bands_taken)

    blank = jnp.zeros((rest, rank), jnp.float32)

    def paired(tail):
        return jnp.concatenate(
            [jnp.concatenate([tail, blank], axis=1), jnp.concatenate([blank, tail], axis=1)], axis=0
        )

    beside = pl.ds(pl.multiple_of(layer * fan, fan), fan)

    def make_update(origin, c):
        group = pl.ds(pl.multiple_of(origin * fan, fan), fan)
        begin, end = (0, head) if c == 0 else (head, tiles)
        depths = full[beside].reshape(-1, rank)
        wide_part = lanes_dot(depths, direction[origin, 128 * begin : 128 * end])
        for t in range(end - begin):
            at = (begin + t) * half
            up_out[group, at : at + half] = wide_part[:, 128 * t : 128 * (t + 1)].reshape(fan, half, 128)
        if c == 1:
            sides = jnp.concatenate(
                [full[beside, : half // 2].reshape(-1, rank), full[beside, half // 2 :].reshape(-1, rank)], axis=1
            )
            tail_part = lanes_dot(sides, paired(direction[origin, main:]))
            up_out[group, tiles * half :] = tail_part.reshape(fan, half // 2, 128)

    def update_copy(origin, f, c):
        at = origin * fan + lax.rem(spot + f, fan)
        home = origin * fan + spot
        return peer_copy(
            up_out.at[at, bands[c]],
            up_in.at[home, bands[c]],
            up_send.at[c, at],
            up_recv.at[c, home],
            {"grp": plane[f]},
        )

    def send_update(origin, c):
        for f in plane:
            update_copy(origin, f, c).start()
        home = pl.ds(origin * fan + spot, 1)
        up_in[home, bands[c]] = up_out[home, bands[c]]

    def take_update(k, bands_taken=(0, 1)):
        for c in bands_taken:
            cross_copy(k, c).wait_recv()
            make_update(origins[k], c)
            send_update(origins[k], c)

    def wait_update(source):
        for c in range(2):
            held = up_in.at[source, bands[c]]
            peer_copy(held, held, up_send.at[c, source], up_recv.at[c, source], {"grp": source}).wait_recv()

    wait_cols(0)
    depths = full[...].reshape(-1, rank)
    partial[pieces[0]] = rows_dot(lane_tiles(cols, pl.ds(0, n), half, head), depths)
    join_copy(0).start()
    small[4].wait()
    small[5].wait()
    finish(0)
    half_pass(0).start()
    make_update(layer, 0)
    send_update(layer, 0)
    everyone = pl.ds(0, n)
    terms[...] = plain_dot(lane_tiles(cols, everyone, half, head), projected[:early]).reshape(n, half, rank)
    forward(0, 0).wait_recv()
    cross_copy(0, 0).start()
    wait_cols(1)

    @pl.when(inner)
    def _():
        middle_pass(0).start()
        forward(0, 0).start()

    partial[pieces[1]] = rows_dot(cols[:, head * half : tiles * half].reshape(-1, 128), depths)
    join_copy(1).start()
    tail = cols[:, tiles * half :].reshape(-1, 128)
    tops = full[:, : half // 2].reshape(-1, rank)
    bottoms = full[:, half // 2 :].reshape(-1, rank)
    partial[pieces[2]] = rows_dot(tail, tops)[:rest] + rows_dot(tail, bottoms)[rest:]
    join_copy(2).start()
    finish(1)
    finish(2)
    half_pass(1).start()

    @pl.when(inner)
    def _():
        middle_pass(1).start()

    pair_proj[...] = paired(projected[main:])

    whole = plain_dot(cols[:, head * half : tiles * half].reshape(-1, 128), projected[early:main])
    whole = whole.reshape(n, half, rank)
    tail = plain_dot(cols[:, tiles * half :].reshape(-1, 128), pair_proj[...])
    terms[:, : half // 2] += whole[:, : half // 2] + tail[:, :rank].reshape(n, half // 2, rank)
    terms[:, half // 2 :] += whole[:, half // 2 :] + tail[:, rank:].reshape(n, half // 2, rank)

    first_hop = []
    for f in plane:
        for d in range(depth):
            source = d * fan + lax.rem(spot + f, fan)
            first_hop.append(
                peer_copy(
                    terms.at[source],
                    near.at[f * depth + d],
                    near_send.at[f * depth + d],
                    near_recv.at[f * depth + d],
                    {"grp": plane[f]},
                )
            )
            first_hop[-1].start()

    rate = learn_rate * galore_scale
    returns = []

    def take_weights(k):
        z = ([layer] + origins)[k]
        for j, y in enumerate((line, 1 - line)):
            base = (z * 2 + y) * 2
            for x in [1 - side] if j == 0 else [side, 1 - side]:
                wait_update(base + x)
            start = pl.multiple_of((z * 2 + y) * wide, 128)
            top, bottom = exchange_tails(up_in[base, tiles * half :], up_in[base + 1, tiles * half :])
            for t in range(2 * tiles + 1):
                lanes = pl.ds(pl.multiple_of(start + 128 * t, 128), 128)
                if t < tiles:
                    change = up_in[base, t * half : (t + 1) * half]
                elif t == tiles:
                    change = jnp.concatenate([top, bottom], axis=0)
                else:
                    change = up_in[base + 1, (t - tiles - 1) * half : (t - tiles) * half]
                weights_in[:, lanes] = weights_in[:, lanes] - rate * change
            ready = weights_in.at[:, pl.ds(start, wide)]
            target = new_weights.at[own, pl.ds(start, wide)]
            i = len(returns)
            returns.append(peer_copy(ready, target, out_send.at[i], out_recv.at[i], partner))
            returns[-1].start()
            store(ready, target)

    store(first_in, new_first)
    store(second_in, new_second)
    make_update(layer, 1)
    take_update(0, (0,))
    for copy in first_hop:
        copy.wait()
    for d in range(depth):
        total = terms[d * fan + spot]
        for f in plane:
            total = total + near[f * depth + d]
        sums[d] = total
    second_hop = []
    for d in column:
        source = sums.at[lax.rem(layer + d, depth)]
        second_hop.append(peer_copy(source, far.at[d], far_send.at[d], far_recv.at[d], {"grp": column[d]}))
        second_hop[-1].start()
    send_update(layer, 1)
    take_pass(0, (1,))
    take_pass_if(inner, 1)
    for copy in second_hop:
        copy.wait()
    total = sums[layer]
    for d in column:
        total = total + far[d]
    rows[pl.ds(me, 1)] = total[None]
    pass_rows = spread(n, me, rows, row_send, row_recv, late)
    row_trade = peer_copy(rows.at[me], other_rows, swap_sems.at[0], swap_sems.at[1], partner)
    row_trade.start()
    take_update(0, (1,))

    for load in small[1:4]:
        load.wait()
    gain_trade.wait()
    gain_grad = gain_mine[...] + gain_other[...]
    gain_one = beta_first * gain_in[1] + (1.0 - beta_first) * gain_grad
    gain_two = beta_second * gain_in[2] + (1.0 - beta_second) * gain_grad * gain_grad
    gain_in[0] = gain_in[0] - learn_rate * (gain_one / corr_first) / (jnp.sqrt(gain_two / corr_second) + adam_eps)
    gain_in[1] = gain_one
    gain_in[2] = gain_two
    store(gain_in.at[0], new_gains)
    store(gain_in.at[1], new_gain_first)
    store(gain_in.at[2], new_gain_second)

    take_pass_if(inner, 2)
    pass_rows()
    take_pass_if(jnp.logical_not(inner), 1)
    take_update(1)
    take_pass_if(jnp.logical_not(inner), 2, (0,))
    take_update(2, (0,))
    small[6].wait()
    take_weights(0)
    for copy in late:
        copy.wait()
    everything = rows[...].reshape(-1, rank)
    gram[...] = rows_dot(everything, everything)
    gram_trade = peer_copy(gram, other_gram, swap_sems.at[2], swap_sems.at[3], partner)
    gram_trade.start()
    take_pass_if(jnp.logical_not(inner), 2, (1,))
    take_weights(1)
    row_trade.wait()
    gram_trade.wait()
    take_update(2, (1,))
    current = gram[...] + other_gram[...]
    scale = jnp.sqrt(jnp.sqrt(jnp.sum(current * current, keepdims=True) + 1e-06))
    current = current / scale / scale
    my_rows = rows[me]
    their_rows = other_rows[...]
    upper_rows = jnp.where(rep == 0, my_rows, their_rows)
    lower_rows = jnp.where(rep == 0, their_rows, my_rows)
    iterate = jnp.concatenate([upper_rows, lower_rows], axis=0) / scale
    for step in range(NS_STEPS):
        iterate = 1.5 * iterate - 0.5 * plain_dot(iterate, current)
        if step + 1 < NS_STEPS:
            factor = 1.5 * current - 0.5 * plain_dot(current, current)
            current = 1.5 * factor - 0.5 * plain_dot(factor, current)
    basis_in[...] = iterate
    store(basis_in, new_basis)

    take_weights(2)
    take_weights(3)
    for target in send_order:
        for c in range(2):
            col_copy(target, c).wait_send()
    for origin in [layer] + origins:
        for f in plane:
            for c in range(2):
                update_copy(origin, f, c).wait_send()
    for c in range(2):
        half_pass(c).wait_send()

        @pl.when(inner)
        def _():
            middle_pass(c).wait_send()

    for k in range(3):
        for c in range(2):
            cross_copy(k, c).wait_send()

            @pl.when(inner)
            def _():
                forward(k, c).wait_send()

    for copy in returns + stores:
        copy.wait()


def call_step(n, *arrays):
    grad, gain_part, weights, basis, moment_first, moment_second, gains, gain_first, gain_second = arrays
    rows, ncol = grad.shape
    half, block, rank = rows // 2, ncol // n, basis.shape[1]
    depth, fan = groups(n)
    message = half * block // 128
    pairs = n // 2

    def held(*shape):
        return pltpu.VMEM(shape, jnp.float32)

    def sems(*shape):
        return pltpu.SemaphoreType.DMA(shape)

    return pl.pallas_call(
        lambda *refs: one_step(n, *refs),
        out_shape=tuple(
            jax.ShapeDtypeStruct(x.shape, jnp.float32)
            for x in (weights, moment_first, moment_second, basis, gains, gain_first, gain_second)
        ),
        in_specs=[pl.BlockSpec(memory_space=pltpu.HBM)] * 9,
        out_specs=tuple([pl.BlockSpec(memory_space=pltpu.HBM)] * 7),
        scratch_shapes=[
            held(half, ncol),
            held(half, ncol),
            held(n, message, 128),
            held(n, message, 128),
            held(n, half, rank),
            held(block, rank),
            held(block, rank),
            held(block, rank),
            held(depth, block, rank),
            held(128, 2 * rank),
            held(block, rank),
            held(block, rank),
            held(half, ncol),
            held(rows, rank),
            held(3, 2, rows),
            held(2, rows),
            held(2, rows),
            held(n, half, rank),
            held(n, half, rank),
            held(depth, half, rank),
            held(depth, half, rank),
            held(n, half, rank),
            held(half, rank),
            held(rank, rank),
            held(rank, rank),
            held(n, message, 128),
            held(n, message, 128),
            sems(pairs),
            sems(pairs),
            sems(pairs),
            sems(8),
            sems(2),
            sems(n),
            sems(n),
            sems(2, n),
            sems(2, n),
            sems(3),
            sems(3),
            sems(n),
            sems(n),
            sems(n),
            sems(n),
            sems(n),
            sems(n),
            sems(4),
            sems(5, 2),
            sems(depth, 2),
            sems(3, 2),
            sems(3, 2),
            sems(2, n),
            sems(2, n),
            sems(pairs),
            sems(pairs),
            sems(pairs + 6),
        ],
        compiler_params=pltpu.CompilerParams(collective_id=2, has_side_effects=True, vmem_limit_bytes=WIDE_GRANT),
        name="one_step",
    )(*arrays)


def pieces_of(shape):
    count = 1
    while shape[0] % (16 * count) == 0 and shape[0] * shape[1] // count > 1 << 17:
        count *= 2
    size = shape[0] // count
    return [pl.ds(i * size, size) for i in range(count)]


def place(count, *refs):
    sources, targets, held, sems = refs[:count], refs[count : 2 * count], refs[2 * count : 3 * count], refs[-1]
    loads, stores = [], []
    for source, target, buffer in zip(sources, targets, held):
        for piece in pieces_of(source.shape):
            at = len(loads)
            loads.append(pltpu.make_async_copy(source.at[piece], buffer.at[piece], sems.at[0, at]))
            stores.append(pltpu.make_async_copy(buffer.at[piece], target.at[piece], sems.at[1, at]))
            loads[-1].start()
    for load, store in zip(loads, stores):
        load.wait()
        store.start()
    for store in stores:
        store.wait()


def call_place(arrays):
    count = len(arrays)
    space = [pl.BlockSpec(memory_space=pltpu.HBM)] * count
    return pl.pallas_call(
        lambda *refs: place(count, *refs),
        out_shape=tuple(jax.ShapeDtypeStruct(x.shape, x.dtype) for x in arrays),
        in_specs=space,
        out_specs=tuple(space),
        scratch_shapes=[pltpu.VMEM(x.shape, x.dtype) for x in arrays]
        + [pltpu.SemaphoreType.DMA((2, sum(len(pieces_of(x.shape)) for x in arrays)))],
        compiler_params=pltpu.CompilerParams(vmem_limit_bytes=WIDE_GRANT),
        name="place",
    )(*arrays)


def body(grad_parts, *rest):
    n = lax.axis_size("grp")
    rows, ncol = grad_parts.shape[1:]
    half, block = rows // 2, ncol // n
    if n == 16 and half == 32 and block % 128 == 64:
        return call_place(call_step(n, grad_parts[0], *rest))
    return split_body(grad_parts, *rest)


def solution(mesh):
    in_specs = (
        P("rep", "grp", None),
        P("rep", None, "grp"),
        P("grp", None),
        P("grp", None),
        P("grp", None),
        P("grp", None),
        P(None, "grp"),
        P(None, "grp"),
        P(None, "grp"),
    )
    out_specs = (
        P("grp", None),
        P("grp", None),
        P("grp", None),
        P("grp", None),
        P(None, "grp"),
        P(None, "grp"),
        P(None, "grp"),
    )
    return jax.shard_map(body, mesh=mesh, in_specs=in_specs, out_specs=out_specs, check_vma=False)
```

```python
import jax
import jax.numpy as jnp
from jax import lax
from jax.experimental import pallas as pl
from jax.experimental.pallas import tpu as pltpu
from jax.sharding import PartitionSpec as P

NS_STEPS = 3
GRANT = 24 << 20
WIDE_GRANT = 60 << 20


beta_first = 0.9
beta_second = 0.999
learn_rate = 0.1
galore_scale = 0.25
adam_eps = 1e-08


def exact_dot(left, right):
    return jnp.dot(left, right, precision=lax.Precision.HIGHEST, preferred_element_type=jnp.float32)


def far_first(n):
    return sorted(range(1, n), key=lambda k: abs(k - n // 2))


def peer_copy(src, dst, send_sem, recv_sem, where):
    return pltpu.make_async_remote_copy(
        src_ref=src,
        dst_ref=dst,
        send_sem=send_sem,
        recv_sem=recv_sem,
        device_id=where,
        device_id_type=pl.DeviceIdType.MESH,
    )


def greet(others):
    barrier = pltpu.get_barrier_semaphore()
    for other in others:
        pl.semaphore_signal(barrier, inc=1, device_id=other, device_id_type=pl.DeviceIdType.MESH)
    pl.semaphore_wait(barrier, len(others))


def groups(n):
    fan = 4 if n % 4 == 0 else 1
    return n // fan, fan


def peer_maps(n, me):
    depth, fan = groups(n)
    layer, spot = me // fan, lax.rem(me, fan)
    column = {d: lax.rem(layer + d, depth) * fan + spot for d in range(1, depth)}
    plane = {f: layer * fan + lax.rem(spot + f, fan) for f in range(1, fan)}
    return layer, spot, column, plane


def spread(n, me, ref, send, recv, sent):
    depth, fan = groups(n)
    layer, spot, column, plane = peer_maps(n, me)
    down = []
    for d in sorted(column, key=lambda d: abs(d - depth // 2)):
        down.append((d, peer_copy(ref.at[me], ref.at[me], send.at[d * fan], recv.at[d * fan], {"grp": column[d]})))
        down[-1][1].start()
    for f in plane:
        sent.append(peer_copy(ref.at[me], ref.at[me], send.at[f], recv.at[f], {"grp": plane[f]}))
        sent[-1].start()

    def pass_on():
        for d, copy in down:
            copy.wait()
            slot = lax.rem(layer - d + depth, depth) * fan + spot
            for f in plane:
                at = d * fan + f
                sent.append(peer_copy(ref.at[slot], ref.at[slot], send.at[at], recv.at[at], {"grp": plane[f]}))
                sent[-1].start()

    return pass_on


def split_of(half, block):
    rest = block % 128
    return (block - rest, rest) if 2 * rest == 128 and half % 16 == 0 else (block, 0)


def tails_of(n, half, block):
    rest = split_of(half, block)[1]
    return pltpu.VMEM((n, half // 2, 128) if rest else (1, 8, 128), jnp.float32)


def pack_tails(ref, tails):
    half = ref.shape[1]
    main, rest = split_of(half, ref.shape[2])
    if rest:
        tails[:, :, :rest] = ref[:, : half // 2, main:]
        tails[:, :, rest:] = ref[:, half // 2 :, main:]


def unpack_tails(tails, ref):
    half = ref.shape[1]
    main, rest = split_of(half, ref.shape[2])
    if rest:
        ref[:, : half // 2, main:] = tails[:, :, :rest]
        ref[:, half // 2 :, main:] = tails[:, :, rest:]


def keep_own(me, source, target, tails_out, tails_in):
    target[pl.ds(me, 1)] = source[pl.ds(me, 1)]
    if split_of(*source.shape[1:])[1]:
        tails_in[pl.ds(me, 1)] = tails_out[pl.ds(me, 1)]


def send_block(me, k, where, source, target, tails_out, tails_in, send, recv):
    main, rest = split_of(*source.shape[1:])
    peer = where["grp"]
    copies = [peer_copy(source.at[peer, :, :main], target.at[me, :, :main], send.at[0, k], recv.at[0, k], where)]
    if rest:
        copies.append(peer_copy(tails_out.at[peer], tails_in.at[me], send.at[1, k], recv.at[1, k], where))
    for copy in copies:
        copy.start()
    return copies


def scatter_grad(n, grad, basis, cols, full, mine, swap, parts, tails_out, tails_in, load_sem, swap_sems, basis_send, basis_recv, col_send, col_recv):
    me, rep = lax.axis_index("grp"), lax.axis_index("rep")
    half = swap.shape[0]
    block = cols.shape[2]
    offsets = far_first(n)
    peers = {k: {"grp": lax.rem(me + k, n)} for k in offsets}
    own = pl.ds(pl.multiple_of(rep * half, half), half)
    other = pl.ds(pl.multiple_of((1 - rep) * half, half), half)
    load = pltpu.make_async_copy(grad.at[own], mine, load_sem)
    load.start()
    full[pl.ds(me, 1)] = basis[own][None]
    greet([{"rep": 1 - rep}] + [peers[k] for k in offsets])
    trade = peer_copy(grad.at[other], swap, swap_sems.at[0], swap_sems.at[1], {"rep": 1 - rep})
    trade.start()
    copies = []
    pass_on = spread(n, me, full, basis_send, basis_recv, copies)
    load.wait()
    trade.wait()
    for j in range(n):
        parts[j] = mine[:, j * block : (j + 1) * block] + swap[:, j * block : (j + 1) * block]
    pack_tails(parts, tails_out)
    keep_own(me, parts, cols, tails_out, tails_in)
    late = n // 4
    for at, k in enumerate(offsets):
        if at == late:
            pass_on()
        copies += send_block(me, k, peers[k], parts, cols, tails_out, tails_in, col_send, col_recv)
    for copy in copies:
        copy.wait()
    unpack_tails(tails_in, cols)


def reduce_and_return(
    n, terms, moved, rows, update, near, sums, far, tails_out, tails_in, near_send, near_recv, far_send, far_recv, row_send, row_recv, up_send, up_recv
):
    me = lax.axis_index("grp")
    depth, fan = groups(n)
    layer, spot, column, plane = peer_maps(n, me)
    offsets = far_first(n)
    peers = {k: {"grp": lax.rem(me + k, n)} for k in offsets}
    greet([peers[k] for k in offsets])
    late = []
    waiting = list(offsets)

    def send_update(count):
        for k in waiting[:count]:
            late.extend(send_block(me, k, peers[k], moved, update, tails_out, tails_in, up_send, up_recv))
        del waiting[:count]

    first = []
    for f in plane:
        source = terms.at[:, lax.rem(spot + f, fan)]
        first.append(peer_copy(source, near.at[f], near_send.at[f], near_recv.at[f], {"grp": plane[f]}))
        first[-1].start()
    pack_tails(moved, tails_out)
    send_update(n // 4)
    keep_own(me, moved, update, tails_out, tails_in)
    near[0] = terms[:, pl.ds(spot, 1)][:, 0]
    for copy in first:
        copy.wait()
    partial = near[0]
    for f in plane:
        partial = partial + near[f]
    sums[...] = partial
    second = []
    for d in column:
        source = sums.at[lax.rem(layer + d, depth)]
        second.append(peer_copy(source, far.at[d], far_send.at[d], far_recv.at[d], {"grp": column[d]}))
        second[-1].start()
    send_update(n // 8)
    far[0] = sums[pl.ds(layer, 1)][0]
    for copy in second:
        copy.wait()
    total = far[0]
    for d in column:
        total = total + far[d]
    rows[pl.ds(me, 1)] = total[None]
    pass_on = spread(n, me, rows, row_send, row_recv, late)
    send_update(n // 4)
    pass_on()
    send_update(n)
    for copy in late:
        copy.wait()
    unpack_tails(tails_in, update)


def in_vmem(count):
    return [pl.BlockSpec(memory_space=pltpu.VMEM)] * count


def call_scatter(n, grad, basis):
    rows, ncol = grad.shape
    half, block, rank = rows // 2, ncol // n, basis.shape[1]
    sems = pltpu.SemaphoreType.DMA((n,))
    return pl.pallas_call(
        lambda *refs: scatter_grad(n, *refs),
        out_shape=(
            jax.ShapeDtypeStruct((n, half, block), jnp.float32),
            jax.ShapeDtypeStruct((n, half, rank), jnp.float32),
        ),
        in_specs=[pl.BlockSpec(memory_space=pltpu.HBM)] + in_vmem(1),
        out_specs=tuple(in_vmem(2)),
        scratch_shapes=[
            pltpu.VMEM((half, ncol), jnp.float32),
            pltpu.VMEM((half, ncol), jnp.float32),
            pltpu.VMEM((n, half, block), jnp.float32),
            tails_of(n, half, block),
            tails_of(n, half, block),
            pltpu.SemaphoreType.DMA,
            pltpu.SemaphoreType.DMA((2,)),
            sems,
            sems,
            pltpu.SemaphoreType.DMA((2, n)),
            pltpu.SemaphoreType.DMA((2, n)),
        ],
        compiler_params=pltpu.CompilerParams(collective_id=0, has_side_effects=True, vmem_limit_bytes=GRANT),
        name="scatter_grad",
    )(grad, basis)


def call_return(n, terms, moved):
    half, rank = terms.shape[2:]
    depth, fan = groups(n)
    sems = pltpu.SemaphoreType.DMA((n,))
    return pl.pallas_call(
        lambda *refs: reduce_and_return(n, *refs),
        out_shape=(
            jax.ShapeDtypeStruct((n, half, rank), jnp.float32),
            jax.ShapeDtypeStruct(moved.shape, jnp.float32),
        ),
        in_specs=in_vmem(2),
        out_specs=tuple(in_vmem(2)),
        scratch_shapes=[
            pltpu.VMEM((fan, depth, half, rank), jnp.float32),
            pltpu.VMEM((depth, half, rank), jnp.float32),
            pltpu.VMEM((depth, half, rank), jnp.float32),
            tails_of(*moved.shape),
            tails_of(*moved.shape),
        ]
        + [sems] * 6
        + [pltpu.SemaphoreType.DMA((2, n))] * 2,
        compiler_params=pltpu.CompilerParams(collective_id=1, has_side_effects=True, vmem_limit_bytes=GRANT),
        name="reduce_and_return",
    )(terms, moved)


def split_body(
    grad_parts,
    gain_grad_parts,
    weights,
    basis,
    moment_first,
    moment_second,
    gains,
    gain_first,
    gain_second,
):
    corr_first = 1.0 - beta_first**10
    corr_second = 1.0 - beta_second**10
    n = lax.axis_size("grp")
    rep = lax.axis_index("rep")
    swap = [(0, 1), (1, 0)]
    local_grad = grad_parts[0]
    local_gain = gain_grad_parts[0]
    rows, ncol = local_grad.shape
    half = rows // 2
    block = ncol // n
    rank = basis.shape[1]

    def own_half(x):
        return lax.dynamic_slice_in_dim(x, rep * half, half, 0)

    def swapped(x):
        return lax.ppermute(x, "rep", swap)

    def joined(mine, other):
        return jnp.where(rep == 0, jnp.concatenate([mine, other], 0), jnp.concatenate([other, mine], 0))

    gain_grad = local_gain + swapped(local_gain)
    col_block, half_basis = call_scatter(n, local_grad, basis)
    col_block = col_block.reshape(n * half, block)
    half_basis = half_basis.reshape(n * half, rank)
    partial = exact_dot(col_block.T, half_basis)
    projected = partial + swapped(partial)
    new_first = beta_first * moment_first + (1.0 - beta_first) * projected
    new_second = beta_second * moment_second + (1.0 - beta_second) * projected * projected
    direction = new_first / corr_first / (jnp.sqrt(new_second / corr_second) + adam_eps)
    terms = exact_dot(col_block, projected).reshape(*groups(n), half, rank)
    update_cols = exact_dot(half_basis, direction.T).reshape(n, half, block)
    sub_all, update = call_return(n, terms, update_cols)
    sub_half = lax.dynamic_index_in_dim(sub_all, lax.axis_index("grp"), 0, keepdims=False)
    sub_all = sub_all.reshape(n * half, rank)
    update = jnp.swapaxes(update, 0, 1).reshape(half, ncol)
    gram_half = exact_dot(sub_all.T, sub_all)
    gram = gram_half + swapped(gram_half)
    subspace = joined(sub_half, swapped(sub_half))
    new_half = own_half(weights) - learn_rate * galore_scale * update
    new_weights = joined(new_half, swapped(new_half))
    scale = jnp.sqrt(jnp.sqrt(jnp.sum(gram * gram) + 1e-06))
    iterate = subspace / scale
    current = gram / scale / scale
    for step in range(NS_STEPS):
        iterate = 1.5 * iterate - 0.5 * exact_dot(iterate, current)
        if step + 1 < NS_STEPS:
            side = 1.5 * current - 0.5 * exact_dot(current, current)
            current = 1.5 * side - 0.5 * exact_dot(side, current)
    new_gain_first = beta_first * gain_first + (1.0 - beta_first) * gain_grad
    new_gain_second = beta_second * gain_second + (1.0 - beta_second) * gain_grad * gain_grad
    new_gains = gains - learn_rate * (new_gain_first / corr_first) / (
        jnp.sqrt(new_gain_second / corr_second) + adam_eps
    )
    return (new_weights, new_first, new_second, iterate, new_gains, new_gain_first, new_gain_second)


def halves(x):
    high = x.astype(jnp.bfloat16)
    return high, (x - high.astype(jnp.float32)).astype(jnp.bfloat16)


def three_dots(left, right, dims):
    left_high, left_low = halves(left)
    right_high, right_low = halves(right)

    def product(a, b):
        return lax.dot_general(a, b, (dims, ((), ())), preferred_element_type=jnp.float32)

    return product(left_high, right_high) + (product(left_high, right_low) + product(left_low, right_high))


def plain_dot(left, right):
    return three_dots(left, right, ((1,), (0,)))


def rows_dot(left, right):
    return three_dots(left, right, ((0,), (0,)))


def lanes_dot(left, right):
    return three_dots(left, right, ((1,), (1,)))


def exchange_tails(top, bottom):
    low = lax.broadcasted_iota(jnp.int32, top.shape, 1) < 64
    even = jnp.where(low, top, pltpu.roll(bottom, 64, 1))
    odd = jnp.where(low, pltpu.roll(top, 64, 1), bottom)
    return even, odd


def lane_tiles(ref, group, half, tiles):
    return jnp.concatenate(
        [ref[group, t * half : (t + 1) * half].reshape(-1, 128) for t in range(tiles)], axis=1
    )


def one_step(
    n,
    grad,
    gain_part,
    weights,
    basis,
    moment_first,
    moment_second,
    gains,
    gain_first,
    gain_second,
    new_weights,
    new_first,
    new_second,
    new_basis,
    new_gains,
    new_gain_first,
    new_gain_second,
    mine,
    swap,
    parts,
    cols,
    full,
    partial,
    other_partial,
    projected,
    direction,
    pair_proj,
    first_in,
    second_in,
    weights_in,
    basis_in,
    gain_in,
    gain_mine,
    gain_other,
    terms,
    near,
    sums,
    far,
    rows,
    other_rows,
    gram,
    other_gram,
    up_out,
    up_in,
    chunk_sem,
    trade_send,
    trade_recv,
    load_sem,
    gain_sems,
    basis_send,
    basis_recv,
    col_send,
    col_recv,
    part_send,
    part_recv,
    near_send,
    near_recv,
    far_send,
    far_recv,
    row_send,
    row_recv,
    swap_sems,
    pass_send,
    pass_recv,
    cross_send,
    cross_recv,
    up_send,
    up_recv,
    out_send,
    out_recv,
    store_sem,
):
    corr_first = 1.0 - beta_first**10
    corr_second = 1.0 - beta_second**10
    me, rep = lax.axis_index("grp"), lax.axis_index("rep")
    depth, fan = groups(n)
    layer, spot, column, plane = peer_maps(n, me)
    half, ncol = mine.shape
    wide = 2 * ncol // n
    block = ncol // n
    tiles = block // 128
    main = tiles * 128
    rest = block - main
    rank = basis.shape[1]
    upper, deep = layer // 2, lax.rem(layer, 2)
    line, side = spot // 2, lax.rem(spot, 2)
    partner = {"rep": 1 - rep}
    own = pl.ds(pl.multiple_of(rep * half, half), half)
    other = pl.ds(pl.multiple_of((1 - rep) * half, half), half)
    layers = [2 * (1 - upper) + deep, 2 * (1 - upper) + 1 - deep, 2 * upper + 1 - deep, layer]
    order = [(z, y) for z in layers for y in (line, 1 - line)]
    order[-2:] = order[-2:][::-1]
    spans = [pl.ds(pl.multiple_of((z * 2 + y) * wide, 128), wide) for z, y in order]

    loads = [
        pltpu.make_async_copy(grad.at[own, span], mine.at[:, span], chunk_sem.at[i]) for i, span in enumerate(spans)
    ]
    for load in loads:
        load.start()
    basis_load = pltpu.make_async_copy(basis, basis_in, load_sem.at[0])
    basis_load.start()
    small = [
        pltpu.make_async_copy(gain_part.at[0], gain_mine, load_sem.at[1]),
        pltpu.make_async_copy(gains, gain_in.at[0], load_sem.at[2]),
        pltpu.make_async_copy(gain_first, gain_in.at[1], load_sem.at[3]),
        pltpu.make_async_copy(gain_second, gain_in.at[2], load_sem.at[4]),
        pltpu.make_async_copy(moment_first, first_in, load_sem.at[5]),
        pltpu.make_async_copy(moment_second, second_in, load_sem.at[6]),
        pltpu.make_async_copy(weights.at[own], weights_in, load_sem.at[7]),
    ]
    greet([partner] + [{"grp": lax.rem(me + k, n)} for k in far_first(n)])
    late = []
    trades = [
        peer_copy(grad.at[other, span], swap.at[:, span], trade_send.at[i], trade_recv.at[i], partner)
        for i, span in enumerate(spans)
    ]
    for trade in trades[:4]:
        trade.start()
    basis_load.wait()
    full[pl.ds(me, 1)] = basis_in[own][None]
    pass_basis = spread(n, me, full, basis_send, basis_recv, late)
    for load in small:
        load.start()

    for i, (z, y) in enumerate(order):
        loads[i].wait()
        trades[i].wait()
        if i == 0:
            for trade in trades[4:]:
                trade.start()
        span = spans[i]
        total = mine[:, span] + swap[:, span]
        base = (z * 2 + y) * 2
        even_tail, odd_tail = exchange_tails(total[: half // 2, main : main + 128], total[half // 2 :, main : main + 128])
        packed = [
            [total[:, 128 * t : 128 * (t + 1)] for t in range(tiles)] + [even_tail],
            [total[:, main + 128 * (t + 1) : main + 128 * (t + 2)] for t in range(tiles)] + [odd_tail],
        ]
        last = i + 1 == len(order)
        for x in range(2):
            at = 0
            for piece in packed[x]:
                parts[base + x, at : at + piece.shape[0]] = piece
                at += piece.shape[0]
        for x in [1 - side] if last else [side, 1 - side]:
            copy = peer_copy(
                parts.at[base + x], cols.at[me], col_send.at[base + x], col_recv.at[me], {"grp": base + x}
            )
            copy.start()
        if i == 1:
            pass_basis()
    cols[pl.ds(me, 1)] = parts[pl.ds(me, 1)]
    for copy in late:
        copy.wait()
    late = []
    gain_trade = peer_copy(gain_mine, gain_other, gain_sems.at[0], gain_sems.at[1], partner)
    small[0].wait()
    gain_trade.start()

    def landed(buffer, send, recv, source):
        return peer_copy(buffer.at[source], buffer.at[source], send.at[source], recv.at[source], {"grp": source})

    near_group = pl.ds(pl.multiple_of(upper * (n // 2), n // 2), n // 2)
    far_group = pl.ds(pl.multiple_of((1 - upper) * (n // 2), n // 2), n // 2)
    near_sources = [2 * (2 * z + y) + x for z, y in order[4:] for x in (side, 1 - side)]
    far_sources = [2 * (2 * z + y) + x for z, y in order[:4] for x in (side, 1 - side)]
    del near_sources[-2]

    def products(group):
        depths = full[group].reshape(-1, rank)
        tops = full[group, : half // 2].reshape(-1, rank)
        bottoms = full[group, half // 2 :].reshape(-1, rank)
        left = lane_tiles(cols, group, half, tiles)
        tail = cols[group, tiles * half :].reshape(-1, 128)
        yield rows_dot(left[:, : main // 2], depths)
        yield rows_dot(left[:, main // 2 :], depths)
        yield rows_dot(tail, tops)[:rest] + rows_dot(tail, bottoms)[rest:]

    pieces = [pl.ds(0, main // 2), pl.ds(main // 2, main // 2), pl.ds(main, rest)]
    for source in near_sources:
        landed(cols, col_send, col_recv, source).wait_recv()
    for piece, product in zip(pieces, products(near_group)):
        partial[piece] = product
    for source in far_sources:
        landed(cols, col_send, col_recv, source).wait_recv()
    joins = []
    for i, (piece, product) in enumerate(zip(pieces, products(far_group))):
        partial[piece] += product
        joins.append(peer_copy(partial.at[piece], other_partial.at[piece], part_send.at[i], part_recv.at[i], partner))
        joins[-1].start()
    small[4].wait()
    small[5].wait()
    natural = [
        pl.ds(pl.multiple_of(side * rest, rest), main // 2),
        pl.ds(pl.multiple_of(side * rest + main // 2, rest), main // 2),
        pl.ds(pl.multiple_of((1 - side) * main, rest), rest),
    ]
    for piece, place, join in zip(pieces, natural, joins):
        join.wait()
        proj = partial[piece] + other_partial[piece]
        projected[piece] = proj
        first = beta_first * first_in[place] + (1.0 - beta_first) * proj
        second = beta_second * second_in[place] + (1.0 - beta_second) * proj * proj
        first_in[place] = first
        second_in[place] = second
        direction[layer, piece] = first / corr_first / (jnp.sqrt(second / corr_second) + adam_eps)
    stores = []

    def store(source, target):
        stores.append(pltpu.make_async_copy(source, target, store_sem.at[len(stores)]))
        stores[-1].start()

    part = block // 4
    ranges = [pl.ds(pl.multiple_of(rep * (block // 2) + c * part, 8), part) for c in range(2)]
    inner = jnp.logical_and(layer > 0, layer < depth - 1)
    low = layer < 2
    mirrored = jnp.where(low, layer, depth - 1 - layer)
    origins = [jnp.where(low, k, depth - 1 - k) for k in (1 - mirrored, 2, 3)]

    def pass_copy(origin, c, toward, at):
        chip = jnp.clip(layer + toward, 0, depth - 1) * fan + spot
        held = direction.at[origin, ranges[c]]
        return peer_copy(held, held, pass_send.at[at, c], pass_recv.at[origin, c], {"grp": chip})

    def own_pass(act):
        for c in range(2):

            @pl.when(layer < depth - 1)
            def _():
                act(pass_copy(layer, c, 1, 0))

            @pl.when(layer > 0)
            def _():
                act(pass_copy(layer, c, -1, 1))

    own_pass(lambda copy: copy.start())

    def cross_copy(k, c):
        held = direction.at[origins[k], ranges[c]]
        return peer_copy(held, held, cross_send.at[k, c], cross_recv.at[k, c], partner)

    def forward(k, c):
        return pass_copy(origins[k], c, jnp.where(origins[k] < layer, 1, -1), 2 + k)

    def take_pass(k):
        for c in range(2):
            forward(k, c).wait_recv()

            @pl.when(inner)
            def _():
                forward(k, c).start()

            cross_copy(k, c).start()

    def take_pass_if(chosen, k):
        @pl.when(chosen)
        def _():
            take_pass(k)

    blank = jnp.zeros((rest, rank), jnp.float32)

    def paired(tail):
        return jnp.concatenate(
            [jnp.concatenate([tail, blank], axis=1), jnp.concatenate([blank, tail], axis=1)], axis=0
        )

    pair_proj[...] = paired(projected[main:])

    whole = plain_dot(lane_tiles(cols, pl.ds(0, n), half, tiles), projected[:main]).reshape(n, half, rank)
    tail = plain_dot(cols[:, tiles * half :].reshape(-1, 128), pair_proj[...])
    terms[:, : half // 2] = whole[:, : half // 2] + tail[:, :rank].reshape(n, half // 2, rank)
    terms[:, half // 2 :] = whole[:, half // 2 :] + tail[:, rank:].reshape(n, half // 2, rank)

    first_hop = []
    for f in plane:
        for d in range(depth):
            source = d * fan + lax.rem(spot + f, fan)
            first_hop.append(
                peer_copy(
                    terms.at[source],
                    near.at[f * depth + d],
                    near_send.at[f * depth + d],
                    near_recv.at[f * depth + d],
                    {"grp": plane[f]},
                )
            )
            first_hop[-1].start()

    beside = pl.ds(pl.multiple_of(layer * fan, fan), fan)

    def make_update(origin):
        group = pl.ds(pl.multiple_of(origin * fan, fan), fan)
        depths = full[beside].reshape(-1, rank)
        sides = jnp.concatenate(
            [full[beside, : half // 2].reshape(-1, rank), full[beside, half // 2 :].reshape(-1, rank)], axis=1
        )
        wide_part = lanes_dot(depths, direction[origin, :main])
        for t in range(tiles):
            up_out[group, t * half : (t + 1) * half] = wide_part[:, 128 * t : 128 * (t + 1)].reshape(fan, half, 128)
        up_out[group, tiles * half :] = lanes_dot(sides, paired(direction[origin, main:])).reshape(fan, half // 2, 128)

    def send_update(origin):
        for f in plane:
            at = origin * fan + lax.rem(spot + f, fan)
            peer_copy(
                up_out.at[at],
                up_in.at[origin * fan + spot],
                up_send.at[at],
                up_recv.at[origin * fan + spot],
                {"grp": plane[f]},
            ).start()
        up_in[pl.ds(origin * fan + spot, 1)] = up_out[pl.ds(origin * fan + spot, 1)]

    def take_update(k):
        for c in range(2):
            cross_copy(k, c).wait_recv()
        make_update(origins[k])
        send_update(origins[k])

    rate = learn_rate * galore_scale
    returns = []

    def take_weights(k):
        z = ([layer] + origins)[k]
        for j, y in enumerate((line, 1 - line)):
            base = (z * 2 + y) * 2
            for x in [1 - side] if j == 0 else [side, 1 - side]:
                landed(up_in, up_send, up_recv, base + x).wait_recv()
            start = pl.multiple_of((z * 2 + y) * wide, 128)
            top, bottom = exchange_tails(up_in[base, tiles * half :], up_in[base + 1, tiles * half :])
            for t in range(2 * tiles + 1):
                lanes = pl.ds(pl.multiple_of(start + 128 * t, 128), 128)
                if t < tiles:
                    change = up_in[base, t * half : (t + 1) * half]
                elif t == tiles:
                    change = jnp.concatenate([top, bottom], axis=0)
                else:
                    change = up_in[base + 1, (t - tiles - 1) * half : (t - tiles) * half]
                weights_in[:, lanes] = weights_in[:, lanes] - rate * change
            ready = weights_in.at[:, pl.ds(start, wide)]
            target = new_weights.at[own, pl.ds(start, wide)]
            i = len(returns)
            returns.append(peer_copy(ready, target, out_send.at[i], out_recv.at[i], partner))
            returns[-1].start()
            store(ready, target)

    store(first_in, new_first)
    store(second_in, new_second)
    make_update(layer)
    for copy in first_hop:
        copy.wait()
    for d in range(depth):
        total = terms[d * fan + spot]
        for f in plane:
            total = total + near[f * depth + d]
        sums[d] = total
    second_hop = []
    for d in column:
        source = sums.at[lax.rem(layer + d, depth)]
        second_hop.append(peer_copy(source, far.at[d], far_send.at[d], far_recv.at[d], {"grp": column[d]}))
        second_hop[-1].start()
    send_update(layer)
    take_pass(0)
    take_pass_if(inner, 1)
    for copy in second_hop:
        copy.wait()
    total = sums[layer]
    for d in column:
        total = total + far[d]
    rows[pl.ds(me, 1)] = total[None]
    pass_rows = spread(n, me, rows, row_send, row_recv, late)
    row_trade = peer_copy(rows.at[me], other_rows, swap_sems.at[0], swap_sems.at[1], partner)
    row_trade.start()
    take_update(0)

    for load in small[1:4]:
        load.wait()
    gain_trade.wait()
    gain_grad = gain_mine[...] + gain_other[...]
    gain_one = beta_first * gain_in[1] + (1.0 - beta_first) * gain_grad
    gain_two = beta_second * gain_in[2] + (1.0 - beta_second) * gain_grad * gain_grad
    gain_in[0] = gain_in[0] - learn_rate * (gain_one / corr_first) / (jnp.sqrt(gain_two / corr_second) + adam_eps)
    gain_in[1] = gain_one
    gain_in[2] = gain_two
    store(gain_in.at[0], new_gains)
    store(gain_in.at[1], new_gain_first)
    store(gain_in.at[2], new_gain_second)

    take_pass_if(inner, 2)
    pass_rows()
    take_pass_if(jnp.logical_not(inner), 1)
    take_update(1)
    small[6].wait()
    take_weights(0)
    for copy in late:
        copy.wait()
    everything = rows[...].reshape(-1, rank)
    gram[...] = rows_dot(everything, everything)
    gram_trade = peer_copy(gram, other_gram, swap_sems.at[2], swap_sems.at[3], partner)
    gram_trade.start()
    take_pass_if(jnp.logical_not(inner), 2)
    take_weights(1)
    row_trade.wait()
    gram_trade.wait()
    take_update(2)
    take_weights(2)
    current = gram[...] + other_gram[...]
    scale = jnp.sqrt(jnp.sqrt(jnp.sum(current * current, keepdims=True) + 1e-06))
    current = current / scale / scale
    first_rows = rows[me]
    second_rows = other_rows[...]
    upper_rows = jnp.where(rep == 0, first_rows, second_rows)
    lower_rows = jnp.where(rep == 0, second_rows, first_rows)
    iterate = jnp.concatenate([upper_rows, lower_rows], axis=0) / scale
    for step in range(NS_STEPS):
        iterate = 1.5 * iterate - 0.5 * plain_dot(iterate, current)
        if step + 1 < NS_STEPS:
            factor = 1.5 * current - 0.5 * plain_dot(current, current)
            current = 1.5 * factor - 0.5 * plain_dot(factor, current)
    basis_in[...] = iterate
    store(basis_in, new_basis)

    take_weights(3)
    for source in far_sources + near_sources:
        landed(parts, col_send, col_recv, source).wait_send()
    for origin in [layer] + origins:
        for f in plane:
            landed(up_out, up_send, up_recv, origin * fan + lax.rem(spot + f, fan)).wait_send()
    own_pass(lambda copy: copy.wait_send())
    for k in range(3):
        for c in range(2):
            cross_copy(k, c).wait_send()

            @pl.when(inner)
            def _():
                forward(k, c).wait_send()

    for copy in returns + stores:
        copy.wait()


def call_step(n, *arrays):
    grad, gain_part, weights, basis, moment_first, moment_second, gains, gain_first, gain_second = arrays
    rows, ncol = grad.shape
    half, block, rank = rows // 2, ncol // n, basis.shape[1]
    depth, fan = groups(n)
    message = half * block // 128
    pairs = n // 2

    def held(*shape):
        return pltpu.VMEM(shape, jnp.float32)

    def sems(*shape):
        return pltpu.SemaphoreType.DMA(shape)

    return pl.pallas_call(
        lambda *refs: one_step(n, *refs),
        out_shape=tuple(
            jax.ShapeDtypeStruct(x.shape, jnp.float32)
            for x in (weights, moment_first, moment_second, basis, gains, gain_first, gain_second)
        ),
        in_specs=[pl.BlockSpec(memory_space=pltpu.HBM)] * 9,
        out_specs=tuple([pl.BlockSpec(memory_space=pltpu.HBM)] * 7),
        scratch_shapes=[
            held(half, ncol),
            held(half, ncol),
            held(n, message, 128),
            held(n, message, 128),
            held(n, half, rank),
            held(block, rank),
            held(block, rank),
            held(block, rank),
            held(depth, block, rank),
            held(128, 2 * rank),
            held(block, rank),
            held(block, rank),
            held(half, ncol),
            held(rows, rank),
            held(3, 2, rows),
            held(2, rows),
            held(2, rows),
            held(n, half, rank),
            held(n, half, rank),
            held(depth, half, rank),
            held(depth, half, rank),
            held(n, half, rank),
            held(half, rank),
            held(rank, rank),
            held(rank, rank),
            held(n, message, 128),
            held(n, message, 128),
            sems(pairs),
            sems(pairs),
            sems(pairs),
            sems(8),
            sems(2),
            sems(n),
            sems(n),
            sems(n),
            sems(n),
            sems(3),
            sems(3),
            sems(n),
            sems(n),
            sems(n),
            sems(n),
            sems(n),
            sems(n),
            sems(4),
            sems(5, 2),
            sems(depth, 2),
            sems(3, 2),
            sems(3, 2),
            sems(n),
            sems(n),
            sems(pairs),
            sems(pairs),
            sems(pairs + 6),
        ],
        compiler_params=pltpu.CompilerParams(collective_id=2, has_side_effects=True, vmem_limit_bytes=WIDE_GRANT),
        name="one_step",
    )(*arrays)


def pieces_of(shape):
    count = 1
    while shape[0] % (16 * count) == 0 and shape[0] * shape[1] // count > 1 << 17:
        count *= 2
    size = shape[0] // count
    return [pl.ds(i * size, size) for i in range(count)]


def place(count, *refs):
    sources, targets, held, sems = refs[:count], refs[count : 2 * count], refs[2 * count : 3 * count], refs[-1]
    loads, stores = [], []
    for source, target, buffer in zip(sources, targets, held):
        for piece in pieces_of(source.shape):
            at = len(loads)
            loads.append(pltpu.make_async_copy(source.at[piece], buffer.at[piece], sems.at[0, at]))
            stores.append(pltpu.make_async_copy(buffer.at[piece], target.at[piece], sems.at[1, at]))
            loads[-1].start()
    for load, store in zip(loads, stores):
        load.wait()
        store.start()
    for store in stores:
        store.wait()


def call_place(arrays):
    count = len(arrays)
    space = [pl.BlockSpec(memory_space=pltpu.HBM)] * count
    return pl.pallas_call(
        lambda *refs: place(count, *refs),
        out_shape=tuple(jax.ShapeDtypeStruct(x.shape, x.dtype) for x in arrays),
        in_specs=space,
        out_specs=tuple(space),
        scratch_shapes=[pltpu.VMEM(x.shape, x.dtype) for x in arrays]
        + [pltpu.SemaphoreType.DMA((2, sum(len(pieces_of(x.shape)) for x in arrays)))],
        compiler_params=pltpu.CompilerParams(vmem_limit_bytes=WIDE_GRANT),
        name="place",
    )(*arrays)


def body(grad_parts, *rest):
    n = lax.axis_size("grp")
    rows, ncol = grad_parts.shape[1:]
    half, block = rows // 2, ncol // n
    if n == 16 and half == 32 and block % 128 == 64:
        return call_place(call_step(n, grad_parts[0], *rest))
    return split_body(grad_parts, *rest)


def solution(mesh):
    in_specs = (
        P("rep", "grp", None),
        P("rep", None, "grp"),
        P("grp", None),
        P("grp", None),
        P("grp", None),
        P("grp", None),
        P(None, "grp"),
        P(None, "grp"),
        P(None, "grp"),
    )
    out_specs = (
        P("grp", None),
        P("grp", None),
        P("grp", None),
        P("grp", None),
        P(None, "grp"),
        P(None, "grp"),
        P(None, "grp"),
    )
    return jax.shard_map(body, mesh=mesh, in_specs=in_specs, out_specs=out_specs, check_vma=False)
```

```python
import jax
import jax.numpy as jnp
from jax import lax
from jax.experimental import pallas as pl
from jax.experimental.pallas import tpu as pltpu
from jax.sharding import PartitionSpec as P

NS_STEPS = 3
GRANT = 24 << 20
WIDE_GRANT = 60 << 20


beta_first = 0.9
beta_second = 0.999
learn_rate = 0.1
galore_scale = 0.25
adam_eps = 1e-08


def exact_dot(left, right):
    return jnp.dot(left, right, precision=lax.Precision.HIGHEST, preferred_element_type=jnp.float32)


def far_first(n):
    return sorted(range(1, n), key=lambda k: abs(k - n // 2))


def peer_copy(src, dst, send_sem, recv_sem, where):
    return pltpu.make_async_remote_copy(
        src_ref=src,
        dst_ref=dst,
        send_sem=send_sem,
        recv_sem=recv_sem,
        device_id=where,
        device_id_type=pl.DeviceIdType.MESH,
    )


def greet(others):
    barrier = pltpu.get_barrier_semaphore()
    for other in others:
        pl.semaphore_signal(barrier, inc=1, device_id=other, device_id_type=pl.DeviceIdType.MESH)
    pl.semaphore_wait(barrier, len(others))


def groups(n):
    fan = 4 if n % 4 == 0 else 1
    return n // fan, fan


def peer_maps(n, me):
    depth, fan = groups(n)
    layer, spot = me // fan, lax.rem(me, fan)
    column = {d: lax.rem(layer + d, depth) * fan + spot for d in range(1, depth)}
    plane = {f: layer * fan + lax.rem(spot + f, fan) for f in range(1, fan)}
    return layer, spot, column, plane


def spread(n, me, ref, send, recv, sent):
    depth, fan = groups(n)
    layer, spot, column, plane = peer_maps(n, me)
    down = []
    for d in sorted(column, key=lambda d: abs(d - depth // 2)):
        down.append((d, peer_copy(ref.at[me], ref.at[me], send.at[d * fan], recv.at[d * fan], {"grp": column[d]})))
        down[-1][1].start()
    for f in plane:
        sent.append(peer_copy(ref.at[me], ref.at[me], send.at[f], recv.at[f], {"grp": plane[f]}))
        sent[-1].start()

    def pass_on():
        for d, copy in down:
            copy.wait()
            slot = lax.rem(layer - d + depth, depth) * fan + spot
            for f in plane:
                at = d * fan + f
                sent.append(peer_copy(ref.at[slot], ref.at[slot], send.at[at], recv.at[at], {"grp": plane[f]}))
                sent[-1].start()

    return pass_on


def split_of(half, block):
    rest = block % 128
    return (block - rest, rest) if 2 * rest == 128 and half % 16 == 0 else (block, 0)


def tails_of(n, half, block):
    rest = split_of(half, block)[1]
    return pltpu.VMEM((n, half // 2, 128) if rest else (1, 8, 128), jnp.float32)


def pack_tails(ref, tails):
    half = ref.shape[1]
    main, rest = split_of(half, ref.shape[2])
    if rest:
        tails[:, :, :rest] = ref[:, : half // 2, main:]
        tails[:, :, rest:] = ref[:, half // 2 :, main:]


def unpack_tails(tails, ref):
    half = ref.shape[1]
    main, rest = split_of(half, ref.shape[2])
    if rest:
        ref[:, : half // 2, main:] = tails[:, :, :rest]
        ref[:, half // 2 :, main:] = tails[:, :, rest:]


def keep_own(me, source, target, tails_out, tails_in):
    target[pl.ds(me, 1)] = source[pl.ds(me, 1)]
    if split_of(*source.shape[1:])[1]:
        tails_in[pl.ds(me, 1)] = tails_out[pl.ds(me, 1)]


def send_block(me, k, where, source, target, tails_out, tails_in, send, recv):
    main, rest = split_of(*source.shape[1:])
    peer = where["grp"]
    copies = [peer_copy(source.at[peer, :, :main], target.at[me, :, :main], send.at[0, k], recv.at[0, k], where)]
    if rest:
        copies.append(peer_copy(tails_out.at[peer], tails_in.at[me], send.at[1, k], recv.at[1, k], where))
    for copy in copies:
        copy.start()
    return copies


def scatter_grad(n, grad, basis, cols, full, mine, swap, parts, tails_out, tails_in, load_sem, swap_sems, basis_send, basis_recv, col_send, col_recv):
    me, rep = lax.axis_index("grp"), lax.axis_index("rep")
    half = swap.shape[0]
    block = cols.shape[2]
    offsets = far_first(n)
    peers = {k: {"grp": lax.rem(me + k, n)} for k in offsets}
    own = pl.ds(pl.multiple_of(rep * half, half), half)
    other = pl.ds(pl.multiple_of((1 - rep) * half, half), half)
    load = pltpu.make_async_copy(grad.at[own], mine, load_sem)
    load.start()
    full[pl.ds(me, 1)] = basis[own][None]
    greet([{"rep": 1 - rep}] + [peers[k] for k in offsets])
    trade = peer_copy(grad.at[other], swap, swap_sems.at[0], swap_sems.at[1], {"rep": 1 - rep})
    trade.start()
    copies = []
    pass_on = spread(n, me, full, basis_send, basis_recv, copies)
    load.wait()
    trade.wait()
    for j in range(n):
        parts[j] = mine[:, j * block : (j + 1) * block] + swap[:, j * block : (j + 1) * block]
    pack_tails(parts, tails_out)
    keep_own(me, parts, cols, tails_out, tails_in)
    late = n // 4
    for at, k in enumerate(offsets):
        if at == late:
            pass_on()
        copies += send_block(me, k, peers[k], parts, cols, tails_out, tails_in, col_send, col_recv)
    for copy in copies:
        copy.wait()
    unpack_tails(tails_in, cols)


def reduce_and_return(
    n, terms, moved, rows, update, near, sums, far, tails_out, tails_in, near_send, near_recv, far_send, far_recv, row_send, row_recv, up_send, up_recv
):
    me = lax.axis_index("grp")
    depth, fan = groups(n)
    layer, spot, column, plane = peer_maps(n, me)
    offsets = far_first(n)
    peers = {k: {"grp": lax.rem(me + k, n)} for k in offsets}
    greet([peers[k] for k in offsets])
    late = []
    waiting = list(offsets)

    def send_update(count):
        for k in waiting[:count]:
            late.extend(send_block(me, k, peers[k], moved, update, tails_out, tails_in, up_send, up_recv))
        del waiting[:count]

    first = []
    for f in plane:
        source = terms.at[:, lax.rem(spot + f, fan)]
        first.append(peer_copy(source, near.at[f], near_send.at[f], near_recv.at[f], {"grp": plane[f]}))
        first[-1].start()
    pack_tails(moved, tails_out)
    send_update(n // 4)
    keep_own(me, moved, update, tails_out, tails_in)
    near[0] = terms[:, pl.ds(spot, 1)][:, 0]
    for copy in first:
        copy.wait()
    partial = near[0]
    for f in plane:
        partial = partial + near[f]
    sums[...] = partial
    second = []
    for d in column:
        source = sums.at[lax.rem(layer + d, depth)]
        second.append(peer_copy(source, far.at[d], far_send.at[d], far_recv.at[d], {"grp": column[d]}))
        second[-1].start()
    send_update(n // 8)
    far[0] = sums[pl.ds(layer, 1)][0]
    for copy in second:
        copy.wait()
    total = far[0]
    for d in column:
        total = total + far[d]
    rows[pl.ds(me, 1)] = total[None]
    pass_on = spread(n, me, rows, row_send, row_recv, late)
    send_update(n // 4)
    pass_on()
    send_update(n)
    for copy in late:
        copy.wait()
    unpack_tails(tails_in, update)


def in_vmem(count):
    return [pl.BlockSpec(memory_space=pltpu.VMEM)] * count


def call_scatter(n, grad, basis):
    rows, ncol = grad.shape
    half, block, rank = rows // 2, ncol // n, basis.shape[1]
    sems = pltpu.SemaphoreType.DMA((n,))
    return pl.pallas_call(
        lambda *refs: scatter_grad(n, *refs),
        out_shape=(
            jax.ShapeDtypeStruct((n, half, block), jnp.float32),
            jax.ShapeDtypeStruct((n, half, rank), jnp.float32),
        ),
        in_specs=[pl.BlockSpec(memory_space=pltpu.HBM)] + in_vmem(1),
        out_specs=tuple(in_vmem(2)),
        scratch_shapes=[
            pltpu.VMEM((half, ncol), jnp.float32),
            pltpu.VMEM((half, ncol), jnp.float32),
            pltpu.VMEM((n, half, block), jnp.float32),
            tails_of(n, half, block),
            tails_of(n, half, block),
            pltpu.SemaphoreType.DMA,
            pltpu.SemaphoreType.DMA((2,)),
            sems,
            sems,
            pltpu.SemaphoreType.DMA((2, n)),
            pltpu.SemaphoreType.DMA((2, n)),
        ],
        compiler_params=pltpu.CompilerParams(collective_id=0, has_side_effects=True, vmem_limit_bytes=GRANT),
        name="scatter_grad",
    )(grad, basis)


def call_return(n, terms, moved):
    half, rank = terms.shape[2:]
    depth, fan = groups(n)
    sems = pltpu.SemaphoreType.DMA((n,))
    return pl.pallas_call(
        lambda *refs: reduce_and_return(n, *refs),
        out_shape=(
            jax.ShapeDtypeStruct((n, half, rank), jnp.float32),
            jax.ShapeDtypeStruct(moved.shape, jnp.float32),
        ),
        in_specs=in_vmem(2),
        out_specs=tuple(in_vmem(2)),
        scratch_shapes=[
            pltpu.VMEM((fan, depth, half, rank), jnp.float32),
            pltpu.VMEM((depth, half, rank), jnp.float32),
            pltpu.VMEM((depth, half, rank), jnp.float32),
            tails_of(*moved.shape),
            tails_of(*moved.shape),
        ]
        + [sems] * 6
        + [pltpu.SemaphoreType.DMA((2, n))] * 2,
        compiler_params=pltpu.CompilerParams(collective_id=1, has_side_effects=True, vmem_limit_bytes=GRANT),
        name="reduce_and_return",
    )(terms, moved)


def split_body(
    grad_parts,
    gain_grad_parts,
    weights,
    basis,
    moment_first,
    moment_second,
    gains,
    gain_first,
    gain_second,
):
    corr_first = 1.0 - beta_first**10
    corr_second = 1.0 - beta_second**10
    n = lax.axis_size("grp")
    rep = lax.axis_index("rep")
    swap = [(0, 1), (1, 0)]
    local_grad = grad_parts[0]
    local_gain = gain_grad_parts[0]
    rows, ncol = local_grad.shape
    half = rows // 2
    block = ncol // n
    rank = basis.shape[1]

    def own_half(x):
        return lax.dynamic_slice_in_dim(x, rep * half, half, 0)

    def swapped(x):
        return lax.ppermute(x, "rep", swap)

    def joined(mine, other):
        return jnp.where(rep == 0, jnp.concatenate([mine, other], 0), jnp.concatenate([other, mine], 0))

    gain_grad = local_gain + swapped(local_gain)
    col_block, half_basis = call_scatter(n, local_grad, basis)
    col_block = col_block.reshape(n * half, block)
    half_basis = half_basis.reshape(n * half, rank)
    partial = exact_dot(col_block.T, half_basis)
    projected = partial + swapped(partial)
    new_first = beta_first * moment_first + (1.0 - beta_first) * projected
    new_second = beta_second * moment_second + (1.0 - beta_second) * projected * projected
    direction = new_first / corr_first / (jnp.sqrt(new_second / corr_second) + adam_eps)
    terms = exact_dot(col_block, projected).reshape(*groups(n), half, rank)
    update_cols = exact_dot(half_basis, direction.T).reshape(n, half, block)
    sub_all, update = call_return(n, terms, update_cols)
    sub_half = lax.dynamic_index_in_dim(sub_all, lax.axis_index("grp"), 0, keepdims=False)
    sub_all = sub_all.reshape(n * half, rank)
    update = jnp.swapaxes(update, 0, 1).reshape(half, ncol)
    gram_half = exact_dot(sub_all.T, sub_all)
    gram = gram_half + swapped(gram_half)
    subspace = joined(sub_half, swapped(sub_half))
    new_half = own_half(weights) - learn_rate * galore_scale * update
    new_weights = joined(new_half, swapped(new_half))
    scale = jnp.sqrt(jnp.sqrt(jnp.sum(gram * gram) + 1e-06))
    iterate = subspace / scale
    current = gram / scale / scale
    for step in range(NS_STEPS):
        iterate = 1.5 * iterate - 0.5 * exact_dot(iterate, current)
        if step + 1 < NS_STEPS:
            side = 1.5 * current - 0.5 * exact_dot(current, current)
            current = 1.5 * side - 0.5 * exact_dot(side, current)
    new_gain_first = beta_first * gain_first + (1.0 - beta_first) * gain_grad
    new_gain_second = beta_second * gain_second + (1.0 - beta_second) * gain_grad * gain_grad
    new_gains = gains - learn_rate * (new_gain_first / corr_first) / (
        jnp.sqrt(new_gain_second / corr_second) + adam_eps
    )
    return (new_weights, new_first, new_second, iterate, new_gains, new_gain_first, new_gain_second)


def halves(x):
    high = x.astype(jnp.bfloat16)
    return high, (x - high.astype(jnp.float32)).astype(jnp.bfloat16)


def three_dots(left, right, dims):
    left_high, left_low = halves(left)
    right_high, right_low = halves(right)

    return lax.dot_general(
        jnp.concatenate([left_high, left_high, left_low], axis=dims[0][0]),
        jnp.concatenate([right_high, right_low, right_high], axis=dims[1][0]),
        (dims, ((), ())),
        preferred_element_type=jnp.float32,
    )


def plain_dot(left, right):
    return three_dots(left, right, ((1,), (0,)))


def rows_dot(left, right):
    return three_dots(left, right, ((0,), (0,)))


def lanes_dot(left, right):
    return three_dots(left, right, ((1,), (1,)))


def exchange_tails(top, bottom):
    low = lax.broadcasted_iota(jnp.int32, top.shape, 1) < 64
    even = jnp.where(low, top, pltpu.roll(bottom, 64, 1))
    odd = jnp.where(low, pltpu.roll(top, 64, 1), bottom)
    return even, odd


def lane_tiles(ref, group, half, tiles):
    return jnp.concatenate(
        [ref[group, t * half : (t + 1) * half].reshape(-1, 128) for t in range(tiles)], axis=1
    )


def one_step(
    n,
    grad,
    gain_part,
    weights,
    basis,
    moment_first,
    moment_second,
    gains,
    gain_first,
    gain_second,
    new_weights,
    new_first,
    new_second,
    new_basis,
    new_gains,
    new_gain_first,
    new_gain_second,
    mine,
    swap,
    parts,
    cols,
    full,
    partial,
    other_partial,
    projected,
    direction,
    pair_proj,
    first_in,
    second_in,
    weights_in,
    basis_in,
    gain_in,
    gain_mine,
    gain_other,
    terms,
    near,
    sums,
    far,
    rows,
    other_rows,
    gram,
    other_gram,
    up_out,
    up_in,
    chunk_sem,
    trade_send,
    trade_recv,
    load_sem,
    gain_sems,
    basis_send,
    basis_recv,
    col_send,
    col_recv,
    part_send,
    part_recv,
    near_send,
    near_recv,
    far_send,
    far_recv,
    row_send,
    row_recv,
    swap_sems,
    pass_send,
    pass_recv,
    cross_send,
    cross_recv,
    up_send,
    up_recv,
    out_send,
    out_recv,
    store_sem,
):
    corr_first = 1.0 - beta_first**10
    corr_second = 1.0 - beta_second**10
    me, rep = lax.axis_index("grp"), lax.axis_index("rep")
    depth, fan = groups(n)
    layer, spot, column, plane = peer_maps(n, me)
    half, ncol = mine.shape
    wide = 2 * ncol // n
    block = ncol // n
    tiles = block // 128
    main = tiles * 128
    rest = block - main
    rank = basis.shape[1]
    upper, deep = layer // 2, lax.rem(layer, 2)
    line, side = spot // 2, lax.rem(spot, 2)
    partner = {"rep": 1 - rep}
    own = pl.ds(pl.multiple_of(rep * half, half), half)
    other = pl.ds(pl.multiple_of((1 - rep) * half, half), half)
    layers = [2 * (1 - upper) + deep, 2 * (1 - upper) + 1 - deep, 2 * upper + 1 - deep, layer]
    order = [(z, y) for z in layers for y in (line, 1 - line)]
    order[-2:] = order[-2:][::-1]
    spans = [pl.ds(pl.multiple_of((z * 2 + y) * wide, 128), wide) for z, y in order]

    loads = [
        pltpu.make_async_copy(grad.at[own, span], mine.at[:, span], chunk_sem.at[i]) for i, span in enumerate(spans)
    ]
    for load in loads:
        load.start()
    basis_load = pltpu.make_async_copy(basis, basis_in, load_sem.at[0])
    basis_load.start()
    small = [
        pltpu.make_async_copy(gain_part.at[0], gain_mine, load_sem.at[1]),
        pltpu.make_async_copy(gains, gain_in.at[0], load_sem.at[2]),
        pltpu.make_async_copy(gain_first, gain_in.at[1], load_sem.at[3]),
        pltpu.make_async_copy(gain_second, gain_in.at[2], load_sem.at[4]),
        pltpu.make_async_copy(moment_first, first_in, load_sem.at[5]),
        pltpu.make_async_copy(moment_second, second_in, load_sem.at[6]),
        pltpu.make_async_copy(weights.at[own], weights_in, load_sem.at[7]),
    ]
    greet([partner] + [{"grp": lax.rem(me + k, n)} for k in far_first(n)])
    late = []
    trades = [
        peer_copy(grad.at[other, span], swap.at[:, span], trade_send.at[i], trade_recv.at[i], partner)
        for i, span in enumerate(spans)
    ]
    for trade in trades[:4]:
        trade.start()
    basis_load.wait()
    full[pl.ds(me, 1)] = basis_in[own][None]
    pass_basis = spread(n, me, full, basis_send, basis_recv, late)
    for load in small:
        load.start()

    for i, (z, y) in enumerate(order):
        loads[i].wait()
        trades[i].wait()
        if i == 0:
            for trade in trades[4:]:
                trade.start()
        span = spans[i]
        total = mine[:, span] + swap[:, span]
        base = (z * 2 + y) * 2
        even_tail, odd_tail = exchange_tails(total[: half // 2, main : main + 128], total[half // 2 :, main : main + 128])
        packed = [
            [total[:, 128 * t : 128 * (t + 1)] for t in range(tiles)] + [even_tail],
            [total[:, main + 128 * (t + 1) : main + 128 * (t + 2)] for t in range(tiles)] + [odd_tail],
        ]
        last = i + 1 == len(order)
        for x in range(2):
            at = 0
            for piece in packed[x]:
                parts[base + x, at : at + piece.shape[0]] = piece
                at += piece.shape[0]
        for x in [1 - side] if last else [side, 1 - side]:
            copy = peer_copy(
                parts.at[base + x], cols.at[me], col_send.at[base + x], col_recv.at[me], {"grp": base + x}
            )
            copy.start()
        if i == 1:
            pass_basis()
    cols[pl.ds(me, 1)] = parts[pl.ds(me, 1)]
    for copy in late:
        copy.wait()
    late = []
    gain_trade = peer_copy(gain_mine, gain_other, gain_sems.at[0], gain_sems.at[1], partner)
    small[0].wait()
    gain_trade.start()

    def landed(buffer, send, recv, source):
        return peer_copy(buffer.at[source], buffer.at[source], send.at[source], recv.at[source], {"grp": source})

    near_group = pl.ds(pl.multiple_of(upper * (n // 2), n // 2), n // 2)
    far_group = pl.ds(pl.multiple_of((1 - upper) * (n // 2), n // 2), n // 2)
    near_sources = [2 * (2 * z + y) + x for z, y in order[4:] for x in (side, 1 - side)]
    far_sources = [2 * (2 * z + y) + x for z, y in order[:4] for x in (side, 1 - side)]
    del near_sources[-2]

    def products(group):
        depths = full[group].reshape(-1, rank)
        tops = full[group, : half // 2].reshape(-1, rank)
        bottoms = full[group, half // 2 :].reshape(-1, rank)
        left = lane_tiles(cols, group, half, tiles)
        tail = cols[group, tiles * half :].reshape(-1, 128)
        yield rows_dot(left[:, : main // 2], depths)
        yield rows_dot(left[:, main // 2 :], depths)
        yield rows_dot(tail, tops)[:rest] + rows_dot(tail, bottoms)[rest:]

    pieces = [pl.ds(0, main // 2), pl.ds(main // 2, main // 2), pl.ds(main, rest)]
    for source in near_sources:
        landed(cols, col_send, col_recv, source).wait_recv()
    for piece, product in zip(pieces, products(near_group)):
        partial[piece] = product
    for source in far_sources:
        landed(cols, col_send, col_recv, source).wait_recv()
    joins = []
    for i, (piece, product) in enumerate(zip(pieces, products(far_group))):
        partial[piece] += product
        joins.append(peer_copy(partial.at[piece], other_partial.at[piece], part_send.at[i], part_recv.at[i], partner))
        joins[-1].start()
    small[4].wait()
    small[5].wait()
    natural = [
        pl.ds(pl.multiple_of(side * rest, rest), main // 2),
        pl.ds(pl.multiple_of(side * rest + main // 2, rest), main // 2),
        pl.ds(pl.multiple_of((1 - side) * main, rest), rest),
    ]
    for piece, place, join in zip(pieces, natural, joins):
        join.wait()
        proj = partial[piece] + other_partial[piece]
        projected[piece] = proj
        first = beta_first * first_in[place] + (1.0 - beta_first) * proj
        second = beta_second * second_in[place] + (1.0 - beta_second) * proj * proj
        first_in[place] = first
        second_in[place] = second
        direction[layer, piece] = first / corr_first / (jnp.sqrt(second / corr_second) + adam_eps)
    stores = []

    def store(source, target):
        stores.append(pltpu.make_async_copy(source, target, store_sem.at[len(stores)]))
        stores[-1].start()

    part = block // 4
    ranges = [pl.ds(pl.multiple_of(rep * (block // 2) + c * part, 8), part) for c in range(2)]
    inner = jnp.logical_and(layer > 0, layer < depth - 1)
    low = layer < 2
    mirrored = jnp.where(low, layer, depth - 1 - layer)
    origins = [jnp.where(low, k, depth - 1 - k) for k in (1 - mirrored, 2, 3)]

    def pass_copy(origin, c, toward, at):
        chip = jnp.clip(layer + toward, 0, depth - 1) * fan + spot
        held = direction.at[origin, ranges[c]]
        return peer_copy(held, held, pass_send.at[at, c], pass_recv.at[origin, c], {"grp": chip})

    def own_pass(act):
        for c in range(2):

            @pl.when(layer < depth - 1)
            def _():
                act(pass_copy(layer, c, 1, 0))

            @pl.when(layer > 0)
            def _():
                act(pass_copy(layer, c, -1, 1))

    own_pass(lambda copy: copy.start())

    def cross_copy(k, c):
        held = direction.at[origins[k], ranges[c]]
        return peer_copy(held, held, cross_send.at[k, c], cross_recv.at[k, c], partner)

    def forward(k, c):
        return pass_copy(origins[k], c, jnp.where(origins[k] < layer, 1, -1), 2 + k)

    def take_pass(k):
        for c in range(2):
            forward(k, c).wait_recv()

            @pl.when(inner)
            def _():
                forward(k, c).start()

            cross_copy(k, c).start()

    def take_pass_if(chosen, k):
        @pl.when(chosen)
        def _():
            take_pass(k)

    blank = jnp.zeros((rest, rank), jnp.float32)

    def paired(tail):
        return jnp.concatenate(
            [jnp.concatenate([tail, blank], axis=1), jnp.concatenate([blank, tail], axis=1)], axis=0
        )

    pair_proj[...] = paired(projected[main:])

    whole = plain_dot(lane_tiles(cols, pl.ds(0, n), half, tiles), projected[:main]).reshape(n, half, rank)
    tail = plain_dot(cols[:, tiles * half :].reshape(-1, 128), pair_proj[...])
    terms[:, : half // 2] = whole[:, : half // 2] + tail[:, :rank].reshape(n, half // 2, rank)
    terms[:, half // 2 :] = whole[:, half // 2 :] + tail[:, rank:].reshape(n, half // 2, rank)

    first_hop = []
    for f in plane:
        for d in range(depth):
            source = d * fan + lax.rem(spot + f, fan)
            first_hop.append(
                peer_copy(
                    terms.at[source],
                    near.at[f * depth + d],
                    near_send.at[f * depth + d],
                    near_recv.at[f * depth + d],
                    {"grp": plane[f]},
                )
            )
            first_hop[-1].start()

    beside = pl.ds(pl.multiple_of(layer * fan, fan), fan)

    def make_update(origin):
        group = pl.ds(pl.multiple_of(origin * fan, fan), fan)
        depths = full[beside].reshape(-1, rank)
        sides = jnp.concatenate(
            [full[beside, : half // 2].reshape(-1, rank), full[beside, half // 2 :].reshape(-1, rank)], axis=1
        )
        wide_part = lanes_dot(depths, direction[origin, :main])
        for t in range(tiles):
            up_out[group, t * half : (t + 1) * half] = wide_part[:, 128 * t : 128 * (t + 1)].reshape(fan, half, 128)
        up_out[group, tiles * half :] = lanes_dot(sides, paired(direction[origin, main:])).reshape(fan, half // 2, 128)

    def send_update(origin):
        for f in plane:
            at = origin * fan + lax.rem(spot + f, fan)
            peer_copy(
                up_out.at[at],
                up_in.at[origin * fan + spot],
                up_send.at[at],
                up_recv.at[origin * fan + spot],
                {"grp": plane[f]},
            ).start()
        up_in[pl.ds(origin * fan + spot, 1)] = up_out[pl.ds(origin * fan + spot, 1)]

    def take_update(k):
        for c in range(2):
            cross_copy(k, c).wait_recv()
        make_update(origins[k])
        send_update(origins[k])

    rate = learn_rate * galore_scale
    returns = []

    def take_weights(k):
        z = ([layer] + origins)[k]
        for j, y in enumerate((line, 1 - line)):
            base = (z * 2 + y) * 2
            for x in [1 - side] if j == 0 else [side, 1 - side]:
                landed(up_in, up_send, up_recv, base + x).wait_recv()
            start = pl.multiple_of((z * 2 + y) * wide, 128)
            top, bottom = exchange_tails(up_in[base, tiles * half :], up_in[base + 1, tiles * half :])
            for t in range(2 * tiles + 1):
                lanes = pl.ds(pl.multiple_of(start + 128 * t, 128), 128)
                if t < tiles:
                    change = up_in[base, t * half : (t + 1) * half]
                elif t == tiles:
                    change = jnp.concatenate([top, bottom], axis=0)
                else:
                    change = up_in[base + 1, (t - tiles - 1) * half : (t - tiles) * half]
                weights_in[:, lanes] = weights_in[:, lanes] - rate * change
            ready = weights_in.at[:, pl.ds(start, wide)]
            target = new_weights.at[own, pl.ds(start, wide)]
            i = len(returns)
            returns.append(peer_copy(ready, target, out_send.at[i], out_recv.at[i], partner))
            returns[-1].start()
            store(ready, target)

    store(first_in, new_first)
    store(second_in, new_second)
    make_update(layer)
    for copy in first_hop:
        copy.wait()
    for d in range(depth):
        total = terms[d * fan + spot]
        for f in plane:
            total = total + near[f * depth + d]
        sums[d] = total
    second_hop = []
    for d in column:
        source = sums.at[lax.rem(layer + d, depth)]
        second_hop.append(peer_copy(source, far.at[d], far_send.at[d], far_recv.at[d], {"grp": column[d]}))
        second_hop[-1].start()
    send_update(layer)
    take_pass(0)
    take_pass_if(inner, 1)
    for copy in second_hop:
        copy.wait()
    total = sums[layer]
    for d in column:
        total = total + far[d]
    rows[pl.ds(me, 1)] = total[None]
    pass_rows = spread(n, me, rows, row_send, row_recv, late)
    row_trade = peer_copy(rows.at[me], other_rows, swap_sems.at[0], swap_sems.at[1], partner)
    row_trade.start()
    take_update(0)

    for load in small[1:4]:
        load.wait()
    gain_trade.wait()
    gain_grad = gain_mine[...] + gain_other[...]
    gain_one = beta_first * gain_in[1] + (1.0 - beta_first) * gain_grad
    gain_two = beta_second * gain_in[2] + (1.0 - beta_second) * gain_grad * gain_grad
    gain_in[0] = gain_in[0] - learn_rate * (gain_one / corr_first) / (jnp.sqrt(gain_two / corr_second) + adam_eps)
    gain_in[1] = gain_one
    gain_in[2] = gain_two
    store(gain_in.at[0], new_gains)
    store(gain_in.at[1], new_gain_first)
    store(gain_in.at[2], new_gain_second)

    take_pass_if(inner, 2)
    pass_rows()
    take_pass_if(jnp.logical_not(inner), 1)
    take_update(1)
    small[6].wait()
    take_weights(0)
    for copy in late:
        copy.wait()
    everything = rows[...].reshape(-1, rank)
    gram[...] = rows_dot(everything, everything)
    gram_trade = peer_copy(gram, other_gram, swap_sems.at[2], swap_sems.at[3], partner)
    gram_trade.start()
    take_pass_if(jnp.logical_not(inner), 2)
    take_weights(1)
    row_trade.wait()
    gram_trade.wait()
    take_update(2)
    take_weights(2)
    current = gram[...] + other_gram[...]
    scale = jnp.sqrt(jnp.sqrt(jnp.sum(current * current, keepdims=True) + 1e-06))
    current = current / scale / scale
    first_rows = rows[me]
    second_rows = other_rows[...]
    upper_rows = jnp.where(rep == 0, first_rows, second_rows)
    lower_rows = jnp.where(rep == 0, second_rows, first_rows)
    iterate = jnp.concatenate([upper_rows, lower_rows], axis=0) / scale
    for step in range(NS_STEPS):
        iterate = 1.5 * iterate - 0.5 * plain_dot(iterate, current)
        if step + 1 < NS_STEPS:
            factor = 1.5 * current - 0.5 * plain_dot(current, current)
            current = 1.5 * factor - 0.5 * plain_dot(factor, current)
    basis_in[...] = iterate
    store(basis_in, new_basis)

    take_weights(3)
    for source in far_sources + near_sources:
        landed(parts, col_send, col_recv, source).wait_send()
    for origin in [layer] + origins:
        for f in plane:
            landed(up_out, up_send, up_recv, origin * fan + lax.rem(spot + f, fan)).wait_send()
    own_pass(lambda copy: copy.wait_send())
    for k in range(3):
        for c in range(2):
            cross_copy(k, c).wait_send()

            @pl.when(inner)
            def _():
                forward(k, c).wait_send()

    for copy in returns + stores:
        copy.wait()


def call_step(n, *arrays):
    grad, gain_part, weights, basis, moment_first, moment_second, gains, gain_first, gain_second = arrays
    rows, ncol = grad.shape
    half, block, rank = rows // 2, ncol // n, basis.shape[1]
    depth, fan = groups(n)
    message = half * block // 128
    pairs = n // 2

    def held(*shape):
        return pltpu.VMEM(shape, jnp.float32)

    def sems(*shape):
        return pltpu.SemaphoreType.DMA(shape)

    return pl.pallas_call(
        lambda *refs: one_step(n, *refs),
        out_shape=tuple(
            jax.ShapeDtypeStruct(x.shape, jnp.float32)
            for x in (weights, moment_first, moment_second, basis, gains, gain_first, gain_second)
        ),
        in_specs=[pl.BlockSpec(memory_space=pltpu.HBM)] * 9,
        out_specs=tuple([pl.BlockSpec(memory_space=pltpu.HBM)] * 7),
        scratch_shapes=[
            held(half, ncol),
            held(half, ncol),
            held(n, message, 128),
            held(n, message, 128),
            held(n, half, rank),
            held(block, rank),
            held(block, rank),
            held(block, rank),
            held(depth, block, rank),
            held(128, 2 * rank),
            held(block, rank),
            held(block, rank),
            held(half, ncol),
            held(rows, rank),
            held(3, 2, rows),
            held(2, rows),
            held(2, rows),
            held(n, half, rank),
            held(n, half, rank),
            held(depth, half, rank),
            held(depth, half, rank),
            held(n, half, rank),
            held(half, rank),
            held(rank, rank),
            held(rank, rank),
            held(n, message, 128),
            held(n, message, 128),
            sems(pairs),
            sems(pairs),
            sems(pairs),
            sems(8),
            sems(2),
            sems(n),
            sems(n),
            sems(n),
            sems(n),
            sems(3),
            sems(3),
            sems(n),
            sems(n),
            sems(n),
            sems(n),
            sems(n),
            sems(n),
            sems(4),
            sems(5, 2),
            sems(depth, 2),
            sems(3, 2),
            sems(3, 2),
            sems(n),
            sems(n),
            sems(pairs),
            sems(pairs),
            sems(pairs + 6),
        ],
        compiler_params=pltpu.CompilerParams(collective_id=2, has_side_effects=True, vmem_limit_bytes=WIDE_GRANT),
        name="one_step",
    )(*arrays)


def pieces_of(shape):
    count = 1
    while shape[0] % (16 * count) == 0 and shape[0] * shape[1] // count > 1 << 17:
        count *= 2
    size = shape[0] // count
    return [pl.ds(i * size, size) for i in range(count)]


def place(count, *refs):
    sources, targets, held, sems = refs[:count], refs[count : 2 * count], refs[2 * count : 3 * count], refs[-1]
    loads, stores = [], []
    for source, target, buffer in zip(sources, targets, held):
        for piece in pieces_of(source.shape):
            at = len(loads)
            loads.append(pltpu.make_async_copy(source.at[piece], buffer.at[piece], sems.at[0, at]))
            stores.append(pltpu.make_async_copy(buffer.at[piece], target.at[piece], sems.at[1, at]))
            loads[-1].start()
    for load, store in zip(loads, stores):
        load.wait()
        store.start()
    for store in stores:
        store.wait()


def call_place(arrays):
    count = len(arrays)
    space = [pl.BlockSpec(memory_space=pltpu.HBM)] * count
    return pl.pallas_call(
        lambda *refs: place(count, *refs),
        out_shape=tuple(jax.ShapeDtypeStruct(x.shape, x.dtype) for x in arrays),
        in_specs=space,
        out_specs=tuple(space),
        scratch_shapes=[pltpu.VMEM(x.shape, x.dtype) for x in arrays]
        + [pltpu.SemaphoreType.DMA((2, sum(len(pieces_of(x.shape)) for x in arrays)))],
        compiler_params=pltpu.CompilerParams(vmem_limit_bytes=WIDE_GRANT),
        name="place",
    )(*arrays)


def body(grad_parts, *rest):
    n = lax.axis_size("grp")
    rows, ncol = grad_parts.shape[1:]
    half, block = rows // 2, ncol // n
    if n == 16 and half == 32 and block % 128 == 64:
        return call_place(call_step(n, grad_parts[0], *rest))
    return split_body(grad_parts, *rest)


def solution(mesh):
    in_specs = (
        P("rep", "grp", None),
        P("rep", None, "grp"),
        P("grp", None),
        P("grp", None),
        P("grp", None),
        P("grp", None),
        P(None, "grp"),
        P(None, "grp"),
        P(None, "grp"),
    )
    out_specs = (
        P("grp", None),
        P("grp", None),
        P("grp", None),
        P("grp", None),
        P(None, "grp"),
        P(None, "grp"),
        P(None, "grp"),
    )
    return jax.shard_map(body, mesh=mesh, in_specs=in_specs, out_specs=out_specs, check_vma=False)
```

```python
import jax
import jax.numpy as jnp
from jax import lax
from jax.experimental import pallas as pl
from jax.experimental.pallas import tpu as pltpu
from jax.sharding import PartitionSpec as P

NS_STEPS = 3
GRANT = 24 << 20
WIDE_GRANT = 60 << 20


beta_first = 0.9
beta_second = 0.999
learn_rate = 0.1
galore_scale = 0.25
adam_eps = 1e-08


def exact_dot(left, right):
    return jnp.dot(left, right, precision=lax.Precision.HIGHEST, preferred_element_type=jnp.float32)


def far_first(n):
    return sorted(range(1, n), key=lambda k: abs(k - n // 2))


def peer_copy(src, dst, send_sem, recv_sem, where):
    return pltpu.make_async_remote_copy(
        src_ref=src,
        dst_ref=dst,
        send_sem=send_sem,
        recv_sem=recv_sem,
        device_id=where,
        device_id_type=pl.DeviceIdType.MESH,
    )


def greet(others):
    barrier = pltpu.get_barrier_semaphore()
    for other in others:
        pl.semaphore_signal(barrier, inc=1, device_id=other, device_id_type=pl.DeviceIdType.MESH)
    pl.semaphore_wait(barrier, len(others))


def groups(n):
    fan = 4 if n % 4 == 0 else 1
    return n // fan, fan


def peer_maps(n, me):
    depth, fan = groups(n)
    layer, spot = me // fan, lax.rem(me, fan)
    column = {d: lax.rem(layer + d, depth) * fan + spot for d in range(1, depth)}
    plane = {f: layer * fan + lax.rem(spot + f, fan) for f in range(1, fan)}
    return layer, spot, column, plane


def spread(n, me, ref, send, recv, sent):
    depth, fan = groups(n)
    layer, spot, column, plane = peer_maps(n, me)
    down = []
    for d in sorted(column, key=lambda d: abs(d - depth // 2)):
        down.append((d, peer_copy(ref.at[me], ref.at[me], send.at[d * fan], recv.at[d * fan], {"grp": column[d]})))
        down[-1][1].start()
    for f in plane:
        sent.append(peer_copy(ref.at[me], ref.at[me], send.at[f], recv.at[f], {"grp": plane[f]}))
        sent[-1].start()

    def pass_on():
        for d, copy in down:
            copy.wait()
            slot = lax.rem(layer - d + depth, depth) * fan + spot
            for f in plane:
                at = d * fan + f
                sent.append(peer_copy(ref.at[slot], ref.at[slot], send.at[at], recv.at[at], {"grp": plane[f]}))
                sent[-1].start()

    return pass_on


def split_of(half, block):
    rest = block % 128
    return (block - rest, rest) if 2 * rest == 128 and half % 16 == 0 else (block, 0)


def tails_of(n, half, block):
    rest = split_of(half, block)[1]
    return pltpu.VMEM((n, half // 2, 128) if rest else (1, 8, 128), jnp.float32)


def pack_tails(ref, tails):
    half = ref.shape[1]
    main, rest = split_of(half, ref.shape[2])
    if rest:
        tails[:, :, :rest] = ref[:, : half // 2, main:]
        tails[:, :, rest:] = ref[:, half // 2 :, main:]


def unpack_tails(tails, ref):
    half = ref.shape[1]
    main, rest = split_of(half, ref.shape[2])
    if rest:
        ref[:, : half // 2, main:] = tails[:, :, :rest]
        ref[:, half // 2 :, main:] = tails[:, :, rest:]


def keep_own(me, source, target, tails_out, tails_in):
    target[pl.ds(me, 1)] = source[pl.ds(me, 1)]
    if split_of(*source.shape[1:])[1]:
        tails_in[pl.ds(me, 1)] = tails_out[pl.ds(me, 1)]


def send_block(me, k, where, source, target, tails_out, tails_in, send, recv):
    main, rest = split_of(*source.shape[1:])
    peer = where["grp"]
    copies = [peer_copy(source.at[peer, :, :main], target.at[me, :, :main], send.at[0, k], recv.at[0, k], where)]
    if rest:
        copies.append(peer_copy(tails_out.at[peer], tails_in.at[me], send.at[1, k], recv.at[1, k], where))
    for copy in copies:
        copy.start()
    return copies


def scatter_grad(n, grad, basis, cols, full, mine, swap, parts, tails_out, tails_in, load_sem, swap_sems, basis_send, basis_recv, col_send, col_recv):
    me, rep = lax.axis_index("grp"), lax.axis_index("rep")
    half = swap.shape[0]
    block = cols.shape[2]
    offsets = far_first(n)
    peers = {k: {"grp": lax.rem(me + k, n)} for k in offsets}
    own = pl.ds(pl.multiple_of(rep * half, half), half)
    other = pl.ds(pl.multiple_of((1 - rep) * half, half), half)
    load = pltpu.make_async_copy(grad.at[own], mine, load_sem)
    load.start()
    full[pl.ds(me, 1)] = basis[own][None]
    greet([{"rep": 1 - rep}] + [peers[k] for k in offsets])
    trade = peer_copy(grad.at[other], swap, swap_sems.at[0], swap_sems.at[1], {"rep": 1 - rep})
    trade.start()
    copies = []
    pass_on = spread(n, me, full, basis_send, basis_recv, copies)
    load.wait()
    trade.wait()
    for j in range(n):
        parts[j] = mine[:, j * block : (j + 1) * block] + swap[:, j * block : (j + 1) * block]
    pack_tails(parts, tails_out)
    keep_own(me, parts, cols, tails_out, tails_in)
    late = n // 4
    for at, k in enumerate(offsets):
        if at == late:
            pass_on()
        copies += send_block(me, k, peers[k], parts, cols, tails_out, tails_in, col_send, col_recv)
    for copy in copies:
        copy.wait()
    unpack_tails(tails_in, cols)


def reduce_and_return(
    n, terms, moved, rows, update, near, sums, far, tails_out, tails_in, near_send, near_recv, far_send, far_recv, row_send, row_recv, up_send, up_recv
):
    me = lax.axis_index("grp")
    depth, fan = groups(n)
    layer, spot, column, plane = peer_maps(n, me)
    offsets = far_first(n)
    peers = {k: {"grp": lax.rem(me + k, n)} for k in offsets}
    greet([peers[k] for k in offsets])
    late = []
    waiting = list(offsets)

    def send_update(count):
        for k in waiting[:count]:
            late.extend(send_block(me, k, peers[k], moved, update, tails_out, tails_in, up_send, up_recv))
        del waiting[:count]

    first = []
    for f in plane:
        source = terms.at[:, lax.rem(spot + f, fan)]
        first.append(peer_copy(source, near.at[f], near_send.at[f], near_recv.at[f], {"grp": plane[f]}))
        first[-1].start()
    pack_tails(moved, tails_out)
    send_update(n // 4)
    keep_own(me, moved, update, tails_out, tails_in)
    near[0] = terms[:, pl.ds(spot, 1)][:, 0]
    for copy in first:
        copy.wait()
    partial = near[0]
    for f in plane:
        partial = partial + near[f]
    sums[...] = partial
    second = []
    for d in column:
        source = sums.at[lax.rem(layer + d, depth)]
        second.append(peer_copy(source, far.at[d], far_send.at[d], far_recv.at[d], {"grp": column[d]}))
        second[-1].start()
    send_update(n // 8)
    far[0] = sums[pl.ds(layer, 1)][0]
    for copy in second:
        copy.wait()
    total = far[0]
    for d in column:
        total = total + far[d]
    rows[pl.ds(me, 1)] = total[None]
    pass_on = spread(n, me, rows, row_send, row_recv, late)
    send_update(n // 4)
    pass_on()
    send_update(n)
    for copy in late:
        copy.wait()
    unpack_tails(tails_in, update)


def in_vmem(count):
    return [pl.BlockSpec(memory_space=pltpu.VMEM)] * count


def call_scatter(n, grad, basis):
    rows, ncol = grad.shape
    half, block, rank = rows // 2, ncol // n, basis.shape[1]
    sems = pltpu.SemaphoreType.DMA((n,))
    return pl.pallas_call(
        lambda *refs: scatter_grad(n, *refs),
        out_shape=(
            jax.ShapeDtypeStruct((n, half, block), jnp.float32),
            jax.ShapeDtypeStruct((n, half, rank), jnp.float32),
        ),
        in_specs=[pl.BlockSpec(memory_space=pltpu.HBM)] + in_vmem(1),
        out_specs=tuple(in_vmem(2)),
        scratch_shapes=[
            pltpu.VMEM((half, ncol), jnp.float32),
            pltpu.VMEM((half, ncol), jnp.float32),
            pltpu.VMEM((n, half, block), jnp.float32),
            tails_of(n, half, block),
            tails_of(n, half, block),
            pltpu.SemaphoreType.DMA,
            pltpu.SemaphoreType.DMA((2,)),
            sems,
            sems,
            pltpu.SemaphoreType.DMA((2, n)),
            pltpu.SemaphoreType.DMA((2, n)),
        ],
        compiler_params=pltpu.CompilerParams(collective_id=0, has_side_effects=True, vmem_limit_bytes=GRANT),
        name="scatter_grad",
    )(grad, basis)


def call_return(n, terms, moved):
    half, rank = terms.shape[2:]
    depth, fan = groups(n)
    sems = pltpu.SemaphoreType.DMA((n,))
    return pl.pallas_call(
        lambda *refs: reduce_and_return(n, *refs),
        out_shape=(
            jax.ShapeDtypeStruct((n, half, rank), jnp.float32),
            jax.ShapeDtypeStruct(moved.shape, jnp.float32),
        ),
        in_specs=in_vmem(2),
        out_specs=tuple(in_vmem(2)),
        scratch_shapes=[
            pltpu.VMEM((fan, depth, half, rank), jnp.float32),
            pltpu.VMEM((depth, half, rank), jnp.float32),
            pltpu.VMEM((depth, half, rank), jnp.float32),
            tails_of(*moved.shape),
            tails_of(*moved.shape),
        ]
        + [sems] * 6
        + [pltpu.SemaphoreType.DMA((2, n))] * 2,
        compiler_params=pltpu.CompilerParams(collective_id=1, has_side_effects=True, vmem_limit_bytes=GRANT),
        name="reduce_and_return",
    )(terms, moved)


def split_body(
    grad_parts,
    gain_grad_parts,
    weights,
    basis,
    moment_first,
    moment_second,
    gains,
    gain_first,
    gain_second,
):
    corr_first = 1.0 - beta_first**10
    corr_second = 1.0 - beta_second**10
    n = lax.axis_size("grp")
    rep = lax.axis_index("rep")
    swap = [(0, 1), (1, 0)]
    local_grad = grad_parts[0]
    local_gain = gain_grad_parts[0]
    rows, ncol = local_grad.shape
    half = rows // 2
    block = ncol // n
    rank = basis.shape[1]

    def own_half(x):
        return lax.dynamic_slice_in_dim(x, rep * half, half, 0)

    def swapped(x):
        return lax.ppermute(x, "rep", swap)

    def joined(mine, other):
        return jnp.where(rep == 0, jnp.concatenate([mine, other], 0), jnp.concatenate([other, mine], 0))

    gain_grad = local_gain + swapped(local_gain)
    col_block, half_basis = call_scatter(n, local_grad, basis)
    col_block = col_block.reshape(n * half, block)
    half_basis = half_basis.reshape(n * half, rank)
    partial = exact_dot(col_block.T, half_basis)
    projected = partial + swapped(partial)
    new_first = beta_first * moment_first + (1.0 - beta_first) * projected
    new_second = beta_second * moment_second + (1.0 - beta_second) * projected * projected
    direction = new_first / corr_first / (jnp.sqrt(new_second / corr_second) + adam_eps)
    terms = exact_dot(col_block, projected).reshape(*groups(n), half, rank)
    update_cols = exact_dot(half_basis, direction.T).reshape(n, half, block)
    sub_all, update = call_return(n, terms, update_cols)
    sub_half = lax.dynamic_index_in_dim(sub_all, lax.axis_index("grp"), 0, keepdims=False)
    sub_all = sub_all.reshape(n * half, rank)
    update = jnp.swapaxes(update, 0, 1).reshape(half, ncol)
    gram_half = exact_dot(sub_all.T, sub_all)
    gram = gram_half + swapped(gram_half)
    subspace = joined(sub_half, swapped(sub_half))
    new_half = own_half(weights) - learn_rate * galore_scale * update
    new_weights = joined(new_half, swapped(new_half))
    scale = jnp.sqrt(jnp.sqrt(jnp.sum(gram * gram) + 1e-06))
    iterate = subspace / scale
    current = gram / scale / scale
    for step in range(NS_STEPS):
        iterate = 1.5 * iterate - 0.5 * exact_dot(iterate, current)
        if step + 1 < NS_STEPS:
            side = 1.5 * current - 0.5 * exact_dot(current, current)
            current = 1.5 * side - 0.5 * exact_dot(side, current)
    new_gain_first = beta_first * gain_first + (1.0 - beta_first) * gain_grad
    new_gain_second = beta_second * gain_second + (1.0 - beta_second) * gain_grad * gain_grad
    new_gains = gains - learn_rate * (new_gain_first / corr_first) / (
        jnp.sqrt(new_gain_second / corr_second) + adam_eps
    )
    return (new_weights, new_first, new_second, iterate, new_gains, new_gain_first, new_gain_second)


def halves(x):
    high = x.astype(jnp.bfloat16)
    return high, (x - high.astype(jnp.float32)).astype(jnp.bfloat16)


def three_dots(left, right, dims):
    left_high, left_low = halves(left)
    right_high, right_low = halves(right)

    return lax.dot_general(
        jnp.concatenate([left_high, left_high, left_low], axis=dims[0][0]),
        jnp.concatenate([right_high, right_low, right_high], axis=dims[1][0]),
        (dims, ((), ())),
        preferred_element_type=jnp.float32,
    )


def plain_dot(left, right):
    return three_dots(left, right, ((1,), (0,)))


def rows_dot(left, right):
    return three_dots(left, right, ((0,), (0,)))


def lanes_dot(left, right):
    return three_dots(left, right, ((1,), (1,)))


def exchange_tails(top, bottom):
    low = lax.broadcasted_iota(jnp.int32, top.shape, 1) < 64
    even = jnp.where(low, top, pltpu.roll(bottom, 64, 1))
    odd = jnp.where(low, pltpu.roll(top, 64, 1), bottom)
    return even, odd


def lane_tiles(ref, group, half, tiles):
    return jnp.concatenate(
        [ref[group, t * half : (t + 1) * half].reshape(-1, 128) for t in range(tiles)], axis=1
    )


def one_step(
    n,
    grad,
    gain_part,
    weights,
    basis,
    moment_first,
    moment_second,
    gains,
    gain_first,
    gain_second,
    new_weights,
    new_first,
    new_second,
    new_basis,
    new_gains,
    new_gain_first,
    new_gain_second,
    mine,
    swap,
    parts,
    cols,
    full,
    partial,
    other_partial,
    projected,
    direction,
    pair_proj,
    first_in,
    second_in,
    weights_in,
    basis_in,
    gain_in,
    gain_mine,
    gain_other,
    terms,
    near,
    sums,
    far,
    rows,
    other_rows,
    gram,
    other_gram,
    up_out,
    up_in,
    chunk_sem,
    trade_send,
    trade_recv,
    load_sem,
    gain_sems,
    basis_send,
    basis_recv,
    col_send,
    col_recv,
    part_send,
    part_recv,
    near_send,
    near_recv,
    far_send,
    far_recv,
    row_send,
    row_recv,
    swap_sems,
    pass_send,
    pass_recv,
    cross_send,
    cross_recv,
    up_send,
    up_recv,
    out_send,
    out_recv,
    store_sem,
):
    corr_first = 1.0 - beta_first**10
    corr_second = 1.0 - beta_second**10
    me, rep = lax.axis_index("grp"), lax.axis_index("rep")
    depth, fan = groups(n)
    layer, spot, column, plane = peer_maps(n, me)
    half, ncol = mine.shape
    wide = 2 * ncol // n
    block = ncol // n
    tiles = block // 128
    main = tiles * 128
    rest = block - main
    rank = basis.shape[1]
    upper, deep = layer // 2, lax.rem(layer, 2)
    line, side = spot // 2, lax.rem(spot, 2)
    partner = {"rep": 1 - rep}
    own = pl.ds(pl.multiple_of(rep * half, half), half)
    other = pl.ds(pl.multiple_of((1 - rep) * half, half), half)
    layers = [2 * (1 - upper) + deep, 2 * (1 - upper) + 1 - deep, 2 * upper + 1 - deep, layer]
    order = [(z, y) for z in layers for y in (line, 1 - line)]
    order[-2:] = order[-2:][::-1]
    spans = [pl.ds(pl.multiple_of((z * 2 + y) * wide, 128), wide) for z, y in order]

    loads = [
        pltpu.make_async_copy(grad.at[own, span], mine.at[:, span], chunk_sem.at[i]) for i, span in enumerate(spans)
    ]
    for load in loads:
        load.start()
    basis_load = pltpu.make_async_copy(basis, basis_in, load_sem.at[0])
    basis_load.start()
    small = [
        pltpu.make_async_copy(gain_part.at[0], gain_mine, load_sem.at[1]),
        pltpu.make_async_copy(gains, gain_in.at[0], load_sem.at[2]),
        pltpu.make_async_copy(gain_first, gain_in.at[1], load_sem.at[3]),
        pltpu.make_async_copy(gain_second, gain_in.at[2], load_sem.at[4]),
        pltpu.make_async_copy(moment_first, first_in, load_sem.at[5]),
        pltpu.make_async_copy(moment_second, second_in, load_sem.at[6]),
        pltpu.make_async_copy(weights.at[own], weights_in, load_sem.at[7]),
    ]
    greet([partner] + [{"grp": lax.rem(me + k, n)} for k in far_first(n)])
    late = []
    trades = [
        peer_copy(grad.at[other, span], swap.at[:, span], trade_send.at[i], trade_recv.at[i], partner)
        for i, span in enumerate(spans)
    ]
    for trade in trades[:4]:
        trade.start()
    basis_load.wait()
    full[pl.ds(me, 1)] = basis_in[own][None]
    pass_basis = spread(n, me, full, basis_send, basis_recv, late)
    for load in small:
        load.start()

    for i, (z, y) in enumerate(order):
        loads[i].wait()
        trades[i].wait()
        if i == 0:
            for trade in trades[4:]:
                trade.start()
        span = spans[i]
        total = mine[:, span] + swap[:, span]
        base = (z * 2 + y) * 2
        even_tail, odd_tail = exchange_tails(total[: half // 2, main : main + 128], total[half // 2 :, main : main + 128])
        packed = [
            [total[:, 128 * t : 128 * (t + 1)] for t in range(tiles)] + [even_tail],
            [total[:, main + 128 * (t + 1) : main + 128 * (t + 2)] for t in range(tiles)] + [odd_tail],
        ]
        last = i + 1 == len(order)
        for x in range(2):
            at = 0
            for piece in packed[x]:
                parts[base + x, at : at + piece.shape[0]] = piece
                at += piece.shape[0]
        for x in [1 - side] if last else [side, 1 - side]:
            copy = peer_copy(
                parts.at[base + x], cols.at[me], col_send.at[base + x], col_recv.at[me], {"grp": base + x}
            )
            copy.start()
        if i == 1:
            pass_basis()
    cols[pl.ds(me, 1)] = parts[pl.ds(me, 1)]
    for copy in late:
        copy.wait()
    late = []
    gain_trade = peer_copy(gain_mine, gain_other, gain_sems.at[0], gain_sems.at[1], partner)
    small[0].wait()
    gain_trade.start()

    def landed(buffer, send, recv, source):
        return peer_copy(buffer.at[source], buffer.at[source], send.at[source], recv.at[source], {"grp": source})

    near_group = pl.ds(pl.multiple_of(upper * (n // 2), n // 2), n // 2)
    far_group = pl.ds(pl.multiple_of((1 - upper) * (n // 2), n // 2), n // 2)
    near_sources = [2 * (2 * z + y) + x for z, y in order[4:] for x in (side, 1 - side)]
    far_sources = [2 * (2 * z + y) + x for z, y in order[:4] for x in (side, 1 - side)]
    del near_sources[-2]

    def products(group):
        depths = full[group].reshape(-1, rank)
        tops = full[group, : half // 2].reshape(-1, rank)
        bottoms = full[group, half // 2 :].reshape(-1, rank)
        left = lane_tiles(cols, group, half, tiles)
        tail = cols[group, tiles * half :].reshape(-1, 128)
        yield rows_dot(left[:, : main // 2], depths)
        yield rows_dot(left[:, main // 2 :], depths)
        yield rows_dot(tail, tops)[:rest] + rows_dot(tail, bottoms)[rest:]

    pieces = [pl.ds(0, main // 2), pl.ds(main // 2, main // 2), pl.ds(main, rest)]
    for source in near_sources:
        landed(cols, col_send, col_recv, source).wait_recv()
    for piece, product in zip(pieces, products(near_group)):
        partial[piece] = product
    for source in far_sources:
        landed(cols, col_send, col_recv, source).wait_recv()
    joins = []
    for i, (piece, product) in enumerate(zip(pieces, products(far_group))):
        partial[piece] += product
        joins.append(peer_copy(partial.at[piece], other_partial.at[piece], part_send.at[i], part_recv.at[i], partner))
        joins[-1].start()
    small[4].wait()
    small[5].wait()
    natural = [
        pl.ds(pl.multiple_of(side * rest, rest), main // 2),
        pl.ds(pl.multiple_of(side * rest + main // 2, rest), main // 2),
        pl.ds(pl.multiple_of((1 - side) * main, rest), rest),
    ]
    for piece, place, join in zip(pieces, natural, joins):
        join.wait()
        proj = partial[piece] + other_partial[piece]
        projected[piece] = proj
        first = beta_first * first_in[place] + (1.0 - beta_first) * proj
        second = beta_second * second_in[place] + (1.0 - beta_second) * proj * proj
        first_in[place] = first
        second_in[place] = second
        direction[layer, piece] = first / corr_first / (jnp.sqrt(second / corr_second) + adam_eps)
    stores = []

    def store(source, target):
        stores.append(pltpu.make_async_copy(source, target, store_sem.at[len(stores)]))
        stores[-1].start()

    part = block // 4
    ranges = [pl.ds(pl.multiple_of(rep * (block // 2) + c * part, 8), part) for c in range(2)]
    inner = jnp.logical_and(layer > 0, layer < depth - 1)
    low = layer < 2
    mirrored = jnp.where(low, layer, depth - 1 - layer)
    origins = [jnp.where(low, k, depth - 1 - k) for k in (1 - mirrored, 2, 3)]

    def pass_copy(origin, c, toward, at):
        chip = jnp.clip(layer + toward, 0, depth - 1) * fan + spot
        held = direction.at[origin, ranges[c]]
        return peer_copy(held, held, pass_send.at[at, c], pass_recv.at[origin, c], {"grp": chip})

    def own_pass(act):
        for c in range(2):

            @pl.when(layer < depth - 1)
            def _():
                act(pass_copy(layer, c, 1, 0))

            @pl.when(layer > 0)
            def _():
                act(pass_copy(layer, c, -1, 1))

    own_pass(lambda copy: copy.start())

    def cross_copy(k, c):
        held = direction.at[origins[k], ranges[c]]
        return peer_copy(held, held, cross_send.at[k, c], cross_recv.at[k, c], partner)

    def forward(k, c):
        return pass_copy(origins[k], c, jnp.where(origins[k] < layer, 1, -1), 2 + k)

    def take_pass(k):
        for c in range(2):
            forward(k, c).wait_recv()

            @pl.when(inner)
            def _():
                forward(k, c).start()

            cross_copy(k, c).start()

    def take_pass_if(chosen, k):
        @pl.when(chosen)
        def _():
            take_pass(k)

    blank = jnp.zeros((rest, rank), jnp.float32)

    def paired(tail):
        return jnp.concatenate(
            [jnp.concatenate([tail, blank], axis=1), jnp.concatenate([blank, tail], axis=1)], axis=0
        )

    pair_proj[...] = paired(projected[main:])

    whole = plain_dot(lane_tiles(cols, pl.ds(0, n), half, tiles), projected[:main]).reshape(n, half, rank)
    tail = plain_dot(cols[:, tiles * half :].reshape(-1, 128), pair_proj[...])
    terms[:, : half // 2] = whole[:, : half // 2] + tail[:, :rank].reshape(n, half // 2, rank)
    terms[:, half // 2 :] = whole[:, half // 2 :] + tail[:, rank:].reshape(n, half // 2, rank)

    first_hop = []
    for f in plane:
        for d in range(depth):
            source = d * fan + lax.rem(spot + f, fan)
            first_hop.append(
                peer_copy(
                    terms.at[source],
                    near.at[f * depth + d],
                    near_send.at[f * depth + d],
                    near_recv.at[f * depth + d],
                    {"grp": plane[f]},
                )
            )
            first_hop[-1].start()

    beside = pl.ds(pl.multiple_of(layer * fan, fan), fan)

    def make_update(origin):
        group = pl.ds(pl.multiple_of(origin * fan, fan), fan)
        depths = full[beside].reshape(-1, rank)
        sides = jnp.concatenate(
            [full[beside, : half // 2].reshape(-1, rank), full[beside, half // 2 :].reshape(-1, rank)], axis=1
        )
        wide_part = lanes_dot(depths, direction[origin, :main])
        for t in range(tiles):
            up_out[group, t * half : (t + 1) * half] = wide_part[:, 128 * t : 128 * (t + 1)].reshape(fan, half, 128)
        up_out[group, tiles * half :] = lanes_dot(sides, paired(direction[origin, main:])).reshape(fan, half // 2, 128)

    def send_update(origin):
        for f in plane:
            at = origin * fan + lax.rem(spot + f, fan)
            peer_copy(
                up_out.at[at],
                up_in.at[origin * fan + spot],
                up_send.at[at],
                up_recv.at[origin * fan + spot],
                {"grp": plane[f]},
            ).start()
        up_in[pl.ds(origin * fan + spot, 1)] = up_out[pl.ds(origin * fan + spot, 1)]

    def take_update(k):
        for c in range(2):
            cross_copy(k, c).wait_recv()
        make_update(origins[k])
        send_update(origins[k])

    rate = learn_rate * galore_scale
    returns = []

    def take_weights(k):
        z = ([layer] + origins)[k]
        for j, y in enumerate((line, 1 - line)):
            base = (z * 2 + y) * 2
            for x in [1 - side] if j == 0 else [side, 1 - side]:
                landed(up_in, up_send, up_recv, base + x).wait_recv()
            start = pl.multiple_of((z * 2 + y) * wide, 128)
            top, bottom = exchange_tails(up_in[base, tiles * half :], up_in[base + 1, tiles * half :])
            for t in range(2 * tiles + 1):
                lanes = pl.ds(pl.multiple_of(start + 128 * t, 128), 128)
                if t < tiles:
                    change = up_in[base, t * half : (t + 1) * half]
                elif t == tiles:
                    change = jnp.concatenate([top, bottom], axis=0)
                else:
                    change = up_in[base + 1, (t - tiles - 1) * half : (t - tiles) * half]
                weights_in[:, lanes] = weights_in[:, lanes] - rate * change
            ready = weights_in.at[:, pl.ds(start, wide)]
            target = new_weights.at[own, pl.ds(start, wide)]
            i = len(returns)
            returns.append(peer_copy(ready, target, out_send.at[i], out_recv.at[i], partner))
            returns[-1].start()
            store(ready, target)

    store(first_in, new_first)
    store(second_in, new_second)
    make_update(layer)
    for copy in first_hop:
        copy.wait()
    for d in range(depth):
        total = terms[d * fan + spot]
        for f in plane:
            total = total + near[f * depth + d]
        sums[d] = total
    second_hop = []
    for d in column:
        source = sums.at[lax.rem(layer + d, depth)]
        second_hop.append(peer_copy(source, far.at[d], far_send.at[d], far_recv.at[d], {"grp": column[d]}))
        second_hop[-1].start()
    send_update(layer)
    take_pass(0)
    take_pass_if(inner, 1)
    for copy in second_hop:
        copy.wait()
    total = sums[layer]
    for d in column:
        total = total + far[d]
    rows[pl.ds(me, 1)] = total[None]
    pass_rows = spread(n, me, rows, row_send, row_recv, late)
    row_trade = peer_copy(rows.at[me], other_rows, swap_sems.at[0], swap_sems.at[1], partner)
    row_trade.start()
    take_update(0)

    for load in small[1:4]:
        load.wait()
    gain_trade.wait()
    gain_grad = gain_mine[...] + gain_other[...]
    gain_one = beta_first * gain_in[1] + (1.0 - beta_first) * gain_grad
    gain_two = beta_second * gain_in[2] + (1.0 - beta_second) * gain_grad * gain_grad
    gain_in[0] = gain_in[0] - learn_rate * (gain_one / corr_first) / (jnp.sqrt(gain_two / corr_second) + adam_eps)
    gain_in[1] = gain_one
    gain_in[2] = gain_two
    store(gain_in.at[0], new_gains)
    store(gain_in.at[1], new_gain_first)
    store(gain_in.at[2], new_gain_second)

    take_pass_if(inner, 2)
    pass_rows()
    take_pass_if(jnp.logical_not(inner), 1)
    take_update(1)
    small[6].wait()
    take_weights(0)
    for copy in late:
        copy.wait()
    everything = rows[...].reshape(-1, rank)
    gram[...] = rows_dot(everything, everything)
    gram_trade = peer_copy(gram, other_gram, swap_sems.at[2], swap_sems.at[3], partner)
    gram_trade.start()
    take_pass_if(jnp.logical_not(inner), 2)
    take_weights(1)
    row_trade.wait()
    gram_trade.wait()
    take_update(2)
    current = gram[...] + other_gram[...]
    scale = jnp.sqrt(jnp.sqrt(jnp.sum(current * current, keepdims=True) + 1e-06))
    current = current / scale / scale
    first_rows = rows[me]
    second_rows = other_rows[...]
    upper_rows = jnp.where(rep == 0, first_rows, second_rows)
    lower_rows = jnp.where(rep == 0, second_rows, first_rows)
    iterate = jnp.concatenate([upper_rows, lower_rows], axis=0) / scale
    for step in range(NS_STEPS):
        iterate = 1.5 * iterate - 0.5 * plain_dot(iterate, current)
        if step + 1 < NS_STEPS:
            factor = 1.5 * current - 0.5 * plain_dot(current, current)
            current = 1.5 * factor - 0.5 * plain_dot(factor, current)
    basis_in[...] = iterate
    store(basis_in, new_basis)

    take_weights(2)
    take_weights(3)
    for source in far_sources + near_sources:
        landed(parts, col_send, col_recv, source).wait_send()
    for origin in [layer] + origins:
        for f in plane:
            landed(up_out, up_send, up_recv, origin * fan + lax.rem(spot + f, fan)).wait_send()
    own_pass(lambda copy: copy.wait_send())
    for k in range(3):
        for c in range(2):
            cross_copy(k, c).wait_send()

            @pl.when(inner)
            def _():
                forward(k, c).wait_send()

    for copy in returns + stores:
        copy.wait()


def call_step(n, *arrays):
    grad, gain_part, weights, basis, moment_first, moment_second, gains, gain_first, gain_second = arrays
    rows, ncol = grad.shape
    half, block, rank = rows // 2, ncol // n, basis.shape[1]
    depth, fan = groups(n)
    message = half * block // 128
    pairs = n // 2

    def held(*shape):
        return pltpu.VMEM(shape, jnp.float32)

    def sems(*shape):
        return pltpu.SemaphoreType.DMA(shape)

    return pl.pallas_call(
        lambda *refs: one_step(n, *refs),
        out_shape=tuple(
            jax.ShapeDtypeStruct(x.shape, jnp.float32)
            for x in (weights, moment_first, moment_second, basis, gains, gain_first, gain_second)
        ),
        in_specs=[pl.BlockSpec(memory_space=pltpu.HBM)] * 9,
        out_specs=tuple([pl.BlockSpec(memory_space=pltpu.HBM)] * 7),
        scratch_shapes=[
            held(half, ncol),
            held(half, ncol),
            held(n, message, 128),
            held(n, message, 128),
            held(n, half, rank),
            held(block, rank),
            held(block, rank),
            held(block, rank),
            held(depth, block, rank),
            held(128, 2 * rank),
            held(block, rank),
            held(block, rank),
            held(half, ncol),
            held(rows, rank),
            held(3, 2, rows),
            held(2, rows),
            held(2, rows),
            held(n, half, rank),
            held(n, half, rank),
            held(depth, half, rank),
            held(depth, half, rank),
            held(n, half, rank),
            held(half, rank),
            held(rank, rank),
            held(rank, rank),
            held(n, message, 128),
            held(n, message, 128),
            sems(pairs),
            sems(pairs),
            sems(pairs),
            sems(8),
            sems(2),
            sems(n),
            sems(n),
            sems(n),
            sems(n),
            sems(3),
            sems(3),
            sems(n),
            sems(n),
            sems(n),
            sems(n),
            sems(n),
            sems(n),
            sems(4),
            sems(5, 2),
            sems(depth, 2),
            sems(3, 2),
            sems(3, 2),
            sems(n),
            sems(n),
            sems(pairs),
            sems(pairs),
            sems(pairs + 6),
        ],
        compiler_params=pltpu.CompilerParams(collective_id=2, has_side_effects=True, vmem_limit_bytes=WIDE_GRANT),
        name="one_step",
    )(*arrays)


def pieces_of(shape):
    count = 1
    while shape[0] % (16 * count) == 0 and shape[0] * shape[1] // count > 1 << 17:
        count *= 2
    size = shape[0] // count
    return [pl.ds(i * size, size) for i in range(count)]


def place(count, *refs):
    sources, targets, held, sems = refs[:count], refs[count : 2 * count], refs[2 * count : 3 * count], refs[-1]
    loads, stores = [], []
    for source, target, buffer in zip(sources, targets, held):
        for piece in pieces_of(source.shape):
            at = len(loads)
            loads.append(pltpu.make_async_copy(source.at[piece], buffer.at[piece], sems.at[0, at]))
            stores.append(pltpu.make_async_copy(buffer.at[piece], target.at[piece], sems.at[1, at]))
            loads[-1].start()
    for load, store in zip(loads, stores):
        load.wait()
        store.start()
    for store in stores:
        store.wait()


def call_place(arrays):
    count = len(arrays)
    space = [pl.BlockSpec(memory_space=pltpu.HBM)] * count
    return pl.pallas_call(
        lambda *refs: place(count, *refs),
        out_shape=tuple(jax.ShapeDtypeStruct(x.shape, x.dtype) for x in arrays),
        in_specs=space,
        out_specs=tuple(space),
        scratch_shapes=[pltpu.VMEM(x.shape, x.dtype) for x in arrays]
        + [pltpu.SemaphoreType.DMA((2, sum(len(pieces_of(x.shape)) for x in arrays)))],
        compiler_params=pltpu.CompilerParams(vmem_limit_bytes=WIDE_GRANT),
        name="place",
    )(*arrays)


def body(grad_parts, *rest):
    n = lax.axis_size("grp")
    rows, ncol = grad_parts.shape[1:]
    half, block = rows // 2, ncol // n
    if n == 16 and half == 32 and block % 128 == 64:
        return call_place(call_step(n, grad_parts[0], *rest))
    return split_body(grad_parts, *rest)


def solution(mesh):
    in_specs = (
        P("rep", "grp", None),
        P("rep", None, "grp"),
        P("grp", None),
        P("grp", None),
        P("grp", None),
        P("grp", None),
        P(None, "grp"),
        P(None, "grp"),
        P(None, "grp"),
    )
    out_specs = (
        P("grp", None),
        P("grp", None),
        P("grp", None),
        P("grp", None),
        P(None, "grp"),
        P(None, "grp"),
        P(None, "grp"),
    )
    return jax.shard_map(body, mesh=mesh, in_specs=in_specs, out_specs=out_specs, check_vma=False)
```
